256 devices in a mesh: rhombus: 8 (over z), tile: 32 (over y, x, core).
Axes of the slice: x: 4, y: 4, z: 8, core: 2. Of those that a mesh axis runs over, the one named last changes fastest.
Arguments:
- fine_latent: bfloat16 [131072, 512], P(('rhombus', 'tile')), may hold values from -6 to 6
- mid_latent: bfloat16 [8192, 512], P(('rhombus', 'tile')), may hold values from -6 to 6
- coarse_latent: bfloat16 [642, 512], replicated, may hold values from -6 to 6
- fine_parent: int32 [131072], P(('rhombus', 'tile')), may hold values from 0 to 95, as said below
- mid_parent: int32 [8192], P(('rhombus', 'tile')), may hold values from 0 to 641
- halo_rows: int32 [65536], P(('rhombus', 'tile')), may hold values from 0 to 511
- edge_source: int32 [786432], P(('rhombus', 'tile')), may hold values from 0 to 767
- edge_target: int32 [786432], P(('rhombus', 'tile')), may hold values from 0 to 512, as said below
- w_child: bfloat16 [512, 512], replicated, may hold values from -1 to 1
- mid_w1: bfloat16 [512, 512], replicated, may hold values from -0.25 to 0.25
- mid_w2: bfloat16 [512, 512], replicated, may hold values from -0.5 to 0.5
- mid_w3: bfloat16 [512, 512], replicated, may hold values from -0.25 to 0.25
- w_coarse: bfloat16 [512, 512], replicated, may hold values from -1 to 1
- coarse_w1: bfloat16 [512, 512], replicated, may hold values from -0.25 to 0.25
- coarse_w2: bfloat16 [512, 512], replicated, may hold values from -0.5 to 0.5
- coarse_w3: bfloat16 [512, 512], replicated, may hold values from -0.25 to 0.25
- w_descend: bfloat16 [512, 512], replicated, may hold values from -0.25 to 0.25
- w_fine: bfloat16 [512, 512], replicated, may hold values from -0.25 to 0.25
- edge_w_src: bfloat16 [512, 512], replicated, may hold values from -1 to 1
- edge_w_dst: bfloat16 [512, 512], replicated, may hold values from -0.25 to 0.25
- edge_w2: bfloat16 [512, 512], replicated, may hold values from -0.25 to 0.25
- node_w1: bfloat16 [512, 512], replicated, may hold values from -0.25 to 0.25
- node_w2: bfloat16 [512, 512], replicated, may hold values from -0.125 to 0.125
- node_w3: bfloat16 [512, 512], replicated, may hold values from -0.25 to 0.25
Outputs:
- fine_out: bfloat16 [131072, 512], P(('rhombus', 'tile'))
- mid_out: bfloat16 [8192, 512], P(('rhombus', 'tile'))
- coarse_out: bfloat16 [642, 512], replicated
The draws below stay inside these ranges and needn't reach their ends.
Inputs may be any that keep to these rules, and one draw needn't show every extreme that they name: `fine_parent`: in tile t of a group, an entry p < 32 names a middle slot of the same tile, 32 <= p < 64 a slot of tile t - 1, 64 <= p a slot of tile t + 1; tile 0 never names the tile before and the last tile of a group never names the tile after. `edge_target`: in each tile the live slots come first and name a fine row of that tile; the remaining slots hold 512. Each tile has at least 1536 live slots, and some tile has all 3072 slots live.
All inputs are finite; a program needn't handle non-finite values.
Results may differ from the reference program's by a relative error of at most 0.013.
Values may be sent and summed in bfloat16 or wider, within the bound.
No kernel may reach another device: no remote copies, remote signals or barrier semaphores. Data moves between devices by JAX's collectives and lax.ppermute only.
A program may use at most 64 MiB of HBM per device.

```python
import jax
import jax.numpy as jnp
from jax import lax

D = 512
HIDDEN_SIZE = 512
FINE_DEV = 512
MID_DEV = 32
HALO = 128
EDGES_DEV = 3072
COARSE = 642
GROUPS = 8
TILES = 32
FINE = 131072
MIDS = 8192


def draw_fine_parent(key, part):
    first_key, second_key = jax.random.split(jax.random.fold_in(key, 11))
    total = GROUPS * TILES * FINE_DEV
    side = jax.random.randint(first_key, (total,), 0, 8)
    within = jax.random.randint(second_key, (total,), 0, MID_DEV)
    tile_of = jnp.arange(total, dtype=jnp.int32) // FINE_DEV % TILES
    before = (side == 0) & (tile_of > 0)
    after = (side == 1) & (tile_of < TILES - 1)
    return jnp.where(before, within + MID_DEV, jnp.where(after, within + 2 * MID_DEV, within)).astype(jnp.int32)


def draw_mid_parent(key, part):
    near_key, far_key, pick_key = jax.random.split(jax.random.fold_in(key, 37), 3)
    blocks = GROUPS * TILES
    total = blocks * MID_DEV
    block_of = jnp.arange(total, dtype=jnp.int32) // MID_DEV
    start = block_of * COARSE // blocks
    offset = jax.random.randint(near_key, (total,), 0, 3)
    nearby = (start + offset) % COARSE
    anywhere = jax.random.randint(far_key, (total,), 0, COARSE)
    pick = jax.random.randint(pick_key, (total,), 0, 4)
    return jnp.where(pick == 0, anywhere, nearby).astype(jnp.int32)


def draw_edge_target(key, part):
    live_key, full_key, target_key = jax.random.split(jax.random.fold_in(key, 23), 3)
    blocks = GROUPS * TILES
    live = jax.random.randint(live_key, (blocks,), EDGES_DEV // 2, EDGES_DEV + 1)
    fullest = jax.random.randint(full_key, (), 0, blocks)
    live = jnp.where(jnp.arange(blocks, dtype=jnp.int32) == fullest, EDGES_DEV, live)
    slot_ids = jnp.arange(EDGES_DEV, dtype=jnp.int32)
    target = jax.random.randint(target_key, (blocks, EDGES_DEV), 0, FINE_DEV)
    marked = jnp.where(slot_ids[None, :] < live[:, None], target, FINE_DEV)
    return marked.reshape(blocks * EDGES_DEV).astype(jnp.int32)


def flat_map(key, marker, row_count, column_count, factor):
    widest = max(row_count, column_count)
    noise_key, sign_key = jax.random.split(jax.random.fold_in(key, marker))
    noise_draw = jnp.clip(jax.random.normal(noise_key, (widest, widest), jnp.float32), -4.0, 4.0)
    spread = 0.4
    skewed = (noise_draw - noise_draw.T) / jnp.sqrt(2.0 * widest)
    square = jnp.eye(widest, dtype=jnp.float32) + spread * skewed
    sign_flip = (2 * jax.random.randint(sign_key, (widest,), 0, 2) - 1).astype(jnp.float32)
    return (factor * square * sign_flip[None, :])[:row_count, :column_count]


def draw_w_child(key, part):
    return flat_map(key, 51, D, D, 1.0).astype(jnp.bfloat16)


def draw_mid_w2(key, part):
    return flat_map(key, 53, D, HIDDEN_SIZE, 0.5).astype(jnp.bfloat16)


def draw_w_coarse(key, part):
    return flat_map(key, 57, D, D, 1.0).astype(jnp.bfloat16)


def draw_coarse_w2(key, part):
    return flat_map(key, 59, D, HIDDEN_SIZE, 0.5).astype(jnp.bfloat16)


def draw_edge_w_src(key, part):
    return flat_map(key, 61, D, HIDDEN_SIZE, 1.0).astype(jnp.bfloat16)


def set_ends(drawn, key, smallest, top_value):
    shape = drawn.shape
    spot = [jax.random.randint(jax.random.fold_in(key, axis), (), 0, shape[axis]) for axis in range(len(shape))]
    drawn = drawn.at[tuple(spot)].set(smallest)
    longest = shape.index(max(shape))
    spot[longest] = (spot[longest] + 1) % shape[longest]
    return drawn.at[tuple(spot)].set(top_value)


def block_scale(own_key, shape, pieces, least, largest):
    level = 1.0
    for position, parts in pieces:
        steps = jax.random.uniform(jax.random.fold_in(jax.random.fold_in(own_key, 6), position), (parts,), jnp.float32, least / len(pieces), largest / len(pieces))
        level = level * jnp.repeat(jnp.exp(steps), shape[position] // parts).reshape((-1,) + (1,) * (len(shape) - 1 - position))
    return level


def normal_values(stream_key, dims, width, most, cuts=(), kind=jnp.bfloat16):
    values = jax.random.normal(stream_key, dims, jnp.float32) * width
    if len(cuts) > 0:
        values = block_scale(stream_key, dims, cuts, -0.22, 0.18) * values
    return jnp.clip(values, min=-most, max=most).astype(kind)


def setup_inputs(seed: int = 0) -> dict:
    splits = jax.random.split(jax.random.key(seed), 25)
    fine_latent = normal_values(splits[0], (FINE, D), 1.0, 6.0, ((0, 256),))
    mid_latent = normal_values(splits[1], (MIDS, D), 1.0, 6.0, ((0, 256),))
    coarse_latent = normal_values(splits[2], (COARSE, D), 1.0, 6.0)
    fine_parent = draw_fine_parent(jax.random.fold_in(splits[24], 71), 0)
    mid_parent = draw_mid_parent(jax.random.fold_in(splits[24], 71), 0)
    halo_rows = set_ends(jax.random.randint(splits[5], (FINE // 2,), 0, FINE_DEV), jax.random.fold_in(splits[5], 1), 0, FINE_DEV - 1).astype(jnp.int32)
    edge_source = set_ends(jax.random.randint(splits[6], (FINE * 6,), 0, FINE_DEV + 2 * HALO), jax.random.fold_in(splits[6], 1), 0, (FINE_DEV + 2 * HALO) - 1).astype(jnp.int32)
    edge_target = draw_edge_target(jax.random.fold_in(splits[24], 71), 0)
    w_child = draw_w_child(jax.random.fold_in(splits[24], 71), 0)
    mid_w1 = normal_values(splits[9], (D, HIDDEN_SIZE), D ** -0.5, 0.25)
    mid_w2 = draw_mid_w2(jax.random.fold_in(splits[24], 71), 0)
    mid_w3 = normal_values(splits[11], (HIDDEN_SIZE, D), HIDDEN_SIZE ** -0.5, 0.25)
    w_coarse = draw_w_coarse(jax.random.fold_in(splits[24], 71), 0)
    coarse_w1 = normal_values(splits[13], (D, HIDDEN_SIZE), D ** -0.5, 0.25)
    coarse_w2 = draw_coarse_w2(jax.random.fold_in(splits[24], 71), 0)
    coarse_w3 = normal_values(splits[15], (HIDDEN_SIZE, D), HIDDEN_SIZE ** -0.5, 0.25)
    w_descend = normal_values(splits[16], (D, D), D ** -0.5, 0.25)
    w_fine = normal_values(splits[17], (D, D), D ** -0.5, 0.25)
    edge_w_src = draw_edge_w_src(jax.random.fold_in(splits[24], 71), 0)
    edge_w_dst = normal_values(splits[19], (D, HIDDEN_SIZE), D ** -0.5, 0.25)
    edge_w2 = normal_values(splits[20], (HIDDEN_SIZE, D), HIDDEN_SIZE ** -0.5, 0.25)
    node_w1 = normal_values(splits[21], (D, HIDDEN_SIZE), D ** -0.5, 0.25)
    node_w2 = normal_values(splits[22], (D, HIDDEN_SIZE), (4 * D) ** -0.5, 0.125)
    node_w3 = normal_values(splits[23], (HIDDEN_SIZE, D), HIDDEN_SIZE ** -0.5, 0.25)
    return dict(fine_latent=fine_latent, mid_latent=mid_latent, coarse_latent=coarse_latent, fine_parent=fine_parent, mid_parent=mid_parent, halo_rows=halo_rows, edge_source=edge_source, edge_target=edge_target, w_child=w_child, mid_w1=mid_w1, mid_w2=mid_w2, mid_w3=mid_w3, w_coarse=w_coarse, coarse_w1=coarse_w1, coarse_w2=coarse_w2, coarse_w3=coarse_w3, w_descend=w_descend, w_fine=w_fine, edge_w_src=edge_w_src, edge_w_dst=edge_w_dst, edge_w2=edge_w2, node_w1=node_w1, node_w2=node_w2, node_w3=node_w3)


EPSILON = 1e-05

def product(left, right):
    return jnp.dot(left, right, preferred_element_type=jnp.float32)

def normed(values):
    return values / jnp.sqrt(lax.optimization_barrier(jnp.mean(values * values, axis=-1, keepdims=True)) + EPSILON)

def node_update(latent, incoming, first, second, third):
    hidden = jax.nn.silu(product(latent, first) + product(incoming, second)).astype(jnp.bfloat16)
    return (latent.astype(jnp.float32) + normed(product(hidden, third))).astype(jnp.bfloat16)

def edge_update(node_table, lifted, source, target, edge_w_src, edge_w_dst, edge_w2, node_w1, node_w2, node_w3):
    fine_count = lifted.shape[0]
    sender = product(node_table, edge_w_src).astype(jnp.bfloat16)
    receiver = product(lifted, edge_w_dst).astype(jnp.bfloat16)
    receiver = jnp.concatenate([receiver, jnp.zeros((1, receiver.shape[1]), jnp.bfloat16)], axis=0)
    edge_sum = jnp.take(sender, source, axis=0).astype(jnp.float32) + jnp.take(receiver, target, axis=0).astype(jnp.float32)
    edge_hidden = jax.nn.silu(edge_sum).astype(jnp.bfloat16)
    message = product(edge_hidden, edge_w2)
    aggregate = jax.ops.segment_sum(message, target, num_segments=fine_count + 1)[:fine_count]
    return node_update(lifted, aggregate.astype(jnp.bfloat16), node_w1, node_w2, node_w3)

def take_rows(node_block, row_ids):
    return jnp.take(node_block, row_ids, axis=0)

def reference(fine_latent, mid_latent, coarse_latent, fine_parent, mid_parent, halo_rows, edge_source, edge_target, w_child, mid_w1, mid_w2, mid_w3, w_coarse, coarse_w1, coarse_w2, coarse_w3, w_descend, w_fine, edge_w_src, edge_w_dst, edge_w2, node_w1, node_w2, node_w3):
    blocks = GROUPS * TILES
    fine_block = (jnp.arange(blocks * FINE_DEV, dtype=jnp.int32) // FINE_DEV).astype(jnp.int32)
    parent_side = (fine_parent // MID_DEV).astype(jnp.int32)
    offset = jnp.where(parent_side == 1, -1, jnp.where(parent_side == 2, 1, 0)).astype(jnp.int32)
    parent_index = ((fine_block + offset) * MID_DEV + fine_parent % MID_DEV).astype(jnp.int32)
    child_msg = product(fine_latent, w_child).astype(jnp.bfloat16)
    mid_in = jax.ops.segment_sum(child_msg.astype(jnp.float32), parent_index, num_segments=blocks * MID_DEV)
    mid_up = node_update(mid_latent, mid_in.astype(jnp.bfloat16), mid_w1, mid_w2, mid_w3)
    mid_msg = product(mid_up, w_coarse).astype(jnp.bfloat16)
    coarse_in = jax.ops.segment_sum(mid_msg.astype(jnp.float32), mid_parent, num_segments=COARSE)
    coarse_out = node_update(coarse_latent, coarse_in.astype(jnp.bfloat16), coarse_w1, coarse_w2, coarse_w3)
    down_coarse = product(coarse_out, w_descend).astype(jnp.bfloat16)
    mid_out = (mid_up.astype(jnp.float32) + jnp.take(down_coarse, mid_parent, axis=0).astype(jnp.float32)).astype(jnp.bfloat16)
    fine_down = product(mid_out, w_fine).astype(jnp.bfloat16)
    lifted = (fine_latent.astype(jnp.float32) + jnp.take(fine_down, parent_index, axis=0).astype(jnp.float32)).astype(jnp.bfloat16)
    features = lifted.shape[1]
    lifted_blocks = lifted.reshape(GROUPS, TILES, FINE_DEV, features)
    chosen = halo_rows.reshape(GROUPS, TILES, 2 * HALO)
    boundary = jax.vmap(jax.vmap(take_rows))(lifted_blocks, chosen)
    empty = jnp.zeros((GROUPS, 1, HALO, features), jnp.bfloat16)
    from_before = jnp.concatenate([empty, boundary[:, :-1, HALO:]], axis=1)
    from_after = jnp.concatenate([boundary[:, 1:, :HALO], empty], axis=1)
    node_table = jnp.concatenate([lifted_blocks, from_before, from_after], axis=2).reshape(blocks, FINE_DEV + 2 * HALO, features)

    def one_block(packed):
        return edge_update(packed[0], packed[1], packed[2], packed[3], edge_w_src, edge_w_dst, edge_w2, node_w1, node_w2, node_w3)
    fine_out = lax.map(one_block, (node_table, lifted_blocks.reshape(blocks, FINE_DEV, features), edge_source.reshape(blocks, EDGES_DEV), edge_target.reshape(blocks, EDGES_DEV)))
    return (fine_out.reshape(blocks * FINE_DEV, features), mid_out, coarse_out)
```

```python
import jax
import jax.numpy as jnp
from jax import lax
from jax.sharding import PartitionSpec as P

EPSILON = 1e-05
BLOCK = 24
PLANE = ("y", "x")
TILE = ("y", "x", "c")


def product(left, right):
    return jnp.dot(left, right, preferred_element_type=jnp.float32)


def bf(values):
    return values.astype(jnp.bfloat16)


def normed(values):
    return values / jnp.sqrt(jnp.mean(values * values, axis=-1, keepdims=True) + EPSILON)


def node_update(latent, incoming, first, second, third):
    hidden = bf(jax.nn.silu(product(latent, first) + product(incoming, second)))
    return bf(latent.astype(jnp.float32) + normed(product(hidden, third)))


def selector_rows(row_ids, width):
    columns = lax.broadcasted_iota(jnp.int32, (row_ids.shape[0], width), 1)
    return bf(columns == row_ids[:, None])


def selector_columns(row_ids, height):
    rows = lax.broadcasted_iota(jnp.int32, (height, row_ids.shape[0]), 0)
    return bf(rows == row_ids[None, :])


def shifted(values, axis, step, size):
    pairs = [(i, i + step) for i in range(size) if 0 <= i + step < size]
    return lax.ppermute(values, axis, pairs)


def swapped(values):
    return lax.ppermute(values, "c", [(0, 1), (1, 0)])


def with_columns(rows, columns):
    count = rows.shape[0]
    extra = jnp.stack(columns, axis=1).astype(jnp.bfloat16)
    extra = jnp.concatenate([extra, jnp.zeros((count, 128 - extra.shape[1]), jnp.bfloat16)], axis=1)
    return jnp.concatenate([rows, extra], axis=1)


def on_device(
    fine_latent,
    mid_latent,
    coarse_latent,
    fine_parent,
    mid_parent,
    halo_rows,
    edge_source,
    edge_target,
    w_child,
    mid_w1,
    mid_w2,
    mid_w3,
    w_coarse,
    coarse_w1,
    coarse_w2,
    coarse_w3,
    w_descend,
    w_fine,
    edge_w_src,
    edge_w_dst,
    edge_w2,
    node_w1,
    node_w2,
    node_w3,
):
    fine_count, width = fine_latent.shape
    mid_count = mid_latent.shape[0]
    coarse_count = coarse_latent.shape[0]
    rim = halo_rows.shape[0] // 2
    planes, chips = lax.axis_size("z"), lax.axis_size("y") * lax.axis_size("x")
    tiles = 2 * chips
    half = chips * BLOCK
    core = lax.axis_index("c")
    chip = lax.axis_index("y") * lax.axis_size("x") + lax.axis_index("x")

    child_msg = bf(product(fine_latent, w_child))
    partial_sums = product(selector_columns(fine_parent, 3 * mid_count), child_msg)
    from_before = shifted(partial_sums[2 * mid_count :], TILE, 1, tiles)
    from_after = shifted(partial_sums[mid_count : 2 * mid_count], TILE, -1, tiles)
    mid_in = partial_sums[:mid_count] + from_before + from_after
    mid_up = node_update(mid_latent, bf(mid_in), mid_w1, mid_w2, mid_w3)

    labelled = with_columns(mid_up, [mid_parent // 32, mid_parent % 32])
    other = swapped(labelled)
    pair = jnp.where(core == 0, jnp.concatenate([labelled, other]), jnp.concatenate([other, labelled]))
    pair_ids = pair[:, width].astype(jnp.int32) * 32 + pair[:, width + 1].astype(jnp.int32)

    pair_msg = bf(product(pair[:, :width], w_coarse))
    blocks = bf(product(selector_columns(pair_ids - core * half, half), pair_msg))
    blocks = lax.all_to_all(blocks.reshape(chips, BLOCK, width), PLANE, 0, 0)
    own = bf(jnp.sum(blocks.astype(jnp.float32), axis=0))
    planes_of = lax.all_to_all(jnp.broadcast_to(own, (planes, BLOCK, width)), "z", 0, 0)
    coarse_in = bf(jnp.sum(planes_of.astype(jnp.float32), axis=0))

    padded = jnp.pad(coarse_latent, ((0, 2 * half - coarse_count), (0, 0)))
    own_latent = lax.dynamic_slice_in_dim(padded, core * half + chip * BLOCK, BLOCK)
    own_out = node_update(own_latent, coarse_in, coarse_w1, coarse_w2, coarse_w3)
    mine = lax.all_to_all(jnp.broadcast_to(own_out, (chips, BLOCK, width)), PLANE, 0, 0).reshape(half, width)
    theirs = swapped(mine)
    coarse_all = jnp.where(core == 0, jnp.concatenate([mine, theirs]), jnp.concatenate([theirs, mine]))

    before = shifted(pair, PLANE, 1, chips)
    after = shifted(pair, PLANE, -1, chips)
    window = lax.dynamic_slice_in_dim(jnp.concatenate([before, pair, after]), core * mid_count, 5 * mid_count)
    window_ids = window[:, width].astype(jnp.int32) * 32 + window[:, width + 1].astype(jnp.int32)

    sent = with_columns(fine_latent, [fine_parent + 1])
    boundary = bf(product(selector_rows(halo_rows, fine_count), sent))
    halo_before = shifted(boundary[rim:], TILE, 1, tiles)
    halo_after = shifted(boundary[:rim], TILE, -1, tiles)

    def placed(code, tile):
        parent = code - 1
        side = parent // mid_count
        away = jnp.where(side == 1, -1, jnp.where(side == 2, 1, 0))
        return jnp.where(code > 0, (tile + away) * mid_count + parent % mid_count, -1)

    table = jnp.concatenate([fine_latent, halo_before[:, :width], halo_after[:, :width]])
    own_slot = placed(fine_parent + 1, 2)
    table_slot = jnp.concatenate(
        [
            own_slot,
            placed(halo_before[:, width].astype(jnp.int32), 1),
            placed(halo_after[:, width].astype(jnp.int32), 3),
        ]
    )

    parents = bf(product(selector_rows(window_ids, 2 * half), coarse_all))
    down = bf(product(parents, w_descend))
    window_out = bf(window[:, :width].astype(jnp.float32) + down.astype(jnp.float32))
    mid_out = window_out[2 * mid_count : 3 * mid_count]
    fine_down = bf(product(window_out, w_fine))
    lifted_table = bf(
        table.astype(jnp.float32) + product(selector_rows(table_slot, 5 * mid_count), fine_down)
    )
    lifted = lifted_table[:fine_count]

    sender = bf(product(lifted_table, edge_w_src))
    receiver = bf(product(lifted, edge_w_dst))
    source_pick = selector_rows(edge_source, table.shape[0])
    target_pick = selector_rows(edge_target, fine_count)
    edge_sum = product(source_pick, sender) + product(target_pick, receiver)
    edge_hidden = bf(jax.nn.silu(edge_sum))
    hidden_sums = lax.dot_general(
        target_pick, edge_hidden, (((0,), (0,)), ((), ())), preferred_element_type=jnp.float32
    )
    aggregate = jnp.dot(hidden_sums, edge_w2.astype(jnp.float32), precision=lax.Precision.HIGHEST)
    fine_out = node_update(lifted, bf(aggregate), node_w1, node_w2, node_w3)
    return (fine_out, mid_out, coarse_all[:coarse_count])


def solution(mesh):
    groups, tiles = mesh.shape["rhombus"], mesh.shape["tile"]
    side = {32: (4, 4), 8: (2, 2)}[tiles]
    physical = jax.sharding.Mesh(mesh.devices.reshape(groups, *side, 2), ("z", "y", "x", "c"))
    every = ("z", "y", "x", "c")
    split, copied = P(every), P()
    return jax.shard_map(
        on_device,
        mesh=physical,
        in_specs=(split, split, copied) + (split,) * 5 + (copied,) * 16,
        out_specs=(split, split, copied),
        check_vma=False,
    )
```

```python
import functools

import jax
import jax.numpy as jnp
from jax import lax
from jax.experimental import pallas as pl
from jax.experimental.pallas import tpu as pltpu
from jax.sharding import PartitionSpec as P

EPSILON = 1e-05
BLOCK = 24
LANES = 128
CHUNK = 512
PLANE = ("y", "x")
TILE = ("y", "x", "c")
F32, BF16, I32 = jnp.float32, jnp.bfloat16, jnp.int32
VMEM = pl.BlockSpec(memory_space=pltpu.VMEM)
UNREAD = pl.BlockSpec(memory_space=pl.ANY)


def kernel_call(body, outs, operands, after=(), scratch=(), limit=24, flops=0, name=None):
    count, skipped = len(operands), len(after)

    def kernel(*refs):
        body(*refs[:count], *refs[count + skipped :])

    return pl.pallas_call(
        kernel,
        out_shape=[jax.ShapeDtypeStruct(shape, dtype) for shape, dtype in outs],
        in_specs=[VMEM] * count + [UNREAD] * skipped,
        out_specs=[VMEM] * len(outs),
        scratch_shapes=list(scratch),
        compiler_params=pltpu.CompilerParams(vmem_limit_bytes=limit << 20),
        cost_estimate=pl.CostEstimate(flops=flops, bytes_accessed=1 << 20, transcendentals=0),
        name=name,
    )(*operands, *after)


def product(left, right):
    return jnp.dot(left, right, preferred_element_type=F32)


def silu(values):
    half = 0.5 * values
    return half + half * jnp.tanh(half)


def updated(latent, hidden, third):
    values = product(hidden.astype(BF16), third)
    scale = lax.rsqrt(jnp.mean(values * values, axis=-1, keepdims=True) + EPSILON)
    return (latent.astype(F32) + values * scale).astype(BF16)


def lanes(height, first=0):
    return lax.broadcasted_iota(I32, (height, LANES), 1) + first


def spread(row):
    return jnp.broadcast_to(row, (LANES, LANES)).T


def hot(mask):
    return jnp.where(mask, 1.0, 0.0).astype(BF16)


def picks(spread_ids, first, blocks):
    return [hot(spread_ids == lanes(LANES, first + LANES * q)) for q in range(blocks)]


def sums_body(parent, fine, own, up, down):
    count = own.shape[0]
    rows = lax.broadcasted_iota(I32, (3 * count, LANES), 0)
    blocks = [hot(rows == parent[r : r + 1, :]) for r in range(parent.shape[0])]
    sums = product(jnp.concatenate(blocks, axis=1), fine[...])
    own[...] = sums[:count]
    down[...] = sums[count : 2 * count].astype(BF16)
    up[...] = sums[2 * count :].astype(BF16)


def mid_body(own, before, after, latent, ids, w_child, first, second, third, out):
    count, width = latent.shape
    total = own[...] + before[...].astype(F32) + after[...].astype(F32)
    incoming = product(total.astype(BF16), w_child[...]).astype(BF16)
    hidden = silu(product(latent[...], first[...]) + product(incoming, second[...]))
    out[:, :width] = updated(latent[...], hidden, third[...])
    spread_ids = spread(jnp.concatenate([ids[...], jnp.zeros((1, LANES - count), I32)], axis=1))[:count]
    place = lanes(count)
    label = jnp.where(place == 0, spread_ids >> 5, jnp.where(place == 1, spread_ids & 31, 0))
    out[:, width:] = label.astype(F32).astype(BF16)


def row_ids(labelled, width):
    label = labelled[:, width:].astype(F32)
    return (label[:, :1] * 32.0 + label[:, 1:2]).astype(I32)


def blocks_body(mine, theirs, pair, out):
    count, width = mine.shape[0], out.shape[1]
    half = out.shape[0]
    core = lax.axis_index("c")
    pair[pl.ds(pl.multiple_of(core * count, count), count), :] = mine[...]
    pair[pl.ds(pl.multiple_of((1 - core) * count, count), count), :] = theirs[...]
    both = pair[...]
    columns = lax.broadcasted_iota(I32, (2 * count, half), 1) + core * half
    picked = hot(row_ids(both, width) == columns)
    out[...] = lax.dot_general(
        picked, both[:, :width], (((0,), (0,)), ((), ())), preferred_element_type=F32
    ).astype(BF16)


def tables_body(
    fine, parent, halo, coarse, w_src, w_dst, w_node, w_coarse, coarse_w1, coarse_w2,
    sender, receiver, node, boundary, both, own_latent, own_hidden,
):
    count, width = fine.shape
    blocks = count // LANES
    values = fine[...]
    sender[...] = product(values, w_src[...]).astype(BF16)
    receiver[...] = product(values, w_dst[...]).astype(BF16)
    node[...] = product(values, w_node[...])
    codes = [(spread(parent[r : r + 1, :]) + 1).astype(F32).astype(BF16) for r in range(blocks)]
    codes = jnp.concatenate(codes, axis=0)
    for r in range(halo.shape[0]):
        picked = jnp.concatenate(picks(spread(halo[r : r + 1, :]), 0, blocks), axis=1)
        boundary[r * LANES : (r + 1) * LANES, :width] = product(picked, values).astype(BF16)
        boundary[r * LANES : (r + 1) * LANES, width:] = product(picked, codes).astype(BF16)
    both[...] = product(w_coarse[...], coarse_w2[...]).astype(BF16)
    rows, total = own_latent.shape[0], coarse.shape[0]
    chip = lax.axis_index("y") * lax.axis_size("x") + lax.axis_index("x")
    chips = lax.axis_size("y") * lax.axis_size("x")
    first = (lax.axis_index("c") * chips + chip) * rows
    place = lax.broadcasted_iota(I32, (rows, total), 0) + first
    picked = hot(place == lax.broadcasted_iota(I32, (rows, total), 1))
    latent = product(picked, coarse[...]).astype(BF16)
    own_latent[...] = latent
    own_hidden[...] = product(latent, coarse_w1[...])


def gather_body(parts, out):
    total = jnp.sum(parts[...].astype(F32), axis=0).astype(BF16)
    for i in range(out.shape[0]):
        out[i] = total


def coarse_body(parts, own_latent, own_hidden, both, third, out):
    total = jnp.sum(parts[...].astype(F32), axis=0).astype(BF16)
    hidden = silu(own_hidden[...] + product(total, both[...]))
    result = updated(own_latent[...], hidden, third[...])
    for i in range(out.shape[0]):
        out[i] = result


def own_edges_body(source, target, sender, receiver, out, table):
    count = sender.shape[0]
    table[:count] = sender[...]
    table[count:] = receiver[...]
    for k in range(out.shape[0] // CHUNK):
        rows = []
        for r in range(k * CHUNK // LANES, (k + 1) * CHUNK // LANES):
            row = picks(spread(source[r : r + 1, :]), 0, count // LANES)
            row += picks(spread(target[r : r + 1, :]), 0, count // LANES)
            rows.append(jnp.concatenate(row, axis=1))
        picked = jnp.concatenate(rows, axis=0)
        out[k * CHUNK : (k + 1) * CHUNK, :] = product(picked, table[...]).astype(BF16)


def slots(codes, tile, count):
    parent = codes - 1
    side = parent // count
    away = jnp.where(side == 1, -1, jnp.where(side == 2, 1, 0))
    return jnp.where(codes > 0, (tile + away) * count + (parent & (count - 1)), -1)


def rest_edges_body(mid_count, source, target, parent, before, after, w_src, first, out, select, own_pick, table, where):
    count = own_pick.shape[0]
    width = out.shape[1]
    blocks = count // LANES
    for r in range(blocks):
        place = slots(spread(parent[r : r + 1, :]) + 1, 2, mid_count)
        rows = slice(r * LANES, (r + 1) * LANES)
        where[rows, :] = jnp.concatenate(picks(place, 0, 2), axis=1)
        near = place - mid_count
        own_pick[rows, :] = hot(near == lanes(LANES))
        far = place + 4 * mid_count
        there = slice(count + 2 * LANES + r * LANES, count + 2 * LANES + (r + 1) * LANES)
        where[there, :] = jnp.concatenate(picks(far, 0, 2), axis=1)
    for r, (halo, tile) in enumerate(((before, 1), (after, 3))):
        values = halo[...]
        rows = slice(r * LANES, (r + 1) * LANES)
        table[rows, :] = product(values[:, :width], w_src[...]).astype(BF16)
        place = slots(values[:, width:].astype(F32).astype(I32), tile, mid_count)
        where[count + r * LANES : count + (r + 1) * LANES, :] = jnp.concatenate(picks(place, 0, 2), axis=1)
    for k in range(out.shape[0] // CHUNK):
        rows = []
        for r in range(k * CHUNK // LANES, (k + 1) * CHUNK // LANES):
            row = picks(spread(source[r : r + 1, :]), 0, blocks + 2)
            row += picks(spread(target[r : r + 1, :]), 0, blocks)
            rows.append(jnp.concatenate(row, axis=1))
        picked = jnp.concatenate(rows, axis=0)
        here = slice(k * CHUNK, (k + 1) * CHUNK)
        select[here, :] = product(picked, where[...]).astype(BF16)
        rest = product(picked[:, count : count + 2 * LANES], table[...])
        out[here, :] = (first[here, :].astype(F32) + rest).astype(BF16)


def final_body(
    mine, theirs, before, pair, after, edges, select, target, fine, own_pick, node,
    w_descend, w_fine, w_src, w_dst, w_node, edge_w2, node_w2, node_w3,
    fine_out, mid_out, coarse_out, coarse, window, table, sums,
):
    core = lax.axis_index("c")
    half, width = mine.shape
    two = pair.shape[0]
    count = two // 2
    coarse[pl.ds(pl.multiple_of(core * half, half), half), :] = mine[...]
    coarse[pl.ds(pl.multiple_of((1 - core) * half, half), half), :] = theirs[...]
    window[:two] = before[...]
    window[two : 2 * two] = pair[...]
    window[2 * two :] = after[...]
    near = window[pl.ds(pl.multiple_of(core * count, count), 5 * count), :]
    columns = lax.broadcasted_iota(I32, (5 * count, 2 * half), 1)
    picked = hot(row_ids(near, width) == columns)
    parents = product(picked, coarse[...]).astype(BF16)
    down = product(parents, w_descend[...]).astype(BF16)
    middle = (near[:, :width].astype(F32) + down.astype(F32)).astype(BF16)
    mid_out[...] = middle[2 * count : 3 * count]
    fine_down = product(middle, w_fine[...]).astype(BF16)
    closer = fine_down[count : 4 * count]
    table[: 5 * count] = product(fine_down, w_src[...]).astype(BF16)
    table[5 * count :] = product(closer, w_dst[...]).astype(BF16)
    rows = lax.broadcasted_iota(I32, (fine.shape[0], LANES), 0)
    for k in range(edges.shape[0] // CHUNK):
        here = slice(k * CHUNK, (k + 1) * CHUNK)
        edge_sum = edges[here, :].astype(F32) + product(select[here, :], table[...])
        hidden = silu(edge_sum).astype(BF16)
        marks = range(k * CHUNK // LANES, (k + 1) * CHUNK // LANES)
        scatter = jnp.concatenate([hot(rows == target[r : r + 1, :]) for r in marks], axis=1)
        part = product(scatter, hidden)
        if k == 0:
            sums[...] = part
        else:
            sums[...] += part
    coarse_out[...] = coarse[: coarse_out.shape[0], :]
    reach = fine_down[count : 5 * count]
    lifted = (fine[...].astype(F32) + product(own_pick[...], reach)).astype(BF16)
    near_node = product(reach, w_node[...]).astype(BF16)
    aggregate = product(sums[...].astype(BF16), edge_w2[...]).astype(BF16)
    hidden = silu(node[...] + product(own_pick[...], near_node) + product(aggregate, node_w2[...]))
    fine_out[...] = updated(lifted, hidden, node_w3[...])


def shifted(values, axis, step, size):
    pairs = [(i, i + step) for i in range(size) if 0 <= i + step < size]
    return lax.ppermute(values, axis, pairs)


def swapped(values):
    return lax.ppermute(values, "c", [(0, 1), (1, 0)])


def on_device(
    fine_latent,
    mid_latent,
    coarse_latent,
    fine_parent,
    mid_parent,
    halo_rows,
    edge_source,
    edge_target,
    w_child,
    mid_w1,
    mid_w2,
    mid_w3,
    w_coarse,
    coarse_w1,
    coarse_w2,
    coarse_w3,
    w_descend,
    w_fine,
    edge_w_src,
    edge_w_dst,
    edge_w2,
    node_w1,
    node_w2,
    node_w3,
):
    count, width = fine_latent.shape
    mids = mid_latent.shape[0]
    coarse_count = coarse_latent.shape[0]
    edge_count = edge_source.shape[0]
    planes, chips = lax.axis_size("z"), lax.axis_size("y") * lax.axis_size("x")
    tiles = 2 * chips
    half = chips * BLOCK
    wide = width + LANES
    parent = fine_parent.reshape(-1, LANES)
    source = edge_source.reshape(-1, LANES)
    target = edge_target.reshape(-1, LANES)
    halo = halo_rows.reshape(-1, LANES)

    own, up, down = kernel_call(
        sums_body,
        [((mids, width), F32), ((mids, width), BF16), ((mids, width), BF16)],
        [parent, fine_latent],
        name="child_sums",
    )
    from_before = shifted(up, TILE, 1, tiles)
    from_after = shifted(down, TILE, -1, tiles)
    (labelled,) = kernel_call(
        mid_body,
        [((mids, wide), BF16)],
        [own, from_before, from_after, mid_latent, mid_parent[None], w_child, mid_w1, mid_w2, mid_w3],
        name="mid_update",
    )
    other = swapped(labelled)
    pair, blocks = kernel_call(
        blocks_body,
        [((2 * mids, wide), BF16), ((half, width), BF16)],
        [labelled, other],
        name="coarse_blocks",
    )

    blocks = blocks.reshape(chips, BLOCK, width)
    parts = lax.all_to_all(blocks, PLANE, 0, 0)
    sender, receiver, node, boundary, both, own_latent, own_hidden = kernel_call(
        tables_body,
        [
            ((count, width), BF16),
            ((count, width), BF16),
            ((count, width), F32),
            ((2 * LANES, wide), BF16),
            ((width, width), BF16),
            ((BLOCK, width), BF16),
            ((BLOCK, width), F32),
        ],
        [fine_latent, parent, halo, coarse_latent, edge_w_src, edge_w_dst, node_w1, w_coarse, coarse_w1, coarse_w2],
        after=[blocks],
        flops=2_000_000_000,
        name="tables",
    )

    (own_parts,) = kernel_call(
        gather_body, [((planes, BLOCK, width), BF16)], [parts], after=[own_latent], name="plane_sum"
    )
    in_planes = lax.all_to_all(own_parts, "z", 0, 0)
    pair_sent, boundary, _ = lax.optimization_barrier((pair, boundary, own_parts))
    before = shifted(pair_sent, PLANE, 1, chips)
    after = shifted(pair_sent, PLANE, -1, chips)
    halo_before = shifted(boundary[LANES:], TILE, 1, tiles)
    halo_after = shifted(boundary[:LANES], TILE, -1, tiles)
    (own_edges,) = kernel_call(
        own_edges_body,
        [((edge_count, width), BF16)],
        [source, target, sender, receiver],
        after=[own_parts],
        scratch=[pltpu.VMEM((2 * count, width), BF16)],
        limit=32,
        flops=3_200_000_000,
        name="own_edges",
    )

    (results,) = kernel_call(
        coarse_body,
        [((chips, BLOCK, width), BF16)],
        [in_planes, own_latent, own_hidden, both, coarse_w3],
        after=[own_edges],
        name="coarse_update",
    )
    mine = lax.all_to_all(results, PLANE, 0, 0).reshape(half, width)
    edges, select, own_pick = kernel_call(
        functools.partial(rest_edges_body, mids),
        [((edge_count, width), BF16), ((edge_count, 2 * LANES), BF16), ((count, LANES), BF16)],
        [source, target, parent, halo_before, halo_after, edge_w_src, own_edges],
        after=[results],
        scratch=[pltpu.VMEM((2 * LANES, width), BF16), pltpu.VMEM((2 * count + 2 * LANES, 2 * LANES), BF16)],
        limit=32,
        flops=3_000_000_000,
        name="rest_edges",
    )
    theirs = swapped(mine)

    fine_out, mid_out, coarse_out = kernel_call(
        final_body,
        [((count, width), BF16), ((mids, width), BF16), ((coarse_count, width), BF16)],
        [mine, theirs, before, pair, after, edges, select, target, fine_latent, own_pick, node]
        + [w_descend, w_fine, edge_w_src, edge_w_dst, node_w1, edge_w2, node_w2, node_w3],
        scratch=[
            pltpu.VMEM((2 * half, width), BF16),
            pltpu.VMEM((6 * mids, wide), BF16),
            pltpu.VMEM((8 * mids, width), BF16),
            pltpu.VMEM((count, width), F32),
        ],
        limit=32,
        name="final",
    )
    return (fine_out, mid_out, coarse_out)


def solution(mesh):
    groups, tiles = mesh.shape["rhombus"], mesh.shape["tile"]
    side = {32: (4, 4), 8: (2, 2)}[tiles]
    physical = jax.sharding.Mesh(mesh.devices.reshape(groups, *side, 2), ("z", "y", "x", "c"))
    every = ("z", "y", "x", "c")
    split, copied = P(every), P()
    return jax.shard_map(
        on_device,
        mesh=physical,
        in_specs=(split, split, copied) + (split,) * 5 + (copied,) * 16,
        out_specs=(split, split, copied),
        check_vma=False,
    )
```

```python
import functools

import jax
import jax.numpy as jnp
from jax import lax
from jax.experimental import pallas as pl
from jax.experimental.pallas import tpu as pltpu
from jax.sharding import PartitionSpec as P

EPSILON = 1e-05
BLOCK = 24
LANES = 128
CHUNK = 512
PLANE = ("y", "x")
TILE = ("y", "x", "c")
F32, BF16, I32 = jnp.float32, jnp.bfloat16, jnp.int32
VMEM = pl.BlockSpec(memory_space=pltpu.VMEM)
STORED = pl.BlockSpec(memory_space=pltpu.HBM)
UNREAD = pl.BlockSpec(memory_space=pl.ANY)


class Copied:
    def __init__(self, source, target, semaphore):
        self.copy = pltpu.make_async_copy(source, target, semaphore)
        self.target, self.waiting = target, True
        self.copy.start()

    def get(self):
        if self.waiting:
            self.copy.wait()
            self.waiting = False
        return self.target

    def __getitem__(self, index):
        return self.get()[index]

    @property
    def shape(self):
        return self.target.shape


def kernel_call(body, outs, operands, stored=(), after=(), scratch=(), keep=(), limit=8, flops=0, name=None):
    count, held, skipped, given = len(operands), len(stored), len(after), len(outs)
    target = dict(keep)

    def kernel(*refs):
        inputs, refs = refs[:count], refs[count:]
        sources, refs = refs[:held], refs[held + skipped :]
        results, refs = refs[:given], refs[given:]
        own, refs = refs[: len(scratch)], refs[len(scratch) :]
        buffers = iter(refs)
        places = [results[target[i]] if i in target else next(buffers) for i in range(held)]
        semaphores = next(buffers) if held else None
        copies = [Copied(sources[i], places[i], semaphores.at[i]) for i in range(held)]
        fresh = [results[o] for o in range(given) if o not in target.values()]
        body(*inputs, *copies, *fresh, *own)
        for copy in copies:
            copy.get()

    buffers = [pltpu.VMEM(stored[i].shape, stored[i].dtype) for i in range(held) if i not in target]
    if held:
        buffers.append(pltpu.SemaphoreType.DMA((held,)))
    return pl.pallas_call(
        kernel,
        out_shape=outs,
        in_specs=[VMEM] * count + [STORED] * held + [UNREAD] * skipped,
        out_specs=[VMEM] * given,
        scratch_shapes=[*scratch, *buffers],
        compiler_params=pltpu.CompilerParams(vmem_limit_bytes=limit << 20),
        cost_estimate=pl.CostEstimate(flops=flops, bytes_accessed=1 << 20, transcendentals=0),
        name=name,
    )(*operands, *[pltpu.with_memory_space_constraint(array, pltpu.HBM) for array in stored], *after)


def product(left, right):
    return jnp.dot(left, right, preferred_element_type=F32)


def silu(values):
    half = 0.5 * values
    return half + half * jnp.tanh(half)


def updated(latent, hidden, third):
    values = product(hidden.astype(BF16), third)
    scale = lax.rsqrt(jnp.mean(values * values, axis=-1, keepdims=True) + EPSILON)
    return (latent.astype(F32) + values * scale).astype(BF16)


def lanes(height, first=0):
    return lax.broadcasted_iota(I32, (height, LANES), 1) + first


def spread(row):
    return jnp.broadcast_to(row, (LANES, LANES)).T


def hot(mask):
    return jnp.where(mask, 1.0, 0.0).astype(BF16)


def picks(spread_ids, first, blocks):
    return [hot(spread_ids == lanes(LANES, first + LANES * q)) for q in range(blocks)]


def sums_body(parent, fine, own, up, down):
    count = own.shape[0]
    rows = lax.broadcasted_iota(I32, (3 * count, LANES), 0)
    blocks = [hot(rows == parent[r : r + 1, :]) for r in range(parent.shape[0])]
    sums = product(jnp.concatenate(blocks, axis=1), fine[...])
    own[...] = sums[:count]
    down[...] = sums[count : 2 * count].astype(BF16)
    up[...] = sums[2 * count :].astype(BF16)


def mid_ready_body(latent, ids, first, w_child, second, third, kept, hidden, labels):
    count = hidden.shape[0]
    spread_ids = spread(jnp.concatenate([ids[...], jnp.zeros((1, LANES - count), I32)], axis=1))[:count]
    place = lanes(count)
    label = jnp.where(place == 0, spread_ids >> 5, jnp.where(place == 1, spread_ids & 31, 0))
    labels[...] = label.astype(F32).astype(BF16)
    values = latent[...]
    kept[...] = values
    hidden[...] = product(values, first[...])


def mid_body(own, before, after, latent, hidden, labels, w_child, second, third, out):
    width = latent.shape[1]
    total = own[...] + before[...].astype(F32) + after[...].astype(F32)
    incoming = product(total.astype(BF16), w_child[...]).astype(BF16)
    value = silu(hidden[...] + product(incoming, second[...]))
    out[:, :width] = updated(latent[...], value, third[...])
    out[:, width:] = labels[...]


def row_ids(labelled, width):
    label = labelled[:, width:].astype(F32)
    return (label[:, :1] * 32.0 + label[:, 1:2]).astype(I32)


def blocks_body(mine, theirs, pair, out):
    count, width = mine.shape[0], out.shape[1]
    half = out.shape[0]
    core = lax.axis_index("c")
    pair[pl.ds(pl.multiple_of(core * count, count), count), :] = mine[...]
    pair[pl.ds(pl.multiple_of((1 - core) * count, count), count), :] = theirs[...]
    both = pair[...]
    columns = lax.broadcasted_iota(I32, (2 * count, half), 1) + core * half
    picked = hot(row_ids(both, width) == columns)
    out[...] = lax.dot_general(
        picked, both[:, :width], (((0,), (0,)), ((), ())), preferred_element_type=F32
    ).astype(BF16)


def tables_body(parent, halo, fine, w_src, w_dst, w_node, sender, receiver, node, down, up, token):
    token[...] = jnp.zeros_like(token)
    count, width = fine.shape
    blocks = count // LANES
    values = fine[...]
    codes = [(spread(parent[r : r + 1, :]) + 1).astype(F32).astype(BF16) for r in range(blocks)]
    codes = jnp.concatenate(codes, axis=0)
    for r, out in enumerate((down, up)):
        picked = jnp.concatenate(picks(spread(halo[r : r + 1, :]), 0, blocks), axis=1)
        out[:, :width] = product(picked, values).astype(BF16)
        out[:, width:] = product(picked, codes).astype(BF16)
    sender[...] = product(values, w_src[...]).astype(BF16)
    receiver[...] = product(values, w_dst[...]).astype(BF16)
    node[...] = product(values, w_node[...])


def gather_body(parts, out):
    total = jnp.sum(parts[...].astype(F32), axis=0).astype(BF16)
    for i in range(out.shape[0]):
        out[i] = total


def coarse_body(parts, own_latent, own_hidden, both, third, out):
    total = jnp.sum(parts[...].astype(F32), axis=0).astype(BF16)
    hidden = silu(own_hidden[...] + product(total, both[...]))
    result = updated(own_latent[...], hidden, third[...])
    for i in range(out.shape[0]):
        out[i] = result


def own_edges_body(
    source, target, sender, receiver, coarse, coarse_w1, w_coarse, coarse_w2, third, out, both, own_latent, own_hidden
):
    count = sender.shape[0]
    blocks = count // LANES
    sent, received = sender[...], receiver[...]
    for k in range(out.shape[0] // CHUNK):
        marks = range(k * CHUNK // LANES, (k + 1) * CHUNK // LANES)
        picked = [jnp.concatenate(picks(spread(source[r : r + 1, :]), 0, blocks), axis=1) for r in marks]
        total = product(jnp.concatenate(picked, axis=0), sent)
        picked = [jnp.concatenate(picks(spread(target[r : r + 1, :]), 0, blocks), axis=1) for r in marks]
        total += product(jnp.concatenate(picked, axis=0), received)
        out[k * CHUNK : (k + 1) * CHUNK, :] = total.astype(BF16)
    rows, total = own_latent.shape[0], coarse.shape[0]
    chips = lax.axis_size("y") * lax.axis_size("x")
    chip = lax.axis_index("y") * lax.axis_size("x") + lax.axis_index("x")
    first = (lax.axis_index("c") * chips + chip) * rows
    place = lax.broadcasted_iota(I32, (rows, total), 0) + first
    picked = hot(place == lax.broadcasted_iota(I32, (rows, total), 1))
    latent = product(picked, coarse[...]).astype(BF16)
    own_latent[...] = latent
    own_hidden[...] = product(latent, coarse_w1[...])
    both[...] = product(w_coarse[...], coarse_w2[...]).astype(BF16)


def slots(codes, tile, count):
    parent = codes - 1
    side = parent // count
    away = jnp.where(side == 1, -1, jnp.where(side == 2, 1, 0))
    return jnp.where(codes > 0, (tile + away) * count + (parent & (count - 1)), -1)


def rest_edges_body(
    mid_count, first, source, target, parent, before, after, w_src, out, select, own_pick, token, table, where
):
    token[...] = jnp.zeros_like(token)
    count = own_pick.shape[0]
    width = out.shape[1]
    blocks = count // LANES
    for r in range(blocks):
        place = slots(spread(parent[r : r + 1, :]) + 1, 2, mid_count)
        rows = slice(r * LANES, (r + 1) * LANES)
        where[rows, :] = jnp.concatenate(picks(place, 0, 2), axis=1)
        near = place - mid_count
        own_pick[rows, :] = hot(near == lanes(LANES))
        far = place + 4 * mid_count
        there = slice(count + 2 * LANES + r * LANES, count + 2 * LANES + (r + 1) * LANES)
        where[there, :] = jnp.concatenate(picks(far, 0, 2), axis=1)
    for r, (halo, tile) in enumerate(((before, 1), (after, 3))):
        values = halo[...]
        rows = slice(r * LANES, (r + 1) * LANES)
        table[rows, :] = product(values[:, :width], w_src[...]).astype(BF16)
        place = slots(values[:, width:].astype(F32).astype(I32), tile, mid_count)
        where[count + r * LANES : count + (r + 1) * LANES, :] = jnp.concatenate(picks(place, 0, 2), axis=1)
    for k in range(out.shape[0] // CHUNK):
        rows = []
        for r in range(k * CHUNK // LANES, (k + 1) * CHUNK // LANES):
            row = picks(spread(source[r : r + 1, :]), 0, blocks + 2)
            row += picks(spread(target[r : r + 1, :]), 0, blocks)
            rows.append(jnp.concatenate(row, axis=1))
        picked = jnp.concatenate(rows, axis=0)
        here = slice(k * CHUNK, (k + 1) * CHUNK)
        select[here, :] = product(picked, where[...]).astype(BF16)
        rest = product(picked[:, count : count + 2 * LANES], table[...])
        out[here, :] = (first[here, :].astype(F32) + rest).astype(BF16)


def ready_body(rows, before, pair, after, w_descend, w_fine, w_src, w_dst, middle, picked, window):
    two = pair.shape[0]
    count, width = two // 2, middle.shape[1]
    window[:two] = before[...]
    window[two : 2 * two] = pair[...]
    window[2 * two :] = after[...]
    near = window[pl.ds(pl.multiple_of(lax.axis_index("c") * count, count), 5 * count), :]
    middle[...] = near[:, :width]
    picked[...] = hot(row_ids(near, width) == lax.broadcasted_iota(I32, (5 * count, rows), 1))


def final_body(
    mine, theirs, w_descend, w_fine, w_src, w_dst, near, picked, target, select, edges, edge_w2, own_pick, fine,
    w_node, node, node_w2, node_w3, fine_out, mid_out, coarse_out, coarse, table, sums,
):
    core = lax.axis_index("c")
    half, width = mine.shape
    count = near.shape[0] // 5
    coarse[pl.ds(pl.multiple_of(core * half, half), half), :] = mine[...]
    coarse[pl.ds(pl.multiple_of((1 - core) * half, half), half), :] = theirs[...]
    parents = product(picked[...], coarse[...]).astype(BF16)
    down = product(parents, w_descend[...]).astype(BF16)
    middle = (near[...].astype(F32) + down.astype(F32)).astype(BF16)
    mid_out[...] = middle[2 * count : 3 * count]
    fine_down = product(middle, w_fine[...]).astype(BF16)
    closer = fine_down[count : 4 * count]
    table[: 5 * count] = product(fine_down, w_src[...]).astype(BF16)
    table[5 * count :] = product(closer, w_dst[...]).astype(BF16)
    rows = lax.broadcasted_iota(I32, (fine.shape[0], LANES), 0)
    for k in range(edges.shape[0] // CHUNK):
        here = slice(k * CHUNK, (k + 1) * CHUNK)
        edge_sum = edges[here, :].astype(F32) + product(select[here, :], table[...])
        hidden = silu(edge_sum).astype(BF16)
        marks = range(k * CHUNK // LANES, (k + 1) * CHUNK // LANES)
        scatter = jnp.concatenate([hot(rows == target[r : r + 1, :]) for r in marks], axis=1)
        part = product(scatter, hidden)
        if k == 0:
            sums[...] = part
        else:
            sums[...] += part
    coarse_out[...] = coarse[: coarse_out.shape[0], :]
    reach = fine_down[count : 5 * count]
    lifted = (fine[...].astype(F32) + product(own_pick[...], reach)).astype(BF16)
    near_node = product(reach, w_node[...]).astype(BF16)
    aggregate = product(sums[...].astype(BF16), edge_w2[...]).astype(BF16)
    hidden = silu(node[...] + product(own_pick[...], near_node) + product(aggregate, node_w2[...]))
    fine_out[...] = updated(lifted, hidden, node_w3[...])


def shifted(values, axis, step, size):
    pairs = [(i, i + step) for i in range(size) if 0 <= i + step < size]
    return lax.ppermute(values, axis, pairs)


def swapped(values):
    return lax.ppermute(values, "c", [(0, 1), (1, 0)])


def on_device(
    fine_latent,
    mid_latent,
    coarse_latent,
    fine_parent,
    mid_parent,
    halo_rows,
    edge_source,
    edge_target,
    w_child,
    mid_w1,
    mid_w2,
    mid_w3,
    w_coarse,
    coarse_w1,
    coarse_w2,
    coarse_w3,
    w_descend,
    w_fine,
    edge_w_src,
    edge_w_dst,
    edge_w2,
    node_w1,
    node_w2,
    node_w3,
):
    count, width = fine_latent.shape
    mids = mid_latent.shape[0]
    coarse_count = coarse_latent.shape[0]
    edge_count = edge_source.shape[0]
    planes, chips = lax.axis_size("z"), lax.axis_size("y") * lax.axis_size("x")
    tiles = 2 * chips
    half = chips * BLOCK
    wide = width + LANES
    parent = fine_parent.reshape(-1, LANES)
    source = edge_source.reshape(-1, LANES)
    target = edge_target.reshape(-1, LANES)
    halo = halo_rows.reshape(-1, LANES)

    def near(*shape, dtype=BF16):
        return pltpu.VMEM(shape, dtype)

    def far(*shape, dtype=BF16):
        return pltpu.HBM(shape, dtype)

    def here(array):
        return pltpu.with_memory_space_constraint(array, pltpu.VMEM)

    def free(*shape, dtype=BF16):
        return jax.ShapeDtypeStruct(shape, dtype)

    square = near(width, width)
    own, up, down = kernel_call(
        sums_body,
        [near(mids, width, dtype=F32), free(mids, width), free(mids, width)],
        [],
        stored=[parent, fine_latent],
        name="child_sums",
    )
    from_before = shifted(up, TILE, 1, tiles)
    from_after = shifted(down, TILE, -1, tiles)
    w_child, mid_w2, mid_w3, kept, hidden, labels = kernel_call(
        mid_ready_body,
        [square, square, square, near(mids, width), near(mids, width, dtype=F32), near(mids, LANES)],
        [],
        stored=[mid_latent, mid_parent[None], mid_w1, w_child, mid_w2, mid_w3],
        keep=[(3, 0), (4, 1), (5, 2)],
        after=[own],
        flops=1_000_000_000,
        name="mid_ready",
    )
    (labelled,) = kernel_call(
        mid_body,
        [free(mids, wide)],
        [here(own), from_before, from_after] + [here(a) for a in (kept, hidden, labels, w_child, mid_w2, mid_w3)],
        name="mid_update",
    )
    other = swapped(labelled)
    pair, blocks = kernel_call(
        blocks_body,
        [free(2 * mids, wide), near(half, width)],
        [labelled, other],
        name="coarse_blocks",
    )

    blocks = blocks.reshape(chips, BLOCK, width)
    parts = lax.all_to_all(blocks, PLANE, 0, 0)
    before = shifted(pair, PLANE, 1, chips)
    after = shifted(pair, PLANE, -1, chips)
    sender, receiver, node, halo_down, halo_up, token = kernel_call(
        tables_body,
        [far(count, width), far(count, width), far(count, width, dtype=F32), free(LANES, wide), free(LANES, wide), free(8, LANES)],
        [],
        stored=[parent, halo, fine_latent, edge_w_src, edge_w_dst, node_w1],
        after=[blocks],
        limit=12,
        flops=2_000_000_000,
        name="tables",
    )

    (own_parts,) = kernel_call(
        gather_body,
        [near(planes, BLOCK, width)],
        [parts],
        after=[token, before, after],
        name="plane_sum",
    )
    in_planes = lax.all_to_all(own_parts, "z", 0, 0)
    halo_down, halo_up, _ = lax.optimization_barrier((halo_down, halo_up, own_parts))
    halo_before = shifted(halo_up, TILE, 1, tiles)
    halo_after = shifted(halo_down, TILE, -1, tiles)
    coarse_w3, own_edges, both, own_latent, own_hidden = kernel_call(
        own_edges_body,
        [square, far(edge_count, width), square, near(BLOCK, width), near(BLOCK, width, dtype=F32)],
        [],
        stored=[source, target, sender, receiver, coarse_latent, coarse_w1, w_coarse, coarse_w2, coarse_w3],
        keep=[(8, 0)],
        after=[own_parts],
        limit=16,
        flops=3_500_000_000,
        name="own_edges",
    )

    (results,) = kernel_call(
        coarse_body,
        [near(chips, BLOCK, width)],
        [in_planes] + [here(a) for a in (own_latent, own_hidden, both, coarse_w3)],
        after=[halo_before, halo_after],
        name="coarse_update",
    )
    mine = lax.all_to_all(results, PLANE, 0, 0).reshape(half, width)
    edges, select, own_pick, token = kernel_call(
        functools.partial(rest_edges_body, mids),
        [far(edge_count, width), far(edge_count, 2 * LANES), far(count, LANES), free(8, LANES)],
        [],
        stored=[own_edges, source, target, parent, halo_before, halo_after, edge_w_src],
        after=[results],
        scratch=[pltpu.VMEM((2 * LANES, width), BF16), pltpu.VMEM((2 * count + 2 * LANES, 2 * LANES), BF16)],
        limit=24,
        flops=3_500_000_000,
        name="rest_edges",
    )
    mine, own_pick = lax.optimization_barrier((mine, own_pick))
    theirs = swapped(mine)
    w_descend, w_fine, w_src, w_dst, middle, picked = kernel_call(
        functools.partial(ready_body, 2 * half),
        [square] * 4 + [near(5 * mids, width), near(5 * mids, 2 * half)],
        [],
        stored=[before, pair, after, w_descend, w_fine, edge_w_src, edge_w_dst],
        keep=[(3, 0), (4, 1), (5, 2), (6, 3)],
        after=[mine, token],
        scratch=[pltpu.VMEM((6 * mids, wide), BF16)],
        flops=1_000_000_000,
        name="final_ready",
    )

    fine_out, mid_out, coarse_out = kernel_call(
        final_body,
        [free(count, width), free(mids, width), free(coarse_count, width)],
        [mine, theirs] + [here(a) for a in (w_descend, w_fine, w_src, w_dst, middle, picked)],
        stored=[target, select, edges, edge_w2, own_pick, fine_latent, node_w1, node, node_w2, node_w3],
        scratch=[
            pltpu.VMEM((2 * half, width), BF16),
            pltpu.VMEM((8 * mids, width), BF16),
            pltpu.VMEM((count, width), F32),
        ],
        limit=24,
        name="final",
    )
    return (fine_out, mid_out, coarse_out)


def solution(mesh):
    groups, tiles = mesh.shape["rhombus"], mesh.shape["tile"]
    side = {32: (4, 4), 8: (2, 2)}[tiles]
    physical = jax.sharding.Mesh(mesh.devices.reshape(groups, *side, 2), ("z", "y", "x", "c"))
    every = ("z", "y", "x", "c")
    split, copied = P(every), P()
    return jax.shard_map(
        on_device,
        mesh=physical,
        in_specs=(split, split, copied) + (split,) * 5 + (copied,) * 16,
        out_specs=(split, split, copied),
        check_vma=False,
    )
```

```python
import functools

import jax
import jax.numpy as jnp
from jax import lax
from jax.experimental import pallas as pl
from jax.experimental.pallas import tpu as pltpu
from jax.sharding import PartitionSpec as P

EPSILON = 1e-05
BLOCK = 24
LANES = 128
CHUNK = 512
PLANE = ("y", "x")
TILE = ("y", "x", "c")
F32, BF16, I32 = jnp.float32, jnp.bfloat16, jnp.int32
VMEM = pl.BlockSpec(memory_space=pltpu.VMEM)
STORED = pl.BlockSpec(memory_space=pltpu.HBM)
UNREAD = pl.BlockSpec(memory_space=pl.ANY)


class Copied:
    def __init__(self, source, target, semaphores, first=0, pieces=1):
        rows = target.shape[0] // pieces
        self.target, self.copies = target, []
        for k in range(pieces):
            part = slice(k * rows, (k + 1) * rows) if pieces > 1 else slice(None)
            self.copies.append(pltpu.make_async_copy(source.at[part], target.at[part], semaphores.at[first + k]))
        self.waiting = [False] * pieces

    def start(self, k=None):
        for i in range(len(self.copies)) if k is None else (k,):
            self.copies[i].start()
            self.waiting[i] = True
        return self

    def get(self, k=None):
        for i in range(len(self.copies)) if k is None else (k,):
            if self.waiting[i]:
                self.copies[i].wait()
                self.waiting[i] = False
        return self.target

    def __getitem__(self, index):
        return self.get()[index]

    @property
    def shape(self):
        return self.target.shape


def kernel_call(
    body, outs, operands, stored=(), after=(), scratch=(), keep=(), streams=(), pieces=(), limit=8, flops=0, name=None
):
    count, held, skipped, given = len(operands), len(stored), len(after), len(outs)
    target = dict(keep)
    cuts = [stored[i].shape[0] // CHUNK if i in pieces else 1 for i in range(held)]
    flows = {o: outs[o].shape[0] // CHUNK for o in streams}

    def kernel(*refs):
        inputs, refs = refs[:count], refs[count:]
        sources, refs = refs[:held], refs[held + skipped :]
        results, refs = refs[:given], refs[given:]
        own, refs = refs[: len(scratch)], refs[len(scratch) :]
        buffers = iter(refs)
        places = [results[target[i]] if i in target else next(buffers) for i in range(held)]
        leaving = {o: next(buffers) for o in streams}
        semaphores = next(buffers) if held or streams else None
        first, copies, fresh = 0, [], []
        for i in range(held):
            copies.append(Copied(sources[i], places[i], semaphores, first, cuts[i]).start())
            first += cuts[i]
        for o in range(given):
            if o in flows:
                fresh.append(Copied(leaving[o], results[o], semaphores, first, flows[o]))
                first += flows[o]
            elif o not in target.values():
                fresh.append(results[o])
        body(*inputs, *copies, *fresh, *[leaving[o] for o in streams], *own)
        for copy in copies + fresh:
            if isinstance(copy, Copied):
                copy.get()

    buffers = [pltpu.VMEM(stored[i].shape, stored[i].dtype) for i in range(held) if i not in target]
    buffers += [pltpu.VMEM(outs[o].shape, outs[o].dtype) for o in streams]
    if held or streams:
        buffers.append(pltpu.SemaphoreType.DMA((sum(cuts) + sum(flows.values()),)))
    return pl.pallas_call(
        kernel,
        out_shape=outs,
        in_specs=[VMEM] * count + [STORED] * held + [UNREAD] * skipped,
        out_specs=[STORED if o in flows else VMEM for o in range(given)],
        scratch_shapes=[*scratch, *buffers],
        compiler_params=pltpu.CompilerParams(vmem_limit_bytes=limit << 20),
        cost_estimate=pl.CostEstimate(flops=flops, bytes_accessed=1 << 20, transcendentals=0),
        name=name,
    )(*operands, *[pltpu.with_memory_space_constraint(array, pltpu.HBM) for array in stored], *after)


def product(left, right):
    return jnp.dot(left, right, preferred_element_type=F32)


def silu(values):
    half = 0.5 * values
    return half + half * jnp.tanh(half)


def updated(latent, hidden, third):
    values = product(hidden.astype(BF16), third)
    scale = lax.rsqrt(jnp.mean(values * values, axis=-1, keepdims=True) + EPSILON)
    return (latent.astype(F32) + values * scale).astype(BF16)


def lanes(height, first=0):
    return lax.broadcasted_iota(I32, (height, LANES), 1) + first


def spread(row):
    return jnp.broadcast_to(row, (LANES, LANES)).T


def hot(mask):
    return jnp.where(mask, 1.0, 0.0).astype(BF16)


def picks(spread_ids, first, blocks):
    return [hot(spread_ids == lanes(LANES, first + LANES * q)) for q in range(blocks)]


def sums_body(parent, fine, own, swap, cross):
    count = own.shape[0]
    core = lax.axis_index("c")
    rows = lax.broadcasted_iota(I32, (3 * count, LANES), 0)
    blocks = [hot(rows == parent[r : r + 1, :]) for r in range(parent.shape[0])]
    sums = product(jnp.concatenate(blocks, axis=1), fine[...])
    own[...] = sums[:count]
    down, up = sums[count : 2 * count].astype(BF16), sums[2 * count :].astype(BF16)
    swap[...] = jnp.where(core == 0, up, down)
    cross[...] = jnp.where(core == 0, down, up)


def mid_ready_body(latent, ids, first, w_child, second, third, kept, hidden, labels):
    count = hidden.shape[0]
    spread_ids = spread(jnp.concatenate([ids[...], jnp.zeros((1, LANES - count), I32)], axis=1))[:count]
    place = lanes(count)
    label = jnp.where(place == 0, spread_ids >> 5, jnp.where(place == 1, spread_ids & 31, 0))
    labels[...] = label.astype(F32).astype(BF16)
    values = latent[...]
    kept[...] = values
    hidden[...] = product(values, first[...])


def mid_body(own, before, after, latent, hidden, labels, w_child, second, third, out):
    width = latent.shape[1]
    total = own[...] + before[...].astype(F32) + after[...].astype(F32)
    incoming = product(total.astype(BF16), w_child[...]).astype(BF16)
    value = silu(hidden[...] + product(incoming, second[...]))
    out[:, :width] = updated(latent[...], value, third[...])
    out[:, width:] = labels[...]


def row_ids(labelled, width):
    label = labelled[:, width:].astype(F32)
    return (label[:, :1] * 32.0 + label[:, 1:2]).astype(I32)


def blocks_body(mine, theirs, pair, out):
    count, width = mine.shape[0], out.shape[1]
    half = out.shape[0]
    core = lax.axis_index("c")
    pair[pl.ds(pl.multiple_of(core * count, count), count), :] = mine[...]
    pair[pl.ds(pl.multiple_of((1 - core) * count, count), count), :] = theirs[...]
    both = pair[...]
    columns = lax.broadcasted_iota(I32, (2 * count, half), 1) + core * half
    picked = hot(row_ids(both, width) == columns)
    out[...] = lax.dot_general(
        picked, both[:, :width], (((0,), (0,)), ((), ())), preferred_element_type=F32
    ).astype(BF16)


def boundary_body(parent, halo, fine, pair, swap, cross):
    count, width = fine.shape
    two, blocks = pair.shape[0], count // LANES
    core = lax.axis_index("c")
    codes = [(spread(parent[r : r + 1, :]) + 1).astype(F32).astype(BF16) for r in range(blocks)]
    codes = jnp.concatenate(codes, axis=0)
    rows = halo[...]
    for out, first, row in (
        (swap, 0, jnp.where(core == 0, rows[1:2], rows[:1])),
        (cross, two, jnp.where(core == 0, rows[:1], rows[1:2])),
    ):
        picked = jnp.concatenate(picks(spread(row), 0, blocks), axis=1)
        out[first : first + LANES, :width] = product(picked, fine[...]).astype(BF16)
        out[first : first + LANES, width:] = product(picked, codes).astype(BF16)
    cross[:two] = pair[...]


def tables_body(fine, w_src, w_dst, w_node, sender, receiver, node, token):
    token[...] = jnp.zeros_like(token)
    values = fine[...]
    sender[...] = product(values, w_src[...]).astype(BF16)
    receiver[...] = product(values, w_dst[...]).astype(BF16)
    node[...] = product(values, w_node[...])


def gather_body(parts, out):
    total = jnp.sum(parts[...].astype(F32), axis=0).astype(BF16)
    for i in range(out.shape[0]):
        out[i] = total


def coarse_body(parts, own_latent, own_hidden, both, third, out):
    total = jnp.sum(parts[...].astype(F32), axis=0).astype(BF16)
    hidden = silu(own_hidden[...] + product(total, both[...]))
    result = updated(own_latent[...], hidden, third[...])
    for i in range(out.shape[0]):
        out[i] = result


def own_edges_body(
    source, target, sender, receiver, coarse, coarse_w1, w_coarse, coarse_w2, edge_w2, node_w2, third,
    sent_out, both, last, own_latent, own_hidden, out,
):
    count = sender.shape[0]
    blocks = count // LANES
    sent, received = sender[...], receiver[...]
    for k in range(out.shape[0] // CHUNK):
        marks = range(k * CHUNK // LANES, (k + 1) * CHUNK // LANES)
        picked = [jnp.concatenate(picks(spread(source[r : r + 1, :]), 0, blocks), axis=1) for r in marks]
        total = product(jnp.concatenate(picked, axis=0), sent)
        picked = [jnp.concatenate(picks(spread(target[r : r + 1, :]), 0, blocks), axis=1) for r in marks]
        total += product(jnp.concatenate(picked, axis=0), received)
        out[k * CHUNK : (k + 1) * CHUNK, :] = total.astype(BF16)
        sent_out.start(k)
    last[...] = product(edge_w2[...], node_w2[...]).astype(BF16)
    rows, total = own_latent.shape[0], coarse.shape[0]
    chips = lax.axis_size("y") * lax.axis_size("x")
    chip = lax.axis_index("y") * lax.axis_size("x") + lax.axis_index("x")
    first = (lax.axis_index("c") * chips + chip) * rows
    place = lax.broadcasted_iota(I32, (rows, total), 0) + first
    picked = hot(place == lax.broadcasted_iota(I32, (rows, total), 1))
    latent = product(picked, coarse[...]).astype(BF16)
    own_latent[...] = latent
    own_hidden[...] = product(latent, coarse_w1[...])
    both[...] = product(w_coarse[...], coarse_w2[...]).astype(BF16)


def slots(codes, tile, count):
    parent = codes - 1
    side = parent // count
    away = jnp.where(side == 1, -1, jnp.where(side == 2, 1, 0))
    return jnp.where(codes > 0, (tile + away) * count + (parent & (count - 1)), -1)


def rest_edges_body(
    mid_count, source, target, parent, cross, swap, w_src, first, sent_out, sent_select, own_pick, token,
    out, select, table, where
):
    token[...] = jnp.zeros_like(token)
    core = lax.axis_index("c")
    count = own_pick.shape[0]
    width = out.shape[1]
    blocks = count // LANES
    two = cross.shape[0] - LANES
    for r in range(blocks):
        place = slots(spread(parent[r : r + 1, :]) + 1, 2, mid_count)
        rows = slice(r * LANES, (r + 1) * LANES)
        where[rows, :] = jnp.concatenate(picks(place, 0, 2), axis=1)
        near = place - mid_count
        own_pick[rows, :] = hot(near == lanes(LANES))
        far = place + 4 * mid_count
        there = slice(count + 2 * LANES + r * LANES, count + 2 * LANES + (r + 1) * LANES)
        where[there, :] = jnp.concatenate(picks(far, 0, 2), axis=1)
    for values, late in ((cross[two:], core), (swap[...], 1 - core)):
        rows = pl.ds(pl.multiple_of(late * LANES, LANES), LANES)
        table[rows, :] = product(values[:, :width], w_src[...]).astype(BF16)
        place = slots(values[:, width:].astype(F32).astype(I32), 1 + 2 * late, mid_count)
        rows = pl.ds(pl.multiple_of(count + late * LANES, LANES), LANES)
        where[rows, :] = jnp.concatenate(picks(place, 0, 2), axis=1)
    for k in range(out.shape[0] // CHUNK):
        rows = []
        for r in range(k * CHUNK // LANES, (k + 1) * CHUNK // LANES):
            row = picks(spread(source[r : r + 1, :]), 0, blocks + 2)
            row += picks(spread(target[r : r + 1, :]), 0, blocks)
            rows.append(jnp.concatenate(row, axis=1))
        picked = jnp.concatenate(rows, axis=0)
        here = slice(k * CHUNK, (k + 1) * CHUNK)
        select[here, :] = product(picked, where[...]).astype(BF16)
        sent_select.start(k)
        rest = product(picked[:, count : count + 2 * LANES], table[...])
        out[here, :] = (first.get(k)[here, :].astype(F32) + rest).astype(BF16)
        sent_out.start(k)


def ready_body(rows, cross, pair, swap, w_descend, w_fine, w_src, w_dst, middle, picked, window):
    core = lax.axis_index("c")
    two = pair.shape[0]
    count, width = two // 2, middle.shape[1]
    window[pl.ds(pl.multiple_of((1 - core) * 4 * count, count), count), :] = swap[...]
    window[pl.ds(pl.multiple_of(core * 3 * count, count), two), :] = cross[:two]
    window[pl.ds(pl.multiple_of((2 - core) * count, count), two), :] = pair[...]
    near = window[...]
    middle[...] = near[:, :width]
    picked[...] = hot(row_ids(near, width) == lax.broadcasted_iota(I32, (5 * count, rows), 1))


def final_body(
    mine, theirs, w_descend, w_fine, w_src, w_dst, near, picked, target, select, edges, own_pick, fine,
    w_node, last, node, node_w3, fine_out, mid_out, coarse_out, coarse, table, sums,
):
    core = lax.axis_index("c")
    half, width = mine.shape
    count = near.shape[0] // 5
    coarse[pl.ds(pl.multiple_of(core * half, half), half), :] = mine[...]
    coarse[pl.ds(pl.multiple_of((1 - core) * half, half), half), :] = theirs[...]
    parents = product(picked[...], coarse[...]).astype(BF16)
    down = product(parents, w_descend[...]).astype(BF16)
    middle = (near[...].astype(F32) + down.astype(F32)).astype(BF16)
    mid_out[...] = middle[2 * count : 3 * count]
    fine_down = product(middle, w_fine[...]).astype(BF16)
    closer = fine_down[count : 4 * count]
    table[: 5 * count] = product(fine_down, w_src[...]).astype(BF16)
    table[5 * count :] = product(closer, w_dst[...]).astype(BF16)
    rows = lax.broadcasted_iota(I32, (fine.shape[0], LANES), 0)
    for k in range(edges.shape[0] // CHUNK):
        here = slice(k * CHUNK, (k + 1) * CHUNK)
        edge_sum = edges.get(k)[here, :].astype(F32) + product(select.get(k)[here, :], table[...])
        hidden = silu(edge_sum).astype(BF16)
        marks = range(k * CHUNK // LANES, (k + 1) * CHUNK // LANES)
        scatter = jnp.concatenate([hot(rows == target[r : r + 1, :]) for r in marks], axis=1)
        part = product(scatter, hidden)
        if k == 0:
            sums[...] = part
        else:
            sums[...] += part
    coarse_out[...] = coarse[: coarse_out.shape[0], :]
    reach = fine_down[count : 5 * count]
    lifted = (fine[...].astype(F32) + product(own_pick[...], reach)).astype(BF16)
    near_node = product(reach, w_node[...]).astype(BF16)
    hidden = silu(node[...] + product(own_pick[...], near_node) + product(sums[...].astype(BF16), last[...]))
    fine_out[...] = updated(lifted, hidden, node_w3[...])


def swapped(values):
    return lax.ppermute(values, "c", [(0, 1), (1, 0)])


def crossed(values, tiles):
    pairs = [(t, t + 1) for t in range(1, tiles - 1, 2)]
    return lax.ppermute(values, TILE, pairs + [(b, a) for a, b in pairs])


def on_device(
    fine_latent,
    mid_latent,
    coarse_latent,
    fine_parent,
    mid_parent,
    halo_rows,
    edge_source,
    edge_target,
    w_child,
    mid_w1,
    mid_w2,
    mid_w3,
    w_coarse,
    coarse_w1,
    coarse_w2,
    coarse_w3,
    w_descend,
    w_fine,
    edge_w_src,
    edge_w_dst,
    edge_w2,
    node_w1,
    node_w2,
    node_w3,
):
    count, width = fine_latent.shape
    mids = mid_latent.shape[0]
    coarse_count = coarse_latent.shape[0]
    edge_count = edge_source.shape[0]
    planes, chips = lax.axis_size("z"), lax.axis_size("y") * lax.axis_size("x")
    tiles = 2 * chips
    half = chips * BLOCK
    wide = width + LANES
    parent = fine_parent.reshape(-1, LANES)
    source = edge_source.reshape(-1, LANES)
    target = edge_target.reshape(-1, LANES)
    halo = halo_rows.reshape(-1, LANES)

    def near(*shape, dtype=BF16):
        return pltpu.VMEM(shape, dtype)

    def far(*shape, dtype=BF16):
        return pltpu.HBM(shape, dtype)

    def here(array):
        return pltpu.with_memory_space_constraint(array, pltpu.VMEM)

    def free(*shape, dtype=BF16):
        return jax.ShapeDtypeStruct(shape, dtype)

    square = near(width, width)
    own, swap, cross = kernel_call(
        sums_body,
        [near(mids, width, dtype=F32), free(mids, width), free(mids, width)],
        [],
        stored=[parent, fine_latent],
        name="child_sums",
    )
    from_cross = crossed(cross, tiles)
    from_swap = swapped(swap)
    w_child, mid_w2, mid_w3, kept, hidden, labels = kernel_call(
        mid_ready_body,
        [square, square, square, near(mids, width), near(mids, width, dtype=F32), near(mids, LANES)],
        [],
        stored=[mid_latent, mid_parent[None], mid_w1, w_child, mid_w2, mid_w3],
        keep=[(3, 0), (4, 1), (5, 2)],
        after=[own],
        flops=1_000_000_000,
        name="mid_ready",
    )
    (labelled,) = kernel_call(
        mid_body,
        [free(mids, wide)],
        [here(own), from_swap, from_cross] + [here(a) for a in (kept, hidden, labels, w_child, mid_w2, mid_w3)],
        name="mid_update",
    )
    other = swapped(labelled)
    pair, blocks = kernel_call(
        blocks_body,
        [far(2 * mids, wide), near(half, width)],
        [labelled, other],
        name="coarse_blocks",
    )

    blocks = blocks.reshape(chips, BLOCK, width)
    parts = lax.all_to_all(blocks, PLANE, 0, 0)
    halo_swap, cross = kernel_call(
        boundary_body,
        [free(LANES, wide), free(2 * mids + LANES, wide)],
        [],
        stored=[parent, halo, fine_latent, pair],
        after=[blocks],
        flops=500_000_000,
        name="boundary",
    )
    cross_in = crossed(cross, tiles)
    halo_in = swapped(halo_swap)
    sender, receiver, node, token = kernel_call(
        tables_body,
        [far(count, width), far(count, width), far(count, width, dtype=F32), free(8, LANES)],
        [],
        stored=[fine_latent, edge_w_src, edge_w_dst, node_w1],
        after=[halo_swap],
        limit=12,
        flops=2_000_000_000,
        name="tables",
    )

    (own_parts,) = kernel_call(
        gather_body,
        [near(planes, BLOCK, width)],
        [parts],
        after=[token, cross_in, halo_in],
        name="plane_sum",
    )
    in_planes = lax.all_to_all(own_parts, "z", 0, 0)
    mid_in = swapped(jnp.where(lax.axis_index("c") == 0, cross_in[mids : 2 * mids], cross_in[:mids]))
    coarse_w3, own_edges, both, last, own_latent, own_hidden = kernel_call(
        own_edges_body,
        [square, far(edge_count, width), square, far(width, width), near(BLOCK, width), near(BLOCK, width, dtype=F32)],
        [],
        stored=[source, target, sender, receiver, coarse_latent, coarse_w1, w_coarse, coarse_w2, edge_w2, node_w2, coarse_w3],
        keep=[(10, 0)],
        streams=[1],
        after=[own_parts],
        limit=20,
        flops=3_500_000_000,
        name="own_edges",
    )

    (results,) = kernel_call(
        coarse_body,
        [near(chips, BLOCK, width)],
        [in_planes] + [here(a) for a in (own_latent, own_hidden, both, coarse_w3)],
        after=[mid_in],
        name="coarse_update",
    )
    mine = lax.all_to_all(results, PLANE, 0, 0).reshape(half, width)
    edges, select, own_pick, token = kernel_call(
        functools.partial(rest_edges_body, mids),
        [far(edge_count, width), far(edge_count, 2 * LANES), far(count, LANES), free(8, LANES)],
        [],
        stored=[source, target, parent, cross_in, halo_in, edge_w_src, own_edges],
        pieces=[6],
        streams=[0, 1],
        after=[results],
        scratch=[pltpu.VMEM((2 * LANES, width), BF16), pltpu.VMEM((2 * count + 2 * LANES, 2 * LANES), BF16)],
        limit=24,
        flops=3_500_000_000,
        name="rest_edges",
    )
    mine, own_pick = lax.optimization_barrier((mine, own_pick))
    theirs = swapped(mine)
    w_descend, w_fine, w_src, w_dst, middle, picked = kernel_call(
        functools.partial(ready_body, 2 * half),
        [square] * 4 + [near(5 * mids, width), near(5 * mids, 2 * half)],
        [],
        stored=[cross_in, pair, mid_in, w_descend, w_fine, edge_w_src, edge_w_dst],
        keep=[(3, 0), (4, 1), (5, 2), (6, 3)],
        after=[mine, token],
        scratch=[pltpu.VMEM((5 * mids, wide), BF16)],
        flops=1_000_000_000,
        name="final_ready",
    )

    fine_out, mid_out, coarse_out = kernel_call(
        final_body,
        [free(count, width), free(mids, width), free(coarse_count, width)],
        [mine, theirs] + [here(a) for a in (w_descend, w_fine, w_src, w_dst, middle, picked)],
        stored=[target, select, edges, own_pick, fine_latent, node_w1, last, node, node_w3],
        pieces=[1, 2],
        scratch=[
            pltpu.VMEM((2 * half, width), BF16),
            pltpu.VMEM((8 * mids, width), BF16),
            pltpu.VMEM((count, width), F32),
        ],
        limit=24,
        name="final",
    )
    return (fine_out, mid_out, coarse_out)


def solution(mesh):
    groups, tiles = mesh.shape["rhombus"], mesh.shape["tile"]
    side = {32: (4, 4), 8: (2, 2)}[tiles]
    physical = jax.sharding.Mesh(mesh.devices.reshape(groups, *side, 2), ("z", "y", "x", "c"))
    every = ("z", "y", "x", "c")
    split, copied = P(every), P()
    return jax.shard_map(
        on_device,
        mesh=physical,
        in_specs=(split, split, copied) + (split,) * 5 + (copied,) * 16,
        out_specs=(split, split, copied),
        check_vma=False,
    )
```

```python
import functools

import jax
import jax.numpy as jnp
from jax import lax
from jax.experimental import pallas as pl
from jax.experimental.pallas import tpu as pltpu
from jax.sharding import PartitionSpec as P

EPSILON = 1e-05
BLOCK = 24
LANES = 128
CHUNK = 512
PIECE = 1536
PLANE = ("y", "x")
TILE = ("y", "x", "c")
F32, BF16, I32 = jnp.float32, jnp.bfloat16, jnp.int32
VMEM = pl.BlockSpec(memory_space=pltpu.VMEM)
STORED = pl.BlockSpec(memory_space=pltpu.HBM)
UNREAD = pl.BlockSpec(memory_space=pl.ANY)


class Copied:
    def __init__(self, source, target, semaphores, first=0, pieces=1):
        rows = target.shape[0] // pieces
        self.target, self.copies = target, []
        for k in range(pieces):
            part = slice(k * rows, (k + 1) * rows) if pieces > 1 else slice(None)
            self.copies.append(pltpu.make_async_copy(source.at[part], target.at[part], semaphores.at[first + k]))
        self.waiting = [False] * pieces

    def start(self, k=None):
        for i in range(len(self.copies)) if k is None else (k,):
            self.copies[i].start()
            self.waiting[i] = True
        return self

    def get(self, k=None):
        for i in range(len(self.copies)) if k is None else (k,):
            if self.waiting[i]:
                self.copies[i].wait()
                self.waiting[i] = False
        return self.target

    def __getitem__(self, index):
        return self.get()[index]

    @property
    def shape(self):
        return self.target.shape


def kernel_call(
    body, outs, operands, stored=(), after=(), scratch=(), keep=(), streams=(), pieces=(), limit=8, flops=0, name=None
):
    count, held, skipped, given = len(operands), len(stored), len(after), len(outs)
    target = dict(keep)
    cuts = [stored[i].shape[0] // PIECE if i in pieces else 1 for i in range(held)]
    flows = {o: outs[o].shape[0] // PIECE for o in streams}

    def kernel(*refs):
        inputs, refs = refs[:count], refs[count:]
        sources, refs = refs[:held], refs[held + skipped :]
        results, refs = refs[:given], refs[given:]
        own, refs = refs[: len(scratch)], refs[len(scratch) :]
        buffers = iter(refs)
        places = [results[target[i]] if i in target else next(buffers) for i in range(held)]
        leaving = {o: next(buffers) for o in streams}
        semaphores = next(buffers) if held or streams else None
        first, copies, fresh = 0, [], []
        for i in range(held):
            copies.append(Copied(sources[i], places[i], semaphores, first, cuts[i]).start())
            first += cuts[i]
        for o in range(given):
            if o in flows:
                fresh.append(Copied(leaving[o], results[o], semaphores, first, flows[o]))
                first += flows[o]
            elif o not in target.values():
                fresh.append(results[o])
        body(*inputs, *copies, *fresh, *[leaving[o] for o in streams], *own)
        for copy in copies + fresh:
            if isinstance(copy, Copied):
                copy.get()

    buffers = [pltpu.VMEM(stored[i].shape, stored[i].dtype) for i in range(held) if i not in target]
    buffers += [pltpu.VMEM(outs[o].shape, outs[o].dtype) for o in streams]
    if held or streams:
        buffers.append(pltpu.SemaphoreType.DMA((sum(cuts) + sum(flows.values()),)))
    return pl.pallas_call(
        kernel,
        out_shape=outs,
        in_specs=[VMEM] * count + [STORED] * held + [UNREAD] * skipped,
        out_specs=[STORED if o in flows else VMEM for o in range(given)],
        scratch_shapes=[*scratch, *buffers],
        compiler_params=pltpu.CompilerParams(vmem_limit_bytes=limit << 20),
        cost_estimate=pl.CostEstimate(flops=flops, bytes_accessed=1 << 20, transcendentals=0),
        name=name,
    )(*operands, *[pltpu.with_memory_space_constraint(array, pltpu.HBM) for array in stored], *after)


def product(left, right):
    return jnp.dot(left, right, preferred_element_type=F32)


def silu(values):
    half = 0.5 * values
    return half + half * jnp.tanh(half)


def updated(latent, hidden, third):
    values = product(hidden.astype(BF16), third)
    scale = lax.rsqrt(jnp.mean(values * values, axis=-1, keepdims=True) + EPSILON)
    return (latent.astype(F32) + values * scale).astype(BF16)


def lanes(height, first=0):
    return lax.broadcasted_iota(I32, (height, LANES), 1) + first


def spread(row):
    return jnp.broadcast_to(row, (LANES, LANES)).T


def hot(mask):
    return jnp.where(mask, 1.0, 0.0).astype(BF16)


def picks(spread_ids, first, blocks):
    return [hot(spread_ids == lanes(LANES, first + LANES * q)) for q in range(blocks)]


def sums_body(parent, fine, own, swap, cross):
    count = own.shape[0]
    core = lax.axis_index("c")
    rows = lax.broadcasted_iota(I32, (3 * count, LANES), 0)
    blocks = [hot(rows == parent[r : r + 1, :]) for r in range(parent.shape[0])]
    sums = product(jnp.concatenate(blocks, axis=1), fine[...])
    own[...] = sums[:count]
    down, up = sums[count : 2 * count].astype(BF16), sums[2 * count :].astype(BF16)
    swap[...] = jnp.where(core == 0, up, down)
    cross[...] = jnp.where(core == 0, down, up)


def mid_ready_body(latent, ids, first, w_child, second, third, kept, hidden, labels):
    count = hidden.shape[0]
    spread_ids = spread(jnp.concatenate([ids[...], jnp.zeros((1, LANES - count), I32)], axis=1))[:count]
    place = lanes(count)
    label = jnp.where(place == 0, spread_ids >> 5, jnp.where(place == 1, spread_ids & 31, 0))
    labels[...] = label.astype(F32).astype(BF16)
    values = latent[...]
    kept[...] = values
    hidden[...] = product(values, first[...])


def mid_body(own, before, after, latent, hidden, labels, w_child, second, third, out):
    width = latent.shape[1]
    total = own[...] + before[...].astype(F32) + after[...].astype(F32)
    incoming = product(total.astype(BF16), w_child[...]).astype(BF16)
    value = silu(hidden[...] + product(incoming, second[...]))
    out[:, :width] = updated(latent[...], value, third[...])
    out[:, width:] = labels[...]


def row_ids(labelled, width):
    label = labelled[:, width:].astype(F32)
    return (label[:, :1] * 32.0 + label[:, 1:2]).astype(I32)


def blocks_body(mine, theirs, pair, out):
    count, width = mine.shape[0], out.shape[1]
    half = out.shape[0]
    core = lax.axis_index("c")
    pair[pl.ds(pl.multiple_of(core * count, count), count), :] = mine[...]
    pair[pl.ds(pl.multiple_of((1 - core) * count, count), count), :] = theirs[...]
    both = pair[...]
    columns = lax.broadcasted_iota(I32, (2 * count, half), 1) + core * half
    picked = hot(row_ids(both, width) == columns)
    out[...] = lax.dot_general(
        picked, both[:, :width], (((0,), (0,)), ((), ())), preferred_element_type=F32
    ).astype(BF16)


def boundary_body(parent, halo, fine, pair, swap, cross):
    count, width = fine.shape
    two, blocks = pair.shape[0], count // LANES
    core = lax.axis_index("c")
    codes = [(spread(parent[r : r + 1, :]) + 1).astype(F32).astype(BF16) for r in range(blocks)]
    codes = jnp.concatenate(codes, axis=0)
    rows = halo[...]
    for out, first, row in (
        (swap, 0, jnp.where(core == 0, rows[1:2], rows[:1])),
        (cross, two, jnp.where(core == 0, rows[:1], rows[1:2])),
    ):
        picked = jnp.concatenate(picks(spread(row), 0, blocks), axis=1)
        out[first : first + LANES, :width] = product(picked, fine[...]).astype(BF16)
        out[first : first + LANES, width:] = product(picked, codes).astype(BF16)
    cross[:two] = pair[...]


def tables_body(fine, w_src, w_dst, w_node, sender, receiver, node, token):
    token[...] = jnp.zeros_like(token)
    values = fine[...]
    sender[...] = product(values, w_src[...]).astype(BF16)
    receiver[...] = product(values, w_dst[...]).astype(BF16)
    node[...] = product(values, w_node[...])


def gather_body(parts, out):
    out[...] = jnp.sum(parts[...].astype(F32), axis=0).astype(BF16)


def coarse_body(mine, theirs, own_latent, own_hidden, both, third, out):
    total = (mine[...].astype(F32) + theirs[...].astype(F32)).astype(BF16)
    hidden = silu(own_hidden[...] + product(total, both[...]))
    result = updated(own_latent[...], hidden, third[...])
    for i in range(out.shape[0]):
        out[i] = result


def coarse_ready_body(
    coarse, coarse_w1, w_coarse, coarse_w2, edge_w2, node_w2, third, both, last, own_latent, own_hidden
):
    rows, total = own_latent.shape[0], coarse.shape[0]
    chips = lax.axis_size("y") * lax.axis_size("x")
    chip = lax.axis_index("y") * lax.axis_size("x") + lax.axis_index("x")
    first = (lax.axis_index("c") * chips + chip) * rows
    place = lax.broadcasted_iota(I32, (rows, total), 0) + first
    picked = hot(place == lax.broadcasted_iota(I32, (rows, total), 1))
    latent = product(picked, coarse[...]).astype(BF16)
    own_latent[...] = latent
    own_hidden[...] = product(latent, coarse_w1[...])
    both[...] = product(w_coarse[...], coarse_w2[...]).astype(BF16)
    last[...] = product(edge_w2[...], node_w2[...]).astype(BF16)


def slots(codes, tile, count):
    parent = codes - 1
    side = parent // count
    away = jnp.where(side == 1, -1, jnp.where(side == 2, 1, 0))
    return jnp.where(codes > 0, (tile + away) * count + (parent & (count - 1)), -1)


def edges_body(
    mid_count, parent, source, target, cross, swap, w_src, sender, receiver, sent_out, sent_select, own_pick, token,
    out, select, table, where
):
    token[...] = jnp.zeros_like(token)
    core = lax.axis_index("c")
    count = own_pick.shape[0]
    width = out.shape[1]
    blocks = count // LANES
    two = cross.shape[0] - LANES
    for r in range(blocks):
        place = slots(spread(parent[r : r + 1, :]) + 1, 2, mid_count)
        rows = slice(r * LANES, (r + 1) * LANES)
        where[rows, :] = jnp.concatenate(picks(place, 0, 2), axis=1)
        near = place - mid_count
        own_pick[rows, :] = hot(near == lanes(LANES))
        far = place + 4 * mid_count
        there = slice(count + 2 * LANES + r * LANES, count + 2 * LANES + (r + 1) * LANES)
        where[there, :] = jnp.concatenate(picks(far, 0, 2), axis=1)
    for values, late in ((cross[two:], core), (swap[...], 1 - core)):
        rows = pl.ds(pl.multiple_of(count + late * LANES, LANES), LANES)
        table[rows, :] = product(values[:, :width], w_src[...]).astype(BF16)
        place = slots(values[:, width:].astype(F32).astype(I32), 1 + 2 * late, mid_count)
        where[rows, :] = jnp.concatenate(picks(place, 0, 2), axis=1)
    table[:count] = sender[...]
    table[count + 2 * LANES :] = receiver[...]
    for k in range(out.shape[0] // CHUNK):
        rows = []
        for r in range(k * CHUNK // LANES, (k + 1) * CHUNK // LANES):
            row = picks(spread(source[r : r + 1, :]), 0, blocks + 2)
            row += picks(spread(target[r : r + 1, :]), 0, blocks)
            rows.append(jnp.concatenate(row, axis=1))
        picked = jnp.concatenate(rows, axis=0)
        here = slice(k * CHUNK, (k + 1) * CHUNK)
        select[here, :] = product(picked, where[...]).astype(BF16)
        out[here, :] = product(picked, table[...]).astype(BF16)
        if (k + 1) * CHUNK % PIECE == 0:
            sent_out.start(k * CHUNK // PIECE)
            sent_select.start(k * CHUNK // PIECE)


def ready_body(rows, cross, pair, swap, w_descend, w_fine, w_src, w_dst, middle, picked, window):
    core = lax.axis_index("c")
    two = pair.shape[0]
    count, width = two // 2, middle.shape[1]
    window[pl.ds(pl.multiple_of((1 - core) * 4 * count, count), count), :] = swap[...]
    window[pl.ds(pl.multiple_of(core * 3 * count, count), two), :] = cross[:two]
    window[pl.ds(pl.multiple_of((2 - core) * count, count), two), :] = pair[...]
    near = window[...]
    middle[...] = near[:, :width]
    picked[...] = hot(row_ids(near, width) == lax.broadcasted_iota(I32, (5 * count, rows), 1))


def final_body(
    mine, theirs, w_descend, w_fine, w_src, w_dst, near, picked, target, select, edges, own_pick, fine,
    w_node, last, node, node_w3, fine_out, mid_out, coarse_out, coarse, table, sums,
):
    core = lax.axis_index("c")
    half, width = mine.shape
    count = near.shape[0] // 5
    coarse[pl.ds(pl.multiple_of(core * half, half), half), :] = mine[...]
    coarse[pl.ds(pl.multiple_of((1 - core) * half, half), half), :] = theirs[...]
    parents = product(picked[...], coarse[...]).astype(BF16)
    down = product(parents, w_descend[...]).astype(BF16)
    middle = (near[...].astype(F32) + down.astype(F32)).astype(BF16)
    mid_out[...] = middle[2 * count : 3 * count]
    fine_down = product(middle, w_fine[...]).astype(BF16)
    closer = fine_down[count : 4 * count]
    table[: 5 * count] = product(fine_down, w_src[...]).astype(BF16)
    table[5 * count :] = product(closer, w_dst[...]).astype(BF16)
    rows = lax.broadcasted_iota(I32, (fine.shape[0], LANES), 0)
    for k in range(edges.shape[0] // CHUNK):
        here = slice(k * CHUNK, (k + 1) * CHUNK)
        piece = k * CHUNK // PIECE
        edge_sum = edges.get(piece)[here, :].astype(F32) + product(select.get(piece)[here, :], table[...])
        hidden = silu(edge_sum).astype(BF16)
        marks = range(k * CHUNK // LANES, (k + 1) * CHUNK // LANES)
        scatter = jnp.concatenate([hot(rows == target[r : r + 1, :]) for r in marks], axis=1)
        part = product(scatter, hidden)
        if k == 0:
            sums[...] = part
        else:
            sums[...] += part
    coarse_out[...] = coarse[: coarse_out.shape[0], :]
    reach = fine_down[count : 5 * count]
    lifted = (fine[...].astype(F32) + product(own_pick[...], reach)).astype(BF16)
    near_node = product(reach, w_node[...]).astype(BF16)
    hidden = silu(node[...] + product(own_pick[...], near_node) + product(sums[...].astype(BF16), last[...]))
    fine_out[...] = updated(lifted, hidden, node_w3[...])


def swapped(values):
    return lax.ppermute(values, "c", [(0, 1), (1, 0)])


def paired(values, step):
    return lax.ppermute(values, "z", [(i, i ^ step) for i in range(lax.axis_size("z"))])


def crossed(values, tiles):
    pairs = [(t, t + 1) for t in range(1, tiles - 1, 2)]
    return lax.ppermute(values, TILE, pairs + [(b, a) for a, b in pairs])


def on_device(
    fine_latent,
    mid_latent,
    coarse_latent,
    fine_parent,
    mid_parent,
    halo_rows,
    edge_source,
    edge_target,
    w_child,
    mid_w1,
    mid_w2,
    mid_w3,
    w_coarse,
    coarse_w1,
    coarse_w2,
    coarse_w3,
    w_descend,
    w_fine,
    edge_w_src,
    edge_w_dst,
    edge_w2,
    node_w1,
    node_w2,
    node_w3,
):
    count, width = fine_latent.shape
    mids = mid_latent.shape[0]
    coarse_count = coarse_latent.shape[0]
    edge_count = edge_source.shape[0]
    planes, chips = lax.axis_size("z"), lax.axis_size("y") * lax.axis_size("x")
    tiles = 2 * chips
    half = chips * BLOCK
    wide = width + LANES
    parent = fine_parent.reshape(-1, LANES)
    source = edge_source.reshape(-1, LANES)
    target = edge_target.reshape(-1, LANES)
    halo = halo_rows.reshape(-1, LANES)

    def near(*shape, dtype=BF16):
        return pltpu.VMEM(shape, dtype)

    def far(*shape, dtype=BF16):
        return pltpu.HBM(shape, dtype)

    def here(array):
        return pltpu.with_memory_space_constraint(array, pltpu.VMEM)

    def free(*shape, dtype=BF16):
        return jax.ShapeDtypeStruct(shape, dtype)

    square = near(width, width)
    own, swap, cross = kernel_call(
        sums_body,
        [near(mids, width, dtype=F32), free(mids, width), free(mids, width)],
        [],
        stored=[parent, fine_latent],
        name="child_sums",
    )
    from_cross = crossed(cross, tiles)
    from_swap = swapped(swap)
    w_child, mid_w2, mid_w3, kept, hidden, labels = kernel_call(
        mid_ready_body,
        [square, square, square, near(mids, width), near(mids, width, dtype=F32), near(mids, LANES)],
        [],
        stored=[mid_latent, mid_parent[None], mid_w1, w_child, mid_w2, mid_w3],
        keep=[(3, 0), (4, 1), (5, 2)],
        after=[own],
        flops=1_000_000_000,
        name="mid_ready",
    )
    (labelled,) = kernel_call(
        mid_body,
        [free(mids, wide)],
        [here(own), from_swap, from_cross] + [here(a) for a in (kept, hidden, labels, w_child, mid_w2, mid_w3)],
        name="mid_update",
    )
    other = swapped(labelled)
    pair, blocks = kernel_call(
        blocks_body,
        [far(2 * mids, wide), near(half, width)],
        [labelled, other],
        name="coarse_blocks",
    )

    blocks = blocks.reshape(chips, BLOCK, width)
    parts = lax.all_to_all(blocks, PLANE, 0, 0)
    halo_swap, cross = kernel_call(
        boundary_body,
        [free(LANES, wide), free(2 * mids + LANES, wide)],
        [],
        stored=[parent, halo, fine_latent, pair],
        after=[blocks],
        flops=500_000_000,
        name="boundary",
    )
    cross_in = crossed(cross, tiles)
    halo_in = swapped(halo_swap)
    sender, receiver, node, token = kernel_call(
        tables_body,
        [far(count, width), far(count, width), far(count, width, dtype=F32), free(8, LANES)],
        [],
        stored=[fine_latent, edge_w_src, edge_w_dst, node_w1],
        after=[halo_swap],
        limit=12,
        flops=2_000_000_000,
        name="tables",
    )

    (total,) = kernel_call(
        gather_body, [free(BLOCK, width)], [parts], after=[token, cross_in, halo_in], name="plane_sum"
    )
    mid_in = swapped(jnp.where(lax.axis_index("c") == 0, cross_in[mids : 2 * mids], cross_in[:mids]))
    step = 1
    while 2 * step < planes:
        total = (total.astype(F32) + paired(total, step).astype(F32)).astype(BF16)
        step *= 2
    other = paired(total, step)
    coarse_w3, both, last, own_latent, own_hidden = kernel_call(
        coarse_ready_body,
        [square, square, far(width, width), near(BLOCK, width), near(BLOCK, width, dtype=F32)],
        [],
        stored=[coarse_latent, coarse_w1, w_coarse, coarse_w2, edge_w2, node_w2, coarse_w3],
        keep=[(6, 0)],
        after=[total],
        flops=1_500_000_000,
        name="coarse_ready",
    )

    (results,) = kernel_call(
        coarse_body,
        [near(chips, BLOCK, width)],
        [total, other] + [here(a) for a in (own_latent, own_hidden, both, coarse_w3)],
        after=[mid_in],
        name="coarse_update",
    )
    mine = lax.all_to_all(results, PLANE, 0, 0).reshape(half, width)
    edges, select, own_pick, token = kernel_call(
        functools.partial(edges_body, mids),
        [far(edge_count, width), far(edge_count, 2 * LANES), far(count, LANES), free(8, LANES)],
        [],
        stored=[parent, source, target, cross_in, halo_in, edge_w_src, sender, receiver],
        streams=[0, 1],
        after=[results],
        scratch=[pltpu.VMEM((2 * count + 2 * LANES, width), BF16), pltpu.VMEM((2 * count + 2 * LANES, 2 * LANES), BF16)],
        limit=24,
        flops=6_500_000_000,
        name="edges",
    )
    mine, own_pick = lax.optimization_barrier((mine, own_pick))
    theirs = swapped(mine)
    w_descend, w_fine, w_src, w_dst, middle, picked = kernel_call(
        functools.partial(ready_body, 2 * half),
        [square] * 4 + [near(5 * mids, width), near(5 * mids, 2 * half)],
        [],
        stored=[cross_in, pair, mid_in, w_descend, w_fine, edge_w_src, edge_w_dst],
        keep=[(3, 0), (4, 1), (5, 2), (6, 3)],
        after=[mine, token],
        scratch=[pltpu.VMEM((5 * mids, wide), BF16)],
        flops=1_000_000_000,
        name="final_ready",
    )

    fine_out, mid_out, coarse_out = kernel_call(
        final_body,
        [free(count, width), free(mids, width), free(coarse_count, width)],
        [mine, theirs] + [here(a) for a in (w_descend, w_fine, w_src, w_dst, middle, picked)],
        stored=[target, select, edges, own_pick, fine_latent, node_w1, last, node, node_w3],
        pieces=[1, 2],
        scratch=[
            pltpu.VMEM((2 * half, width), BF16),
            pltpu.VMEM((8 * mids, width), BF16),
            pltpu.VMEM((count, width), F32),
        ],
        limit=24,
        name="final",
    )
    return (fine_out, mid_out, coarse_out)


def solution(mesh):
    groups, tiles = mesh.shape["rhombus"], mesh.shape["tile"]
    side = {32: (4, 4), 8: (2, 2)}[tiles]
    physical = jax.sharding.Mesh(mesh.devices.reshape(groups, *side, 2), ("z", "y", "x", "c"))
    every = ("z", "y", "x", "c")
    split, copied = P(every), P()
    return jax.shard_map(
        on_device,
        mesh=physical,
        in_specs=(split, split, copied) + (split,) * 5 + (copied,) * 16,
        out_specs=(split, split, copied),
        check_vma=False,
    )
```

```python
import functools

import jax
import jax.numpy as jnp
from jax import lax
from jax.experimental import pallas as pl
from jax.experimental.pallas import tpu as pltpu
from jax.sharding import PartitionSpec as P

EPSILON = 1e-05
BLOCK = 24
LANES = 128
CHUNK = 512
PIECE = 1024
PLANE = ("y", "x")
TILE = ("y", "x", "c")
F32, BF16, I32 = jnp.float32, jnp.bfloat16, jnp.int32
VMEM = pl.BlockSpec(memory_space=pltpu.VMEM)
STORED = pl.BlockSpec(memory_space=pltpu.HBM)
UNREAD = pl.BlockSpec(memory_space=pl.ANY)


class Copied:
    def __init__(self, source, target, semaphores, first=0, pieces=1):
        rows = target.shape[0] // pieces
        self.target, self.copies = target, []
        for k in range(pieces):
            part = slice(k * rows, (k + 1) * rows) if pieces > 1 else slice(None)
            self.copies.append(pltpu.make_async_copy(source.at[part], target.at[part], semaphores.at[first + k]))
        self.waiting = [False] * pieces

    def start(self, k=None):
        for i in range(len(self.copies)) if k is None else (k,):
            self.copies[i].start()
            self.waiting[i] = True
        return self

    def get(self, k=None):
        for i in range(len(self.copies)) if k is None else (k,):
            if self.waiting[i]:
                self.copies[i].wait()
                self.waiting[i] = False
        return self.target

    def __getitem__(self, index):
        return self.get()[index]

    @property
    def shape(self):
        return self.target.shape


def kernel_call(
    body, outs, operands, stored=(), after=(), scratch=(), keep=(), streams=(), pieces=(), limit=8, flops=0, name=None
):
    count, held, skipped, given = len(operands), len(stored), len(after), len(outs)
    target = dict(keep)
    cuts = [stored[i].shape[0] // PIECE if i in pieces else 1 for i in range(held)]
    flows = {o: outs[o].shape[0] // PIECE for o in streams}

    def kernel(*refs):
        inputs, refs = refs[:count], refs[count:]
        sources, refs = refs[:held], refs[held + skipped :]
        results, refs = refs[:given], refs[given:]
        own, refs = refs[: len(scratch)], refs[len(scratch) :]
        buffers = iter(refs)
        places = [results[target[i]] if i in target else next(buffers) for i in range(held)]
        leaving = {o: next(buffers) for o in streams}
        semaphores = next(buffers) if held or streams else None
        first, copies, fresh = 0, [], []
        for i in range(held):
            copies.append(Copied(sources[i], places[i], semaphores, first, cuts[i]).start())
            first += cuts[i]
        for o in range(given):
            if o in flows:
                fresh.append(Copied(leaving[o], results[o], semaphores, first, flows[o]))
                first += flows[o]
            elif o not in target.values():
                fresh.append(results[o])
        body(*inputs, *copies, *fresh, *[leaving[o] for o in streams], *own)
        for copy in copies + fresh:
            if isinstance(copy, Copied):
                copy.get()

    buffers = [pltpu.VMEM(stored[i].shape, stored[i].dtype) for i in range(held) if i not in target]
    buffers += [pltpu.VMEM(outs[o].shape, outs[o].dtype) for o in streams]
    if held or streams:
        buffers.append(pltpu.SemaphoreType.DMA((sum(cuts) + sum(flows.values()),)))
    return pl.pallas_call(
        kernel,
        out_shape=outs,
        in_specs=[VMEM] * count + [STORED] * held + [UNREAD] * skipped,
        out_specs=[STORED if o in flows else VMEM for o in range(given)],
        scratch_shapes=[*scratch, *buffers],
        compiler_params=pltpu.CompilerParams(vmem_limit_bytes=limit << 20),
        cost_estimate=pl.CostEstimate(flops=flops, bytes_accessed=1 << 20, transcendentals=0),
        name=name,
    )(*operands, *[pltpu.with_memory_space_constraint(array, pltpu.HBM) for array in stored], *after)


def product(left, right):
    return jnp.dot(left, right, preferred_element_type=F32)


def silu(values):
    half = 0.5 * values
    return half + half * jnp.tanh(half)


def updated(latent, hidden, third):
    values = product(hidden.astype(BF16), third)
    scale = lax.rsqrt(jnp.mean(values * values, axis=-1, keepdims=True) + EPSILON)
    return (latent.astype(F32) + values * scale).astype(BF16)


def lanes(height, first=0):
    return lax.broadcasted_iota(I32, (height, LANES), 1) + first


def spread(row):
    return jnp.broadcast_to(row, (LANES, LANES)).T


def hot(mask):
    return jnp.where(mask, 1.0, 0.0).astype(BF16)


def picks(spread_ids, first, blocks):
    return [hot(spread_ids == lanes(LANES, first + LANES * q)) for q in range(blocks)]


def sums_body(parent, fine, own, swap, cross):
    count = own.shape[0]
    core = lax.axis_index("c")
    rows = lax.broadcasted_iota(I32, (3 * count, LANES), 0)
    blocks = [hot(rows == parent[r : r + 1, :]) for r in range(parent.shape[0])]
    sums = product(jnp.concatenate(blocks, axis=1), fine[...])
    own[...] = sums[:count]
    down, up = sums[count : 2 * count].astype(BF16), sums[2 * count :].astype(BF16)
    swap[...] = jnp.where(core == 0, up, down)
    cross[...] = jnp.where(core == 0, down, up)


def mid_ready_body(latent, ids, first, w_child, second, third, kept, hidden, labels):
    count = hidden.shape[0]
    spread_ids = spread(jnp.concatenate([ids[...], jnp.zeros((1, LANES - count), I32)], axis=1))[:count]
    place = lanes(count)
    label = jnp.where(place == 0, spread_ids >> 5, jnp.where(place == 1, spread_ids & 31, 0))
    labels[...] = label.astype(F32).astype(BF16)
    values = latent[...]
    kept[...] = values
    hidden[...] = product(values, first[...])


def mid_body(own, before, after, latent, hidden, labels, w_child, second, third, out):
    width = latent.shape[1]
    total = own[...] + before[...].astype(F32) + after[...].astype(F32)
    incoming = product(total.astype(BF16), w_child[...]).astype(BF16)
    value = silu(hidden[...] + product(incoming, second[...]))
    out[:, :width] = updated(latent[...], value, third[...])
    out[:, width:] = labels[...]


def row_ids(labelled, width):
    label = labelled[:, width:].astype(F32)
    return (label[:, :1] * 32.0 + label[:, 1:2]).astype(I32)


def blocks_body(mine, theirs, pair, out):
    count, width = mine.shape[0], out.shape[1]
    half = out.shape[0]
    core = lax.axis_index("c")
    pair[pl.ds(pl.multiple_of(core * count, count), count), :] = mine[...]
    pair[pl.ds(pl.multiple_of((1 - core) * count, count), count), :] = theirs[...]
    both = pair[...]
    columns = lax.broadcasted_iota(I32, (2 * count, half), 1) + core * half
    picked = hot(row_ids(both, width) == columns)
    out[...] = lax.dot_general(
        picked, both[:, :width], (((0,), (0,)), ((), ())), preferred_element_type=F32
    ).astype(BF16)


def own_edges_body(
    parent, halo, source, target, fine, w_src, w_dst, pair, sent_out, swap, cross, token, out
):
    token[...] = jnp.zeros_like(token)
    count, width = fine.shape
    two, blocks = pair.shape[0], count // LANES
    core = lax.axis_index("c")
    codes = [(spread(parent[r : r + 1, :]) + 1).astype(F32).astype(BF16) for r in range(blocks)]
    codes = jnp.concatenate(codes, axis=0)
    rows = halo[...]
    values = fine[...]
    sent = product(values, w_src[...]).astype(BF16)
    received = product(values, w_dst[...]).astype(BF16)
    for k in range(out.shape[0] // CHUNK):
        marks = range(k * CHUNK // LANES, (k + 1) * CHUNK // LANES)
        picked = [jnp.concatenate(picks(spread(source[r : r + 1, :]), 0, blocks), axis=1) for r in marks]
        total = product(jnp.concatenate(picked, axis=0), sent)
        picked = [jnp.concatenate(picks(spread(target[r : r + 1, :]), 0, blocks), axis=1) for r in marks]
        total += product(jnp.concatenate(picked, axis=0), received)
        out[k * CHUNK : (k + 1) * CHUNK, :] = total.astype(BF16)
        if (k + 1) * CHUNK % PIECE == 0:
            sent_out.start(k * CHUNK // PIECE)
    for place, first, row in (
        (swap, 0, jnp.where(core == 0, rows[1:2], rows[:1])),
        (cross, two, jnp.where(core == 0, rows[:1], rows[1:2])),
    ):
        picked = jnp.concatenate(picks(spread(row), 0, blocks), axis=1)
        place[first : first + LANES, :width] = product(picked, values).astype(BF16)
        place[first : first + LANES, width:] = product(picked, codes).astype(BF16)
    cross[:two] = pair[...]


def gather_body(parts, out):
    total = jnp.sum(parts[...].astype(F32), axis=0).astype(BF16)
    for i in range(out.shape[0]):
        out[i] = total


def coarse_body(parts, own_latent, own_hidden, both, third, out):
    total = jnp.sum(parts[...].astype(F32), axis=0).astype(BF16)
    hidden = silu(own_hidden[...] + product(total, both[...]))
    result = updated(own_latent[...], hidden, third[...])
    for i in range(out.shape[0]):
        out[i] = result


def coarse_rows_body(coarse, coarse_w1, own_latent, own_hidden):
    rows, total = own_latent.shape[0], coarse.shape[0]
    chips = lax.axis_size("y") * lax.axis_size("x")
    chip = lax.axis_index("y") * lax.axis_size("x") + lax.axis_index("x")
    first = (lax.axis_index("c") * chips + chip) * rows
    place = lax.broadcasted_iota(I32, (rows, total), 0) + first
    picked = hot(place == lax.broadcasted_iota(I32, (rows, total), 1))
    latent = product(picked, coarse[...]).astype(BF16)
    own_latent[...] = latent
    own_hidden[...] = product(latent, coarse_w1[...])


def weights_body(w_coarse, coarse_w2, edge_w2, node_w2, third, rows, hidden, both, last, own_latent, own_hidden):
    own_latent[...] = rows[...]
    own_hidden[...] = hidden[...]
    both[...] = product(w_coarse[...], coarse_w2[...]).astype(BF16)
    last[...] = product(edge_w2[...], node_w2[...]).astype(BF16)


def slots(codes, tile, count):
    parent = codes - 1
    side = parent // count
    away = jnp.where(side == 1, -1, jnp.where(side == 2, 1, 0))
    return jnp.where(codes > 0, (tile + away) * count + (parent & (count - 1)), -1)


def rest_edges_body(
    mid_count, parent, source, target, cross, swap, w_src, pair, mid_swap, first, w_descend, w_fine,
    sent_out, sent_select, own_pick, middle, picked, out, select, table, where, window
):
    core = lax.axis_index("c")
    count = own_pick.shape[0]
    width = out.shape[1]
    blocks = count // LANES
    two = pair.shape[0]
    for r in range(blocks):
        place = slots(spread(parent[r : r + 1, :]) + 1, 2, mid_count)
        rows = slice(r * LANES, (r + 1) * LANES)
        where[rows, :] = jnp.concatenate(picks(place, 0, 2), axis=1)
        near = place - mid_count
        own_pick[rows, :] = hot(near == lanes(LANES))
        far = place + 4 * mid_count
        there = slice(count + 2 * LANES + r * LANES, count + 2 * LANES + (r + 1) * LANES)
        where[there, :] = jnp.concatenate(picks(far, 0, 2), axis=1)
    for values, late in ((cross[two:], core), (swap[...], 1 - core)):
        rows = pl.ds(pl.multiple_of(late * LANES, LANES), LANES)
        table[rows, :] = product(values[:, :width], w_src[...]).astype(BF16)
        place = slots(values[:, width:].astype(F32).astype(I32), 1 + 2 * late, mid_count)
        rows = pl.ds(pl.multiple_of(count + late * LANES, LANES), LANES)
        where[rows, :] = jnp.concatenate(picks(place, 0, 2), axis=1)
    window[pl.ds(pl.multiple_of((1 - core) * 4 * mid_count, mid_count), mid_count), :] = mid_swap[...]
    window[pl.ds(pl.multiple_of(core * 3 * mid_count, mid_count), two), :] = cross[:two]
    window[pl.ds(pl.multiple_of((2 - core) * mid_count, mid_count), two), :] = pair[...]
    near = window[...]
    middle[...] = near[:, :width]
    picked[...] = hot(row_ids(near, width) == lax.broadcasted_iota(I32, picked.shape, 1))
    for k in range(out.shape[0] // CHUNK):
        rows = []
        for r in range(k * CHUNK // LANES, (k + 1) * CHUNK // LANES):
            row = picks(spread(source[r : r + 1, :]), 0, blocks + 2)
            row += picks(spread(target[r : r + 1, :]), 0, blocks)
            rows.append(jnp.concatenate(row, axis=1))
        marks = jnp.concatenate(rows, axis=0)
        here = slice(k * CHUNK, (k + 1) * CHUNK)
        select[here, :] = product(marks, where[...]).astype(BF16)
        rest = product(marks[:, count : count + 2 * LANES], table[...])
        out[here, :] = (first.get(k * CHUNK // PIECE)[here, :].astype(F32) + rest).astype(BF16)
        if (k + 1) * CHUNK % PIECE == 0:
            sent_out.start(k * CHUNK // PIECE)
            sent_select.start(k * CHUNK // PIECE)


def final_body(
    mine, theirs, w_descend, w_fine, near, picked, w_src, w_dst, target, select, edges, own_pick, fine,
    w_node, last, node_w3, fine_out, mid_out, coarse_out, coarse, table, sums,
):
    core = lax.axis_index("c")
    half, width = mine.shape
    count = near.shape[0] // 5
    coarse[pl.ds(pl.multiple_of(core * half, half), half), :] = mine[...]
    coarse[pl.ds(pl.multiple_of((1 - core) * half, half), half), :] = theirs[...]
    parents = product(picked[...], coarse[...]).astype(BF16)
    down = product(parents, w_descend[...]).astype(BF16)
    middle = (near[...].astype(F32) + down.astype(F32)).astype(BF16)
    mid_out[...] = middle[2 * count : 3 * count]
    fine_down = product(middle, w_fine[...]).astype(BF16)
    closer = fine_down[count : 4 * count]
    table[: 5 * count] = product(fine_down, w_src[...]).astype(BF16)
    table[5 * count :] = product(closer, w_dst[...]).astype(BF16)
    rows = lax.broadcasted_iota(I32, (fine.shape[0], LANES), 0)
    for k in range(edges.shape[0] // CHUNK):
        here = slice(k * CHUNK, (k + 1) * CHUNK)
        piece = k * CHUNK // PIECE
        edge_sum = edges.get(piece)[here, :].astype(F32) + product(select.get(piece)[here, :], table[...])
        hidden = silu(edge_sum).astype(BF16)
        marks = range(k * CHUNK // LANES, (k + 1) * CHUNK // LANES)
        scatter = jnp.concatenate([hot(rows == target[r : r + 1, :]) for r in marks], axis=1)
        part = product(scatter, hidden)
        if k == 0:
            sums[...] = part
        else:
            sums[...] += part
    coarse_out[...] = coarse[: coarse_out.shape[0], :]
    reach = fine_down[count : 5 * count]
    lifted = (fine[...].astype(F32) + product(own_pick[...], reach)).astype(BF16)
    hidden = silu(product(lifted, w_node[...]) + product(sums[...].astype(BF16), last[...]))
    fine_out[...] = updated(lifted, hidden, node_w3[...])


def swapped(values):
    return lax.ppermute(values, "c", [(0, 1), (1, 0)])


def crossed(values, tiles):
    pairs = [(t, t + 1) for t in range(1, tiles - 1, 2)]
    return lax.ppermute(values, TILE, pairs + [(b, a) for a, b in pairs])


def on_device(
    fine_latent,
    mid_latent,
    coarse_latent,
    fine_parent,
    mid_parent,
    halo_rows,
    edge_source,
    edge_target,
    w_child,
    mid_w1,
    mid_w2,
    mid_w3,
    w_coarse,
    coarse_w1,
    coarse_w2,
    coarse_w3,
    w_descend,
    w_fine,
    edge_w_src,
    edge_w_dst,
    edge_w2,
    node_w1,
    node_w2,
    node_w3,
):
    count, width = fine_latent.shape
    mids = mid_latent.shape[0]
    coarse_count = coarse_latent.shape[0]
    edge_count = edge_source.shape[0]
    planes, chips = lax.axis_size("z"), lax.axis_size("y") * lax.axis_size("x")
    tiles = 2 * chips
    half = chips * BLOCK
    wide = width + LANES
    parent = fine_parent.reshape(-1, LANES)
    source = edge_source.reshape(-1, LANES)
    target = edge_target.reshape(-1, LANES)
    halo = halo_rows.reshape(-1, LANES)

    def near(*shape, dtype=BF16):
        return pltpu.VMEM(shape, dtype)

    def far(*shape, dtype=BF16):
        return pltpu.HBM(shape, dtype)

    def here(array):
        return pltpu.with_memory_space_constraint(array, pltpu.VMEM)

    def free(*shape, dtype=BF16):
        return jax.ShapeDtypeStruct(shape, dtype)

    square = near(width, width)
    own, swap, cross = kernel_call(
        sums_body,
        [near(mids, width, dtype=F32), free(mids, width), free(mids, width)],
        [],
        stored=[parent, fine_latent],
        name="child_sums",
    )
    from_cross = crossed(cross, tiles)
    from_swap = swapped(swap)
    w_child, mid_w2, mid_w3, kept, hidden, labels = kernel_call(
        mid_ready_body,
        [square, square, square, near(mids, width), near(mids, width, dtype=F32), near(mids, LANES)],
        [],
        stored=[mid_latent, mid_parent[None], mid_w1, w_child, mid_w2, mid_w3],
        keep=[(3, 0), (4, 1), (5, 2)],
        after=[own],
        flops=1_000_000_000,
        name="mid_ready",
    )
    (labelled,) = kernel_call(
        mid_body,
        [free(mids, wide)],
        [here(own), from_swap, from_cross] + [here(a) for a in (kept, hidden, labels, w_child, mid_w2, mid_w3)],
        name="mid_update",
    )
    other = swapped(labelled)
    pair, blocks = kernel_call(
        blocks_body,
        [far(2 * mids, wide), near(half, width)],
        [labelled, other],
        name="coarse_blocks",
    )

    blocks = blocks.reshape(chips, BLOCK, width)
    parts = lax.all_to_all(blocks, PLANE, 0, 0)
    own_edges, halo_swap, cross, token = kernel_call(
        own_edges_body,
        [far(edge_count, width), far(LANES, wide), far(2 * mids + LANES, wide), free(8, LANES)],
        [],
        stored=[parent, halo, source, target, fine_latent, edge_w_src, edge_w_dst, pair],
        streams=[0],
        after=[blocks],
        limit=24,
        flops=4_000_000_000,
        name="own_edges",
    )

    (own_parts,) = kernel_call(
        gather_body, [near(planes, BLOCK, width)], [parts], after=[token], name="plane_sum"
    )
    in_planes = lax.all_to_all(own_parts, "z", 0, 0)
    rows, hidden = kernel_call(
        coarse_rows_body,
        [far(BLOCK, width), far(BLOCK, width, dtype=F32)],
        [],
        stored=[coarse_latent, coarse_w1],
        after=[own_parts],

        name="coarse_rows",
    )
    halo_swap, cross, rows = lax.optimization_barrier((halo_swap, cross, rows))
    cross_in = crossed(cross, tiles)
    halo_in = swapped(halo_swap)
    coarse_w3, both, last, own_latent, own_hidden = kernel_call(
        weights_body,
        [square, square, far(width, width), near(BLOCK, width), near(BLOCK, width, dtype=F32)],
        [],
        stored=[w_coarse, coarse_w2, edge_w2, node_w2, coarse_w3, rows, hidden],
        keep=[(4, 0)],
        flops=3_000_000_000,
        name="weights",
    )
    nearest, own_latent = lax.optimization_barrier((cross_in, own_latent))
    mid_in = swapped(jnp.where(lax.axis_index("c") == 0, nearest[mids : 2 * mids], nearest[:mids]))

    (results,) = kernel_call(
        coarse_body,
        [near(chips, BLOCK, width)],
        [in_planes] + [here(a) for a in (own_latent, own_hidden, both, coarse_w3)],
        after=[cross_in, halo_in],
        name="coarse_update",
    )
    mine = lax.all_to_all(results, PLANE, 0, 0).reshape(half, width)
    w_descend, w_fine, edges, select, own_pick, middle, picked = kernel_call(
        functools.partial(rest_edges_body, mids),
        [square, square, far(edge_count, width), far(edge_count, 2 * LANES), far(count, LANES)]
        + [near(5 * mids, width), near(5 * mids, 2 * half)],
        [],
        stored=[parent, source, target, cross_in, halo_in, edge_w_src, pair, mid_in, own_edges, w_descend, w_fine],
        keep=[(9, 0), (10, 1)],
        pieces=[8],
        streams=[2, 3],
        after=[results],
        scratch=[
            pltpu.VMEM((2 * LANES, width), BF16),
            pltpu.VMEM((2 * count + 2 * LANES, 2 * LANES), BF16),
            pltpu.VMEM((5 * mids, wide), BF16),
        ],
        limit=24,
        flops=4_000_000_000,
        name="rest_edges",
    )
    mine, own_pick = lax.optimization_barrier((mine, own_pick))
    theirs = swapped(mine)

    fine_out, mid_out, coarse_out = kernel_call(
        final_body,
        [free(count, width), free(mids, width), free(coarse_count, width)],
        [mine, theirs] + [here(a) for a in (w_descend, w_fine, middle, picked)],
        stored=[edge_w_src, edge_w_dst, target, select, edges, own_pick, fine_latent, node_w1, last, node_w3],
        pieces=[3, 4],
        scratch=[
            pltpu.VMEM((2 * half, width), BF16),
            pltpu.VMEM((8 * mids, width), BF16),
            pltpu.VMEM((count, width), F32),
        ],
        limit=24,
        name="final",
    )
    return (fine_out, mid_out, coarse_out)


def solution(mesh):
    groups, tiles = mesh.shape["rhombus"], mesh.shape["tile"]
    side = {32: (4, 4), 8: (2, 2)}[tiles]
    physical = jax.sharding.Mesh(mesh.devices.reshape(groups, *side, 2), ("z", "y", "x", "c"))
    every = ("z", "y", "x", "c")
    split, copied = P(every), P()
    return jax.shard_map(
        on_device,
        mesh=physical,
        in_specs=(split, split, copied) + (split,) * 5 + (copied,) * 16,
        out_specs=(split, split, copied),
        check_vma=False,
    )
```

```python
import functools

import jax
import jax.numpy as jnp
from jax import lax
from jax.experimental import pallas as pl
from jax.experimental.pallas import tpu as pltpu
from jax.sharding import PartitionSpec as P

EPSILON = 1e-05
BLOCK = 24
LANES = 128
CHUNK = 512
PIECE = 1024
PLANE = ("y", "x")
TILE = ("y", "x", "c")
F32, BF16, I32 = jnp.float32, jnp.bfloat16, jnp.int32
VMEM = pl.BlockSpec(memory_space=pltpu.VMEM)
STORED = pl.BlockSpec(memory_space=pltpu.HBM)
UNREAD = pl.BlockSpec(memory_space=pl.ANY)


class Copied:
    def __init__(self, source, target, semaphores, first=0, pieces=1):
        rows = target.shape[0] // pieces
        self.target, self.copies = target, []
        for k in range(pieces):
            part = slice(k * rows, (k + 1) * rows) if pieces > 1 else slice(None)
            self.copies.append(pltpu.make_async_copy(source.at[part], target.at[part], semaphores.at[first + k]))
        self.waiting = [False] * pieces

    def start(self, k=None):
        for i in range(len(self.copies)) if k is None else (k,):
            self.copies[i].start()
            self.waiting[i] = True
        return self

    def get(self, k=None):
        for i in range(len(self.copies)) if k is None else (k,):
            if self.waiting[i]:
                self.copies[i].wait()
                self.waiting[i] = False
        return self.target

    def __getitem__(self, index):
        return self.get()[index]

    @property
    def shape(self):
        return self.target.shape


def kernel_call(
    body, outs, operands, stored=(), after=(), scratch=(), keep=(), streams=(), pieces=(), limit=8, flops=0, name=None
):
    count, held, skipped, given = len(operands), len(stored), len(after), len(outs)
    target = dict(keep)
    cuts = [stored[i].shape[0] // PIECE if i in pieces else 1 for i in range(held)]
    flows = {o: outs[o].shape[0] // PIECE for o in streams}

    def kernel(*refs):
        inputs, refs = refs[:count], refs[count:]
        sources, refs = refs[:held], refs[held + skipped :]
        results, refs = refs[:given], refs[given:]
        own, refs = refs[: len(scratch)], refs[len(scratch) :]
        buffers = iter(refs)
        places = [results[target[i]] if i in target else next(buffers) for i in range(held)]
        leaving = {o: next(buffers) for o in streams}
        semaphores = next(buffers) if held or streams else None
        first, copies, fresh = 0, [], []
        for i in range(held):
            copies.append(Copied(sources[i], places[i], semaphores, first, cuts[i]).start())
            first += cuts[i]
        for o in range(given):
            if o in flows:
                fresh.append(Copied(leaving[o], results[o], semaphores, first, flows[o]))
                first += flows[o]
            elif o not in target.values():
                fresh.append(results[o])
        body(*inputs, *copies, *fresh, *[leaving[o] for o in streams], *own)
        for copy in copies + fresh:
            if isinstance(copy, Copied):
                copy.get()

    buffers = [pltpu.VMEM(stored[i].shape, stored[i].dtype) for i in range(held) if i not in target]
    buffers += [pltpu.VMEM(outs[o].shape, outs[o].dtype) for o in streams]
    if held or streams:
        buffers.append(pltpu.SemaphoreType.DMA((sum(cuts) + sum(flows.values()),)))
    return pl.pallas_call(
        kernel,
        out_shape=outs,
        in_specs=[VMEM] * count + [STORED] * held + [UNREAD] * skipped,
        out_specs=[STORED if o in flows else VMEM for o in range(given)],
        scratch_shapes=[*scratch, *buffers],
        compiler_params=pltpu.CompilerParams(vmem_limit_bytes=limit << 20),
        cost_estimate=pl.CostEstimate(flops=flops, bytes_accessed=1 << 20, transcendentals=0),
        name=name,
    )(*operands, *[pltpu.with_memory_space_constraint(array, pltpu.HBM) for array in stored], *after)


def product(left, right):
    return jnp.dot(left, right, preferred_element_type=F32)


def silu(values):
    half = 0.5 * values
    return half + half * jnp.tanh(half)


def updated(latent, hidden, third):
    values = product(hidden.astype(BF16), third)
    scale = lax.rsqrt(jnp.mean(values * values, axis=-1, keepdims=True) + EPSILON)
    return (latent.astype(F32) + values * scale).astype(BF16)


def lanes(height, first=0):
    return lax.broadcasted_iota(I32, (height, LANES), 1) + first


def spread(row):
    return jnp.broadcast_to(row, (LANES, LANES)).T


def hot(mask):
    return jnp.where(mask, 1.0, 0.0).astype(BF16)


def picks(spread_ids, first, blocks):
    return [hot(spread_ids == lanes(LANES, first + LANES * q)) for q in range(blocks)]


def sums_body(parent, fine, own, swap, cross):
    count = own.shape[0]
    core = lax.axis_index("c")
    rows = lax.broadcasted_iota(I32, (3 * count, LANES), 0)
    blocks = [hot(rows == parent[r : r + 1, :]) for r in range(parent.shape[0])]
    sums = product(jnp.concatenate(blocks, axis=1), fine[...])
    own[...] = sums[:count]
    down, up = sums[count : 2 * count].astype(BF16), sums[2 * count :].astype(BF16)
    swap[...] = jnp.where(core == 0, up, down)
    cross[...] = jnp.where(core == 0, down, up)


def mid_ready_body(latent, ids, first, w_child, second, third, kept, hidden, labels):
    count = hidden.shape[0]
    spread_ids = spread(jnp.concatenate([ids[...], jnp.zeros((1, LANES - count), I32)], axis=1))[:count]
    place = lanes(count)
    label = jnp.where(place == 0, spread_ids >> 5, jnp.where(place == 1, spread_ids & 31, 0))
    labels[...] = label.astype(F32).astype(BF16)
    values = latent[...]
    kept[...] = values
    hidden[...] = product(values, first[...])


def mid_body(own, before, after, latent, hidden, labels, w_child, second, third, out):
    width = latent.shape[1]
    total = own[...] + before[...].astype(F32) + after[...].astype(F32)
    incoming = product(total.astype(BF16), w_child[...]).astype(BF16)
    value = silu(hidden[...] + product(incoming, second[...]))
    out[:, :width] = updated(latent[...], value, third[...])
    out[:, width:] = labels[...]


def row_ids(labelled, width):
    label = labelled[:, width:].astype(F32)
    return (label[:, :1] * 32.0 + label[:, 1:2]).astype(I32)


def blocks_body(mine, theirs, pair, out):
    count, width = mine.shape[0], out.shape[1]
    half = out.shape[0]
    core = lax.axis_index("c")
    pair[pl.ds(pl.multiple_of(core * count, count), count), :] = mine[...]
    pair[pl.ds(pl.multiple_of((1 - core) * count, count), count), :] = theirs[...]
    both = pair[...]
    columns = lax.broadcasted_iota(I32, (2 * count, half), 1) + core * half
    picked = hot(row_ids(both, width) == columns)
    out[...] = lax.dot_general(
        picked, both[:, :width], (((0,), (0,)), ((), ())), preferred_element_type=F32
    ).astype(BF16)


def own_edges_body(
    parent, halo, source, target, fine, w_src, w_dst, pair, sent_out, swap, cross, token, out
):
    token[...] = jnp.zeros_like(token)
    count, width = fine.shape
    two, blocks = pair.shape[0], count // LANES
    core = lax.axis_index("c")
    codes = [(spread(parent[r : r + 1, :]) + 1).astype(F32).astype(BF16) for r in range(blocks)]
    codes = jnp.concatenate(codes, axis=0)
    rows = halo[...]
    values = fine[...]
    sent = product(values, w_src[...]).astype(BF16)
    received = product(values, w_dst[...]).astype(BF16)

    def marks_of(k):
        both = []
        for ids in (source, target):
            rows = range(k * CHUNK // LANES, (k + 1) * CHUNK // LANES)
            rows = [jnp.concatenate(picks(spread(ids[r : r + 1, :]), 0, blocks), axis=1) for r in rows]
            both.append(jnp.concatenate(rows, axis=0))
        return both

    chunks = out.shape[0] // CHUNK
    following = marks_of(0)
    for k in range(chunks):
        sources, targets = following
        if k + 1 < chunks:
            following = marks_of(k + 1)
        total = product(sources, sent) + product(targets, received)
        out[k * CHUNK : (k + 1) * CHUNK, :] = total.astype(BF16)
        if (k + 1) * CHUNK % PIECE == 0:
            sent_out.start(k * CHUNK // PIECE)
    for place, first, row in (
        (swap, 0, jnp.where(core == 0, rows[1:2], rows[:1])),
        (cross, two, jnp.where(core == 0, rows[:1], rows[1:2])),
    ):
        picked = jnp.concatenate(picks(spread(row), 0, blocks), axis=1)
        place[first : first + LANES, :width] = product(picked, values).astype(BF16)
        place[first : first + LANES, width:] = product(picked, codes).astype(BF16)
    cross[:two] = pair[...]


def gather_body(parts, out):
    total = jnp.sum(parts[...].astype(F32), axis=0).astype(BF16)
    for i in range(out.shape[0]):
        out[i] = total


def coarse_body(parts, own_latent, own_hidden, w_coarse, second, third, out):
    total = jnp.sum(parts[...].astype(F32), axis=0).astype(BF16)
    incoming = product(total, w_coarse[...]).astype(BF16)
    hidden = silu(own_hidden[...] + product(incoming, second[...]))
    result = updated(own_latent[...], hidden, third[...])
    for i in range(out.shape[0]):
        out[i] = result


def coarse_ready_body(coarse, coarse_w1, w_coarse, second, third, own_latent, own_hidden):
    rows, total = own_latent.shape[0], coarse.shape[0]
    chips = lax.axis_size("y") * lax.axis_size("x")
    chip = lax.axis_index("y") * lax.axis_size("x") + lax.axis_index("x")
    first = (lax.axis_index("c") * chips + chip) * rows
    place = lax.broadcasted_iota(I32, (rows, total), 0) + first
    picked = hot(place == lax.broadcasted_iota(I32, (rows, total), 1))
    latent = product(picked, coarse[...]).astype(BF16)
    own_latent[...] = latent
    own_hidden[...] = product(latent, coarse_w1[...])


def slots(codes, tile, count):
    parent = codes - 1
    side = parent // count
    away = jnp.where(side == 1, -1, jnp.where(side == 2, 1, 0))
    return jnp.where(codes > 0, (tile + away) * count + (parent & (count - 1)), -1)


def rest_edges_body(
    mid_count, mid_swap, parent, source, target, cross, swap, w_src, pair, first, w_descend, w_fine, w_dst,
    sent_out, sent_select, own_pick, middle, picked, out, select, table, where, window
):
    core = lax.axis_index("c")
    count = own_pick.shape[0]
    width = out.shape[1]
    blocks = count // LANES
    two = pair.shape[0]
    for r in range(blocks):
        place = slots(spread(parent[r : r + 1, :]) + 1, 2, mid_count)
        rows = slice(r * LANES, (r + 1) * LANES)
        where[rows, :] = jnp.concatenate(picks(place, 0, 2), axis=1)
        near = place - mid_count
        own_pick[rows, :] = hot(near == lanes(LANES))
        far = place + 4 * mid_count
        there = slice(count + 2 * LANES + r * LANES, count + 2 * LANES + (r + 1) * LANES)
        where[there, :] = jnp.concatenate(picks(far, 0, 2), axis=1)
    for values, late in ((cross[two:], core), (swap[...], 1 - core)):
        rows = pl.ds(pl.multiple_of(late * LANES, LANES), LANES)
        table[rows, :] = product(values[:, :width], w_src[...]).astype(BF16)
        place = slots(values[:, width:].astype(F32).astype(I32), 1 + 2 * late, mid_count)
        rows = pl.ds(pl.multiple_of(count + late * LANES, LANES), LANES)
        where[rows, :] = jnp.concatenate(picks(place, 0, 2), axis=1)
    window[pl.ds(pl.multiple_of((1 - core) * 4 * mid_count, mid_count), mid_count), :] = mid_swap[...]
    window[pl.ds(pl.multiple_of(core * 3 * mid_count, mid_count), two), :] = cross[:two]
    window[pl.ds(pl.multiple_of((2 - core) * mid_count, mid_count), two), :] = pair[...]
    near = window[...]
    middle[...] = near[:, :width]
    picked[...] = hot(row_ids(near, width) == lax.broadcasted_iota(I32, picked.shape, 1))
    def marks_of(k):
        rows = []
        for r in range(k * CHUNK // LANES, (k + 1) * CHUNK // LANES):
            row = picks(spread(source[r : r + 1, :]), 0, blocks + 2)
            row += picks(spread(target[r : r + 1, :]), 0, blocks)
            rows.append(jnp.concatenate(row, axis=1))
        return jnp.concatenate(rows, axis=0)

    chunks = out.shape[0] // CHUNK
    following = marks_of(0)
    for k in range(chunks):
        here = slice(k * CHUNK, (k + 1) * CHUNK)
        first.get(k * CHUNK // PIECE)
        marks = following
        if k + 1 < chunks:
            following = marks_of(k + 1)
        select[here, :] = product(marks, where[...]).astype(BF16)
        rest = product(marks[:, count : count + 2 * LANES], table[...])
        out[here, :] = (first.target[here, :].astype(F32) + rest).astype(BF16)
        if (k + 1) * CHUNK % PIECE == 0:
            sent_out.start(k * CHUNK // PIECE)
            sent_select.start(k * CHUNK // PIECE)


def final_body(
    mine, theirs, w_src, w_descend, w_fine, w_dst, near, picked, target, select, edges, own_pick, fine,
    w_node, edge_w2, node_w2, node_w3, fine_out, mid_out, coarse_out, coarse, table, sums,
):
    core = lax.axis_index("c")
    half, width = mine.shape
    count = near.shape[0] // 5
    coarse[pl.ds(pl.multiple_of(core * half, half), half), :] = mine[...]
    coarse[pl.ds(pl.multiple_of((1 - core) * half, half), half), :] = theirs[...]
    parents = product(picked[...], coarse[...]).astype(BF16)
    down = product(parents, w_descend[...]).astype(BF16)
    middle = (near[...].astype(F32) + down.astype(F32)).astype(BF16)
    mid_out[...] = middle[2 * count : 3 * count]
    fine_down = product(middle, w_fine[...]).astype(BF16)
    closer = fine_down[count : 4 * count]
    table[: 5 * count] = product(fine_down, w_src[...]).astype(BF16)
    table[5 * count :] = product(closer, w_dst[...]).astype(BF16)
    rows = lax.broadcasted_iota(I32, (fine.shape[0], LANES), 0)
    for k in range(edges.shape[0] // CHUNK):
        here = slice(k * CHUNK, (k + 1) * CHUNK)
        piece = k * CHUNK // PIECE
        edge_sum = edges.get(piece)[here, :].astype(F32) + product(select.get(piece)[here, :], table[...])
        hidden = silu(edge_sum.astype(BF16))
        marks = range(k * CHUNK // LANES, (k + 1) * CHUNK // LANES)
        scatter = jnp.concatenate([hot(rows == target[r : r + 1, :]) for r in marks], axis=1)
        part = product(scatter, hidden)
        if k == 0:
            sums[...] = part
        else:
            sums[...] += part
    coarse_out[...] = coarse[: coarse_out.shape[0], :]
    reach = fine_down[count : 5 * count]
    lifted = (fine[...].astype(F32) + product(own_pick[...], reach)).astype(BF16)
    aggregate = product(sums[...].astype(BF16), edge_w2[...]).astype(BF16)
    hidden = silu(product(lifted, w_node[...]) + product(aggregate, node_w2[...]))
    fine_out[...] = updated(lifted, hidden, node_w3[...])


def swapped(values):
    return lax.ppermute(values, "c", [(0, 1), (1, 0)])


def crossed(values, tiles):
    pairs = [(t, t + 1) for t in range(1, tiles - 1, 2)]
    return lax.ppermute(values, TILE, pairs + [(b, a) for a, b in pairs])


def on_device(
    fine_latent,
    mid_latent,
    coarse_latent,
    fine_parent,
    mid_parent,
    halo_rows,
    edge_source,
    edge_target,
    w_child,
    mid_w1,
    mid_w2,
    mid_w3,
    w_coarse,
    coarse_w1,
    coarse_w2,
    coarse_w3,
    w_descend,
    w_fine,
    edge_w_src,
    edge_w_dst,
    edge_w2,
    node_w1,
    node_w2,
    node_w3,
):
    count, width = fine_latent.shape
    mids = mid_latent.shape[0]
    coarse_count = coarse_latent.shape[0]
    edge_count = edge_source.shape[0]
    planes, chips = lax.axis_size("z"), lax.axis_size("y") * lax.axis_size("x")
    tiles = 2 * chips
    half = chips * BLOCK
    wide = width + LANES
    parent = fine_parent.reshape(-1, LANES)
    source = edge_source.reshape(-1, LANES)
    target = edge_target.reshape(-1, LANES)
    halo = halo_rows.reshape(-1, LANES)

    def near(*shape, dtype=BF16):
        return pltpu.VMEM(shape, dtype)

    def far(*shape, dtype=BF16):
        return pltpu.HBM(shape, dtype)

    def here(array):
        return pltpu.with_memory_space_constraint(array, pltpu.VMEM)

    def free(*shape, dtype=BF16):
        return jax.ShapeDtypeStruct(shape, dtype)

    square = near(width, width)
    own, swap, cross = kernel_call(
        sums_body,
        [near(mids, width, dtype=F32), free(mids, width), free(mids, width)],
        [],
        stored=[parent, fine_latent],
        name="child_sums",
    )
    from_cross = crossed(cross, tiles)
    from_swap = swapped(swap)
    w_child, mid_w2, mid_w3, kept, hidden, labels = kernel_call(
        mid_ready_body,
        [square, square, square, near(mids, width), near(mids, width, dtype=F32), near(mids, LANES)],
        [],
        stored=[mid_latent, mid_parent[None], mid_w1, w_child, mid_w2, mid_w3],
        keep=[(3, 0), (4, 1), (5, 2)],
        after=[own],
        flops=1_000_000_000,
        name="mid_ready",
    )
    (labelled,) = kernel_call(
        mid_body,
        [free(mids, wide)],
        [here(own), from_swap, from_cross] + [here(a) for a in (kept, hidden, labels, w_child, mid_w2, mid_w3)],
        name="mid_update",
    )
    other = swapped(labelled)
    pair, blocks = kernel_call(
        blocks_body,
        [far(2 * mids, wide), near(half, width)],
        [labelled, other],
        name="coarse_blocks",
    )

    blocks = blocks.reshape(chips, BLOCK, width)
    parts = lax.all_to_all(blocks, PLANE, 0, 0)
    own_edges, halo_swap, cross, token = kernel_call(
        own_edges_body,
        [far(edge_count, width), far(LANES, wide), far(2 * mids + LANES, wide), free(8, LANES)],
        [],
        stored=[parent, halo, source, target, fine_latent, edge_w_src, edge_w_dst, pair],
        streams=[0],
        after=[blocks],
        limit=24,
        flops=4_000_000_000,
        name="own_edges",
    )

    (own_parts,) = kernel_call(
        gather_body, [near(planes, BLOCK, width)], [parts], after=[token], name="plane_sum"
    )
    in_planes = lax.all_to_all(own_parts, "z", 0, 0)
    halo_swap, cross, _ = lax.optimization_barrier((halo_swap, cross, own_parts))
    cross_in = crossed(cross, tiles)
    halo_in = swapped(halo_swap)
    w_coarse, coarse_w2, coarse_w3, own_latent, own_hidden = kernel_call(
        coarse_ready_body,
        [square, square, square, near(BLOCK, width), near(BLOCK, width, dtype=F32)],
        [],
        stored=[coarse_latent, coarse_w1, w_coarse, coarse_w2, coarse_w3],
        keep=[(2, 0), (3, 1), (4, 2)],
        after=[own_parts],
        flops=4_000_000_000,
        name="coarse_ready",
    )
    nearest, own_latent = lax.optimization_barrier((cross_in, own_latent))
    mid_in = swapped(jnp.where(lax.axis_index("c") == 0, nearest[mids : 2 * mids], nearest[:mids]))

    (results,) = kernel_call(
        coarse_body,
        [near(chips, BLOCK, width)],
        [in_planes] + [here(a) for a in (own_latent, own_hidden, w_coarse, coarse_w2, coarse_w3)],
        after=[cross_in, halo_in],
        name="coarse_update",
    )
    mine = lax.all_to_all(results, PLANE, 0, 0).reshape(half, width)
    w_src, w_descend, w_fine, w_dst, edges, select, own_pick, middle, picked = kernel_call(
        functools.partial(rest_edges_body, mids),
        [square] * 4
        + [far(edge_count, width), far(edge_count, 2 * LANES), far(count, LANES)]
        + [near(5 * mids, width), near(5 * mids, 2 * half)],
        [mid_in],
        stored=[parent, source, target, cross_in, halo_in, edge_w_src, pair, own_edges, w_descend, w_fine, edge_w_dst],
        keep=[(5, 0), (8, 1), (9, 2), (10, 3)],
        pieces=[7],
        streams=[4, 5],
        after=[results],
        scratch=[
            pltpu.VMEM((2 * LANES, width), BF16),
            pltpu.VMEM((2 * count + 2 * LANES, 2 * LANES), BF16),
            pltpu.VMEM((5 * mids, wide), BF16),
        ],
        limit=24,
        flops=4_000_000_000,
        name="rest_edges",
    )
    mine, own_pick = lax.optimization_barrier((mine, own_pick))
    theirs = swapped(mine)

    fine_out, mid_out, coarse_out = kernel_call(
        final_body,
        [free(count, width), free(mids, width), free(coarse_count, width)],
        [mine, theirs] + [here(a) for a in (w_src, w_descend, w_fine, w_dst, middle, picked)],
        stored=[target, select, edges, own_pick, fine_latent, node_w1, edge_w2, node_w2, node_w3],
        pieces=[1, 2],
        scratch=[
            pltpu.VMEM((2 * half, width), BF16),
            pltpu.VMEM((8 * mids, width), BF16),
            pltpu.VMEM((count, width), F32),
        ],
        limit=24,
        name="final",
    )
    return (fine_out, mid_out, coarse_out)


def solution(mesh):
    groups, tiles = mesh.shape["rhombus"], mesh.shape["tile"]
    side = {32: (4, 4), 8: (2, 2)}[tiles]
    physical = jax.sharding.Mesh(mesh.devices.reshape(groups, *side, 2), ("z", "y", "x", "c"))
    every = ("z", "y", "x", "c")
    split, copied = P(every), P()
    return jax.shard_map(
        on_device,
        mesh=physical,
        in_specs=(split, split, copied) + (split,) * 5 + (copied,) * 16,
        out_specs=(split, split, copied),
        check_vma=False,
    )
```

```python
import functools

import jax
import jax.numpy as jnp
from jax import lax
from jax.experimental import pallas as pl
from jax.experimental.pallas import tpu as pltpu
from jax.sharding import PartitionSpec as P

EPSILON = 1e-05
BLOCK = 24
LANES = 128
CHUNK = 512
PIECE = 1024
PLANE = ("y", "x")
TILE = ("y", "x", "c")
F32, BF16, I32 = jnp.float32, jnp.bfloat16, jnp.int32
VMEM = pl.BlockSpec(memory_space=pltpu.VMEM)
STORED = pl.BlockSpec(memory_space=pltpu.HBM)
UNREAD = pl.BlockSpec(memory_space=pl.ANY)


class Copied:
    def __init__(self, source, target, semaphores, first=0, pieces=1):
        rows = target.shape[0] // pieces
        self.target, self.copies = target, []
        for k in range(pieces):
            part = slice(k * rows, (k + 1) * rows) if pieces > 1 else slice(None)
            self.copies.append(pltpu.make_async_copy(source.at[part], target.at[part], semaphores.at[first + k]))
        self.waiting = [False] * pieces

    def start(self, k=None):
        for i in range(len(self.copies)) if k is None else (k,):
            self.copies[i].start()
            self.waiting[i] = True
        return self

    def get(self, k=None):
        for i in range(len(self.copies)) if k is None else (k,):
            if self.waiting[i]:
                self.copies[i].wait()
                self.waiting[i] = False
        return self.target

    def __getitem__(self, index):
        return self.get()[index]

    @property
    def shape(self):
        return self.target.shape


def kernel_call(
    body, outs, operands, stored=(), after=(), scratch=(), keep=(), streams=(), pieces=(), limit=8, flops=0, name=None
):
    count, held, skipped, given = len(operands), len(stored), len(after), len(outs)
    target = dict(keep)
    cuts = [stored[i].shape[0] // PIECE if i in pieces else 1 for i in range(held)]
    flows = dict(streams)

    def kernel(*refs):
        inputs, refs = refs[:count], refs[count:]
        sources, refs = refs[:held], refs[held + skipped :]
        results, refs = refs[:given], refs[given:]
        own, refs = refs[: len(scratch)], refs[len(scratch) :]
        buffers = iter(refs)
        places = [results[target[i]] if i in target else next(buffers) for i in range(held)]
        leaving = {o: next(buffers) for o in flows}
        semaphores = next(buffers) if held or flows else None
        first, copies, fresh = 0, [], []
        for i in range(held):
            copies.append(Copied(sources[i], places[i], semaphores, first, cuts[i]).start())
            first += cuts[i]
        for o in range(given):
            if o in flows:
                fresh.append(Copied(leaving[o], results[o], semaphores, first, flows[o]))
                first += flows[o]
            elif o not in target.values():
                fresh.append(results[o])
        body(*inputs, *copies, *fresh, *leaving.values(), *own)
        for copy in copies + fresh:
            if isinstance(copy, Copied):
                copy.get()

    buffers = [pltpu.VMEM(stored[i].shape, stored[i].dtype) for i in range(held) if i not in target]
    buffers += [pltpu.VMEM(outs[o].shape, outs[o].dtype) for o in flows]
    if held or flows:
        buffers.append(pltpu.SemaphoreType.DMA((sum(cuts) + sum(flows.values()),)))
    return pl.pallas_call(
        kernel,
        out_shape=outs,
        in_specs=[VMEM] * count + [STORED] * held + [UNREAD] * skipped,
        out_specs=[STORED if o in flows else VMEM for o in range(given)],
        scratch_shapes=[*scratch, *buffers],
        compiler_params=pltpu.CompilerParams(vmem_limit_bytes=limit << 20),
        cost_estimate=pl.CostEstimate(flops=flops, bytes_accessed=1 << 20, transcendentals=0),
        name=name,
    )(*operands, *[pltpu.with_memory_space_constraint(array, pltpu.HBM) for array in stored], *after)


def product(left, right):
    return jnp.dot(left, right, preferred_element_type=F32)


def silu(values):
    half = 0.5 * values
    return half + half * jnp.tanh(half)


def updated(latent, hidden, third):
    values = product(hidden.astype(BF16), third)
    scale = lax.rsqrt(jnp.mean(values * values, axis=-1, keepdims=True) + EPSILON)
    return (latent.astype(F32) + values * scale).astype(BF16)


def lanes(height, first=0):
    return lax.broadcasted_iota(I32, (height, LANES), 1) + first


def spread(row):
    return jnp.broadcast_to(row, (LANES, LANES)).T


def hot(mask):
    return jnp.where(mask, 1.0, 0.0).astype(BF16)


def picks(spread_ids, first, blocks):
    return [hot(spread_ids == lanes(LANES, first + LANES * q)) for q in range(blocks)]


def sums_body(parent, fine, own, swap, cross):
    count = own.shape[0]
    core = lax.axis_index("c")
    rows = lax.broadcasted_iota(I32, (3 * count, LANES), 0)
    blocks = [hot(rows == parent[r : r + 1, :]) for r in range(parent.shape[0])]
    sums = product(jnp.concatenate(blocks, axis=1), fine[...])
    own[...] = sums[:count]
    down, up = sums[count : 2 * count].astype(BF16), sums[2 * count :].astype(BF16)
    swap[...] = jnp.where(core == 0, up, down)
    cross[...] = jnp.where(core == 0, down, up)


def mid_ready_body(latent, ids, first, w_child, second, third, kept, hidden, labels):
    count = hidden.shape[0]
    spread_ids = spread(jnp.concatenate([ids[...], jnp.zeros((1, LANES - count), I32)], axis=1))[:count]
    place = lanes(count)
    label = jnp.where(place == 0, spread_ids >> 5, jnp.where(place == 1, spread_ids & 31, 0))
    labels[...] = label.astype(F32).astype(BF16)
    values = latent[...]
    kept[...] = values
    hidden[...] = product(values, first[...])


def mid_body(own, before, after, latent, hidden, labels, w_child, second, third, out):
    width = latent.shape[1]
    total = own[...] + before[...].astype(F32) + after[...].astype(F32)
    incoming = product(total.astype(BF16), w_child[...]).astype(BF16)
    value = silu(hidden[...] + product(incoming, second[...]))
    out[:, :width] = updated(latent[...], value, third[...])
    out[:, width:] = labels[...]


def row_ids(labelled, width):
    label = labelled[:, width:].astype(F32)
    return (label[:, :1] * 32.0 + label[:, 1:2]).astype(I32)


def blocks_body(mine, theirs, pair, out):
    count, width = mine.shape[0], out.shape[1]
    half = out.shape[0]
    core = lax.axis_index("c")
    pair[pl.ds(pl.multiple_of(core * count, count), count), :] = mine[...]
    pair[pl.ds(pl.multiple_of((1 - core) * count, count), count), :] = theirs[...]
    both = pair[...]
    columns = lax.broadcasted_iota(I32, (2 * count, half), 1) + core * half
    picked = hot(row_ids(both, width) == columns)
    out[...] = lax.dot_general(
        picked, both[:, :width], (((0,), (0,)), ((), ())), preferred_element_type=F32
    ).astype(BF16)


def own_edges_body(
    parent, halo, source, target, fine, w_src, w_dst, pair, sent_out, swap, cross, token, out
):
    token[...] = jnp.zeros_like(token)
    count, width = fine.shape
    two, blocks = pair.shape[0], count // LANES
    core = lax.axis_index("c")
    codes = [(spread(parent[r : r + 1, :]) + 1).astype(F32).astype(BF16) for r in range(blocks)]
    codes = jnp.concatenate(codes, axis=0)
    rows = halo[...]
    values = fine[...]
    sent = product(values, w_src[...]).astype(BF16)
    received = product(values, w_dst[...]).astype(BF16)

    def marks_of(k):
        both = []
        for ids in (source, target):
            rows = range(k * CHUNK // LANES, (k + 1) * CHUNK // LANES)
            rows = [jnp.concatenate(picks(spread(ids[r : r + 1, :]), 0, blocks), axis=1) for r in rows]
            both.append(jnp.concatenate(rows, axis=0))
        return both

    chunks = out.shape[0] // CHUNK
    following = marks_of(0)
    for k in range(chunks):
        sources, targets = following
        if k + 1 < chunks:
            following = marks_of(k + 1)
        total = product(sources, sent) + product(targets, received)
        out[k * CHUNK : (k + 1) * CHUNK, :] = total.astype(BF16)
        if (k + 1) * CHUNK % PIECE == 0:
            sent_out.start(k * CHUNK // PIECE)
    for place, first, row in (
        (swap, 0, jnp.where(core == 0, rows[1:2], rows[:1])),
        (cross, two, jnp.where(core == 0, rows[:1], rows[1:2])),
    ):
        picked = jnp.concatenate(picks(spread(row), 0, blocks), axis=1)
        place[first : first + LANES, :width] = product(picked, values).astype(BF16)
        place[first : first + LANES, width:] = product(picked, codes).astype(BF16)
    cross[:two] = pair[...]


def gather_body(parts, out):
    total = jnp.sum(parts[...].astype(F32), axis=0).astype(BF16)
    for i in range(out.shape[0]):
        out[i] = total


def coarse_body(parts, own_latent, own_hidden, w_coarse, second, third, out):
    total = jnp.sum(parts[...].astype(F32), axis=0).astype(BF16)
    incoming = product(total, w_coarse[...]).astype(BF16)
    hidden = silu(own_hidden[...] + product(incoming, second[...]))
    result = updated(own_latent[...], hidden, third[...])
    for i in range(out.shape[0]):
        out[i] = result


def coarse_ready_body(coarse, coarse_w1, w_coarse, second, third, own_latent, own_hidden):
    rows, total = own_latent.shape[0], coarse.shape[0]
    chips = lax.axis_size("y") * lax.axis_size("x")
    chip = lax.axis_index("y") * lax.axis_size("x") + lax.axis_index("x")
    first = (lax.axis_index("c") * chips + chip) * rows
    place = lax.broadcasted_iota(I32, (rows, total), 0) + first
    picked = hot(place == lax.broadcasted_iota(I32, (rows, total), 1))
    latent = product(picked, coarse[...]).astype(BF16)
    own_latent[...] = latent
    own_hidden[...] = product(latent, coarse_w1[...])


def slots(codes, tile, count):
    parent = codes - 1
    side = parent // count
    away = jnp.where(side == 1, -1, jnp.where(side == 2, 1, 0))
    return jnp.where(codes > 0, (tile + away) * count + (parent & (count - 1)), -1)


def picks_body(mid_count, cross, swap, parent, source, target, sent_select, own_pick, token, select, where):
    token[...] = jnp.zeros_like(token)
    core = lax.axis_index("c")
    count = own_pick.shape[0]
    width = swap.shape[1] - LANES
    blocks = count // LANES
    two = cross.shape[0] - LANES
    for r in range(blocks):
        place = slots(spread(parent[r : r + 1, :]) + 1, 2, mid_count)
        rows = slice(r * LANES, (r + 1) * LANES)
        where[rows, :] = jnp.concatenate(picks(place, 0, 2), axis=1)
        near = place - mid_count
        own_pick[rows, :] = hot(near == lanes(LANES))
        far = place + 4 * mid_count
        there = slice(count + 2 * LANES + r * LANES, count + 2 * LANES + (r + 1) * LANES)
        where[there, :] = jnp.concatenate(picks(far, 0, 2), axis=1)
    for codes, late in ((cross[two:, width:], core), (swap[:, width:], 1 - core)):
        place = slots(codes.astype(F32).astype(I32), 1 + 2 * late, mid_count)
        rows = pl.ds(pl.multiple_of(count + late * LANES, LANES), LANES)
        where[rows, :] = jnp.concatenate(picks(place, 0, 2), axis=1)

    def marks_of(k):
        rows = []
        for r in range(k * CHUNK // LANES, (k + 1) * CHUNK // LANES):
            row = picks(spread(source[r : r + 1, :]), 0, blocks + 2)
            row += picks(spread(target[r : r + 1, :]), 0, blocks)
            rows.append(jnp.concatenate(row, axis=1))
        return jnp.concatenate(rows, axis=0)

    chunks = select.shape[0] // CHUNK
    following = marks_of(0)
    for k in range(chunks):
        marks = following
        if k + 1 < chunks:
            following = marks_of(k + 1)
        select[k * CHUNK : (k + 1) * CHUNK, :] = product(marks, where[...]).astype(BF16)
        if (k + 1) * CHUNK % PIECE == 0:
            sent_select.start(k * CHUNK // PIECE)


def halo_edges_body(
    mid_count, mid_swap, source, cross, swap, w_src, pair, first, w_descend, w_fine, w_dst,
    sent_out, middle, picked, out, table, window
):
    core = lax.axis_index("c")
    count = 4 * LANES
    width = out.shape[1]
    half = picked.shape[1] // 2
    two = pair.shape[0]
    for values, late in ((cross[two:], core), (swap[...], 1 - core)):
        rows = pl.ds(pl.multiple_of(late * LANES, LANES), LANES)
        table[rows, :] = product(values[:, :width], w_src[...]).astype(BF16)
    window[pl.ds(pl.multiple_of((1 - core) * 4 * mid_count, mid_count), mid_count), :] = mid_swap[...]
    window[pl.ds(pl.multiple_of(core * 3 * mid_count, mid_count), two), :] = cross[:two]
    window[pl.ds(pl.multiple_of((2 - core) * mid_count, mid_count), two), :] = pair[...]
    near = window[...]
    middle[...] = near[:, :width]
    ids = row_ids(near, width)
    mine = ids - core * half
    place = jnp.where((mine >= 0) & (mine < half), mine, ids - (1 - core) * half + half)
    picked[...] = hot(place == lax.broadcasted_iota(I32, picked.shape, 1))

    def marks_of(k):
        rows = range(k * CHUNK // LANES, (k + 1) * CHUNK // LANES)
        rows = [jnp.concatenate(picks(spread(source[r : r + 1, :]), count, 2), axis=1) for r in rows]
        return jnp.concatenate(rows, axis=0)

    chunks = out.shape[0] // CHUNK
    following = marks_of(0)
    for k in range(chunks):
        here = slice(k * CHUNK, (k + 1) * CHUNK)
        first.get(k * CHUNK // PIECE)
        marks = following
        if k + 1 < chunks:
            following = marks_of(k + 1)
        out[here, :] = (first.target[here, :].astype(F32) + product(marks, table[...])).astype(BF16)
        if (k + 1) * CHUNK % PIECE == 0:
            sent_out.start(k * CHUNK // PIECE)


def final_body(
    mine, theirs, w_src, w_descend, w_fine, w_dst, near, picked, target, select, edges, own_pick, fine,
    w_node, edge_w2, node_w2, node_w3, sent_fine, sent_mid, sent_coarse, fine_out, mid_out, coarse_out, table, sums,
):
    core = lax.axis_index("c")
    half = mine.shape[0]
    count = near.shape[0] // 5
    parents = product(picked[:, :half], mine[...]) + product(picked[:, half:], theirs[...])
    down = product(parents.astype(BF16), w_descend[...]).astype(BF16)
    middle = (near[...].astype(F32) + down.astype(F32)).astype(BF16)
    mid_out[...] = middle[2 * count : 3 * count]
    sent_mid.start()
    fine_down = product(middle, w_fine[...]).astype(BF16)
    closer = fine_down[count : 4 * count]
    table[: 5 * count] = product(fine_down, w_src[...]).astype(BF16)
    table[5 * count :] = product(closer, w_dst[...]).astype(BF16)
    coarse_out[:half] = jnp.where(core == 0, mine[...], theirs[...])
    rest = coarse_out.shape[0] - half
    coarse_out[half:] = jnp.where(core == 0, theirs[:rest], mine[:rest])
    rows = lax.broadcasted_iota(I32, (fine.shape[0], LANES), 0)
    for k in range(edges.shape[0] // CHUNK):
        here = slice(k * CHUNK, (k + 1) * CHUNK)
        piece = k * CHUNK // PIECE
        edge_sum = edges.get(piece)[here, :].astype(F32) + product(select.get(piece)[here, :], table[...])
        hidden = silu(edge_sum.astype(BF16))
        marks = range(k * CHUNK // LANES, (k + 1) * CHUNK // LANES)
        scatter = jnp.concatenate([hot(rows == target[r : r + 1, :]) for r in marks], axis=1)
        part = product(scatter, hidden)
        if k == 0:
            sums[...] = part
        else:
            sums[...] += part
    sent_coarse.start()
    reach = fine_down[count : 5 * count]
    lifted = (fine[...].astype(F32) + product(own_pick[...], reach)).astype(BF16)
    aggregate = product(sums[...].astype(BF16), edge_w2[...]).astype(BF16)
    hidden = silu(product(lifted, w_node[...]) + product(aggregate, node_w2[...])).astype(BF16)
    third = node_w3[...]
    rows = fine_out.shape[0] // 2
    for i in range(2):
        here = slice(i * rows, (i + 1) * rows)
        fine_out[here, :] = updated(lifted[here], hidden[here], third)
        sent_fine.start(i)


def swapped(values):
    return lax.ppermute(values, "c", [(0, 1), (1, 0)])


def crossed(values, tiles):
    pairs = [(t, t + 1) for t in range(1, tiles - 1, 2)]
    return lax.ppermute(values, TILE, pairs + [(b, a) for a, b in pairs])


def on_device(
    fine_latent,
    mid_latent,
    coarse_latent,
    fine_parent,
    mid_parent,
    halo_rows,
    edge_source,
    edge_target,
    w_child,
    mid_w1,
    mid_w2,
    mid_w3,
    w_coarse,
    coarse_w1,
    coarse_w2,
    coarse_w3,
    w_descend,
    w_fine,
    edge_w_src,
    edge_w_dst,
    edge_w2,
    node_w1,
    node_w2,
    node_w3,
):
    count, width = fine_latent.shape
    mids = mid_latent.shape[0]
    coarse_count = coarse_latent.shape[0]
    edge_count = edge_source.shape[0]
    planes, chips = lax.axis_size("z"), lax.axis_size("y") * lax.axis_size("x")
    tiles = 2 * chips
    half = chips * BLOCK
    wide = width + LANES
    parent = fine_parent.reshape(-1, LANES)
    source = edge_source.reshape(-1, LANES)
    target = edge_target.reshape(-1, LANES)
    halo = halo_rows.reshape(-1, LANES)

    def near(*shape, dtype=BF16):
        return pltpu.VMEM(shape, dtype)

    def far(*shape, dtype=BF16):
        return pltpu.HBM(shape, dtype)

    def here(array):
        return pltpu.with_memory_space_constraint(array, pltpu.VMEM)

    def free(*shape, dtype=BF16):
        return jax.ShapeDtypeStruct(shape, dtype)

    square = near(width, width)
    own, swap, cross = kernel_call(
        sums_body,
        [near(mids, width, dtype=F32), free(mids, width), free(mids, width)],
        [],
        stored=[parent, fine_latent],
        name="child_sums",
    )
    from_cross = crossed(cross, tiles)
    from_swap = swapped(swap)
    w_child, mid_w2, mid_w3, kept, hidden, labels = kernel_call(
        mid_ready_body,
        [square, square, square, near(mids, width), near(mids, width, dtype=F32), near(mids, LANES)],
        [],
        stored=[mid_latent, mid_parent[None], mid_w1, w_child, mid_w2, mid_w3],
        keep=[(3, 0), (4, 1), (5, 2)],
        after=[own],
        flops=1_000_000_000,
        name="mid_ready",
    )
    (labelled,) = kernel_call(
        mid_body,
        [free(mids, wide)],
        [here(own), from_swap, from_cross] + [here(a) for a in (kept, hidden, labels, w_child, mid_w2, mid_w3)],
        name="mid_update",
    )
    other = swapped(labelled)
    pair, blocks = kernel_call(
        blocks_body,
        [far(2 * mids, wide), near(half, width)],
        [labelled, other],
        name="coarse_blocks",
    )

    blocks = blocks.reshape(chips, BLOCK, width)
    parts = lax.all_to_all(blocks, PLANE, 0, 0)
    own_edges, halo_swap, cross, token = kernel_call(
        own_edges_body,
        [far(edge_count, width), far(LANES, wide), far(2 * mids + LANES, wide), free(8, LANES)],
        [],
        stored=[parent, halo, source, target, fine_latent, edge_w_src, edge_w_dst, pair],
        streams=[(0, edge_count // PIECE)],
        after=[blocks],
        limit=24,
        flops=4_000_000_000,
        name="own_edges",
    )

    (own_parts,) = kernel_call(
        gather_body, [near(planes, BLOCK, width)], [parts], after=[token], name="plane_sum"
    )
    in_planes = lax.all_to_all(own_parts, "z", 0, 0)
    halo_swap, cross, _ = lax.optimization_barrier((halo_swap, cross, own_parts))
    cross_in = crossed(cross, tiles)
    halo_in = swapped(halo_swap)
    w_coarse, coarse_w2, coarse_w3, own_latent, own_hidden = kernel_call(
        coarse_ready_body,
        [square, square, square, near(BLOCK, width), near(BLOCK, width, dtype=F32)],
        [],
        stored=[coarse_latent, coarse_w1, w_coarse, coarse_w2, coarse_w3],
        keep=[(2, 0), (3, 1), (4, 2)],
        after=[own_parts],
        flops=1_000_000_000,
        name="coarse_ready",
    )
    nearest, own_latent = lax.optimization_barrier((cross_in, own_latent))
    mid_in = swapped(jnp.where(lax.axis_index("c") == 0, nearest[mids : 2 * mids], nearest[:mids]))
    select, own_pick, token = kernel_call(
        functools.partial(picks_body, mids),
        [far(edge_count, 2 * LANES), far(count, LANES), free(8, LANES)],
        [cross_in, halo_in],
        stored=[parent, source, target],
        streams=[(0, edge_count // PIECE)],
        after=[own_latent],
        scratch=[pltpu.VMEM((2 * count + 2 * LANES, 2 * LANES), BF16)],
        limit=16,
        flops=3_000_000_000,
        name="picks",
    )

    (results,) = kernel_call(
        coarse_body,
        [near(chips, BLOCK, width)],
        [in_planes] + [here(a) for a in (own_latent, own_hidden, w_coarse, coarse_w2, coarse_w3)],
        after=[token, mid_in],
        name="coarse_update",
    )
    mine = lax.all_to_all(results, PLANE, 0, 0).reshape(half, width)
    w_src, w_descend, w_fine, w_dst, edges, middle, picked = kernel_call(
        functools.partial(halo_edges_body, mids),
        [square] * 4 + [far(edge_count, width), near(5 * mids, width), near(5 * mids, 2 * half)],
        [mid_in],
        stored=[source, cross_in, halo_in, edge_w_src, pair, own_edges, w_descend, w_fine, edge_w_dst],
        keep=[(3, 0), (6, 1), (7, 2), (8, 3)],
        pieces=[5],
        streams=[(4, edge_count // PIECE)],
        after=[results],
        scratch=[pltpu.VMEM((2 * LANES, width), BF16), pltpu.VMEM((5 * mids, wide), BF16)],
        limit=24,
        flops=4_000_000_000,
        name="halo_edges",
    )
    mine, edges = lax.optimization_barrier((mine, edges))
    theirs = swapped(mine)

    fine_out, mid_out, coarse_out = kernel_call(
        final_body,
        [far(count, width), far(mids, width), far(coarse_count, width)],
        [mine, theirs] + [here(a) for a in (w_src, w_descend, w_fine, w_dst, middle, picked)],
        stored=[target, select, edges, own_pick, fine_latent, node_w1, edge_w2, node_w2, node_w3],
        pieces=[1, 2],
        streams=[(0, 2), (1, 1), (2, 1)],
        scratch=[pltpu.VMEM((8 * mids, width), BF16), pltpu.VMEM((count, width), F32)],
        limit=24,
        name="final",
    )
    return (fine_out, mid_out, coarse_out)


def solution(mesh):
    groups, tiles = mesh.shape["rhombus"], mesh.shape["tile"]
    side = {32: (4, 4), 8: (2, 2)}[tiles]
    physical = jax.sharding.Mesh(mesh.devices.reshape(groups, *side, 2), ("z", "y", "x", "c"))
    every = ("z", "y", "x", "c")
    split, copied = P(every), P()
    return jax.shard_map(
        on_device,
        mesh=physical,
        in_specs=(split, split, copied) + (split,) * 5 + (copied,) * 16,
        out_specs=(split, split, copied),
        check_vma=False,
    )
```

```python
import functools

import jax
import jax.numpy as jnp
from jax import lax
from jax.experimental import pallas as pl
from jax.experimental.pallas import tpu as pltpu
from jax.sharding import PartitionSpec as P

EPSILON = 1e-05
BLOCK = 24
LANES = 128
CHUNK = 512
PIECE = 1024
PLANE = ("y", "x")
TILE = ("y", "x", "c")
F32, BF16, I32 = jnp.float32, jnp.bfloat16, jnp.int32
VMEM = pl.BlockSpec(memory_space=pltpu.VMEM)
STORED = pl.BlockSpec(memory_space=pltpu.HBM)
UNREAD = pl.BlockSpec(memory_space=pl.ANY)


class Copied:
    def __init__(self, source, target, semaphores, first=0, pieces=1):
        rows = target.shape[0] // pieces
        self.target, self.copies = target, []
        for k in range(pieces):
            part = slice(k * rows, (k + 1) * rows) if pieces > 1 else slice(None)
            self.copies.append(pltpu.make_async_copy(source.at[part], target.at[part], semaphores.at[first + k]))
        self.waiting = [False] * pieces

    def start(self, k=None):
        for i in range(len(self.copies)) if k is None else (k,):
            self.copies[i].start()
            self.waiting[i] = True
        return self

    def get(self, k=None):
        for i in range(len(self.copies)) if k is None else (k,):
            if self.waiting[i]:
                self.copies[i].wait()
                self.waiting[i] = False
        return self.target

    def __getitem__(self, index):
        return self.get()[index]

    @property
    def shape(self):
        return self.target.shape


def kernel_call(
    body, outs, operands, stored=(), after=(), scratch=(), keep=(), streams=(), pieces=(), limit=8, flops=0, name=None
):
    count, held, skipped, given = len(operands), len(stored), len(after), len(outs)
    target = dict(keep)
    cuts = [stored[i].shape[0] // PIECE if i in pieces else 1 for i in range(held)]
    flows = dict(streams)

    def kernel(*refs):
        inputs, refs = refs[:count], refs[count:]
        sources, refs = refs[:held], refs[held + skipped :]
        results, refs = refs[:given], refs[given:]
        own, refs = refs[: len(scratch)], refs[len(scratch) :]
        buffers = iter(refs)
        places = [results[target[i]] if i in target else next(buffers) for i in range(held)]
        leaving = {o: next(buffers) for o in flows}
        semaphores = next(buffers) if held or flows else None
        first, copies, fresh = 0, [], []
        for i in range(held):
            copies.append(Copied(sources[i], places[i], semaphores, first, cuts[i]).start())
            first += cuts[i]
        for o in range(given):
            if o in flows:
                fresh.append(Copied(leaving[o], results[o], semaphores, first, flows[o]))
                first += flows[o]
            elif o not in target.values():
                fresh.append(results[o])
        body(*inputs, *copies, *fresh, *leaving.values(), *own)
        for copy in copies + fresh:
            if isinstance(copy, Copied):
                copy.get()

    buffers = [pltpu.VMEM(stored[i].shape, stored[i].dtype) for i in range(held) if i not in target]
    buffers += [pltpu.VMEM(outs[o].shape, outs[o].dtype) for o in flows]
    if held or flows:
        buffers.append(pltpu.SemaphoreType.DMA((sum(cuts) + sum(flows.values()),)))
    return pl.pallas_call(
        kernel,
        out_shape=outs,
        in_specs=[VMEM] * count + [STORED] * held + [UNREAD] * skipped,
        out_specs=[STORED if o in flows else VMEM for o in range(given)],
        scratch_shapes=[*scratch, *buffers],
        compiler_params=pltpu.CompilerParams(vmem_limit_bytes=limit << 20),
        cost_estimate=pl.CostEstimate(flops=flops, bytes_accessed=1 << 20, transcendentals=0),
        name=name,
    )(*operands, *[pltpu.with_memory_space_constraint(array, pltpu.HBM) for array in stored], *after)


def product(left, right):
    return jnp.dot(left, right, preferred_element_type=F32)


def silu(values):
    half = 0.5 * values
    return half + half * jnp.tanh(half)


def updated(latent, hidden, third):
    values = product(hidden.astype(BF16), third)
    scale = lax.rsqrt(jnp.mean(values * values, axis=-1, keepdims=True) + EPSILON)
    return (latent.astype(F32) + values * scale).astype(BF16)


def lanes(height, first=0):
    return lax.broadcasted_iota(I32, (height, LANES), 1) + first


def spread(row):
    return jnp.broadcast_to(row, (LANES, LANES)).T


def hot(mask):
    return jnp.where(mask, 1.0, 0.0).astype(BF16)


def picks(spread_ids, first, blocks):
    return [hot(spread_ids == lanes(LANES, first + LANES * q)) for q in range(blocks)]


def sums_body(parent, fine, own, swap, cross):
    count = own.shape[0]
    core = lax.axis_index("c")
    rows = lax.broadcasted_iota(I32, (3 * count, LANES), 0)
    blocks = [hot(rows == parent[r : r + 1, :]) for r in range(parent.shape[0])]
    sums = product(jnp.concatenate(blocks, axis=1), fine[...])
    own[...] = sums[:count]
    down, up = sums[count : 2 * count].astype(BF16), sums[2 * count :].astype(BF16)
    swap[...] = jnp.where(core == 0, up, down)
    cross[...] = jnp.where(core == 0, down, up)


def mid_ready_body(latent, ids, first, w_child, second, third, kept, hidden, labels):
    count = hidden.shape[0]
    spread_ids = spread(jnp.concatenate([ids[...], jnp.zeros((1, LANES - count), I32)], axis=1))[:count]
    place = lanes(count)
    label = jnp.where(place == 0, spread_ids >> 5, jnp.where(place == 1, spread_ids & 31, 0))
    labels[...] = label.astype(F32).astype(BF16)
    values = latent[...]
    kept[...] = values
    hidden[...] = product(values, first[...])


def mid_body(own, before, after, latent, hidden, labels, w_child, second, third, out):
    width = latent.shape[1]
    total = own[...] + before[...].astype(F32) + after[...].astype(F32)
    incoming = product(total.astype(BF16), w_child[...]).astype(BF16)
    value = silu(hidden[...] + product(incoming, second[...]))
    out[:, :width] = updated(latent[...], value, third[...])
    out[:, width:] = labels[...]


def row_ids(labelled, width):
    label = labelled[:, width:].astype(F32)
    return (label[:, :1] * 32.0 + label[:, 1:2]).astype(I32)


def blocks_body(mine, theirs, pair, out):
    count, width = mine.shape[0], out.shape[1]
    half = out.shape[0]
    core = lax.axis_index("c")
    pair[pl.ds(pl.multiple_of(core * count, count), count), :] = mine[...]
    pair[pl.ds(pl.multiple_of((1 - core) * count, count), count), :] = theirs[...]
    both = pair[...]
    columns = lax.broadcasted_iota(I32, (2 * count, half), 1) + core * half
    picked = hot(row_ids(both, width) == columns)
    out[...] = lax.dot_general(
        picked, both[:, :width], (((0,), (0,)), ((), ())), preferred_element_type=F32
    ).astype(BF16)


def own_edges_body(
    parent, halo, source, target, fine, w_src, w_dst, pair, sent_out, swap, cross, token, out
):
    token[...] = jnp.zeros_like(token)
    count, width = fine.shape
    two, blocks = pair.shape[0], count // LANES
    core = lax.axis_index("c")
    codes = [(spread(parent[r : r + 1, :]) + 1).astype(F32).astype(BF16) for r in range(blocks)]
    codes = jnp.concatenate(codes, axis=0)
    rows = halo[...]
    values = fine[...]
    sent = product(values, w_src[...]).astype(BF16)
    received = product(values, w_dst[...]).astype(BF16)

    def marks_of(k):
        both = []
        for ids in (source, target):
            rows = range(k * CHUNK // LANES, (k + 1) * CHUNK // LANES)
            rows = [jnp.concatenate(picks(spread(ids[r : r + 1, :]), 0, blocks), axis=1) for r in rows]
            both.append(jnp.concatenate(rows, axis=0))
        return both

    chunks = out.shape[0] // CHUNK
    following = marks_of(0)
    for k in range(chunks):
        sources, targets = following
        if k + 1 < chunks:
            following = marks_of(k + 1)
        total = product(sources, sent) + product(targets, received)
        out[k * CHUNK : (k + 1) * CHUNK, :] = total.astype(BF16)
        if (k + 1) * CHUNK % PIECE == 0:
            sent_out.start(k * CHUNK // PIECE)
    for place, first, row in (
        (swap, 0, jnp.where(core == 0, rows[1:2], rows[:1])),
        (cross, two, jnp.where(core == 0, rows[:1], rows[1:2])),
    ):
        picked = jnp.concatenate(picks(spread(row), 0, blocks), axis=1)
        place[first : first + LANES, :width] = product(picked, values).astype(BF16)
        place[first : first + LANES, width:] = product(picked, codes).astype(BF16)
    cross[:two] = pair[...]


def gather_body(parts, out):
    total = jnp.sum(parts[...].astype(F32), axis=0).astype(BF16)
    for i in range(out.shape[0]):
        out[i] = total


def coarse_body(parts, own_latent, own_hidden, both, third, out):
    total = jnp.sum(parts[...].astype(F32), axis=0).astype(BF16)
    hidden = silu(own_hidden[...] + product(total, both[...]))
    result = updated(own_latent[...], hidden, third[...])
    for i in range(out.shape[0]):
        out[i] = result


def coarse_ready_body(
    coarse, coarse_w1, w_coarse, coarse_w2, edge_w2, node_w2, third, both, last, own_latent, own_hidden
):
    rows, total = own_latent.shape[0], coarse.shape[0]
    chips = lax.axis_size("y") * lax.axis_size("x")
    chip = lax.axis_index("y") * lax.axis_size("x") + lax.axis_index("x")
    first = (lax.axis_index("c") * chips + chip) * rows
    place = lax.broadcasted_iota(I32, (rows, total), 0) + first
    picked = hot(place == lax.broadcasted_iota(I32, (rows, total), 1))
    latent = product(picked, coarse[...]).astype(BF16)
    own_latent[...] = latent
    own_hidden[...] = product(latent, coarse_w1[...])
    both[...] = product(w_coarse[...], coarse_w2[...]).astype(BF16)
    last[...] = product(edge_w2[...], node_w2[...]).astype(BF16)


def slots(codes, tile, count):
    parent = codes - 1
    side = parent // count
    away = jnp.where(side == 1, -1, jnp.where(side == 2, 1, 0))
    return jnp.where(codes > 0, (tile + away) * count + (parent & (count - 1)), -1)


def rest_edges_body(
    mid_count, mid_swap, parent, source, target, cross, swap, w_src, pair, first, w_descend, w_fine, w_dst,
    sent_out, sent_select, own_pick, middle, picked, out, select, table, where, window
):
    core = lax.axis_index("c")
    count = own_pick.shape[0]
    width = out.shape[1]
    blocks = count // LANES
    two = pair.shape[0]
    for r in range(blocks):
        place = slots(spread(parent[r : r + 1, :]) + 1, 2, mid_count)
        rows = slice(r * LANES, (r + 1) * LANES)
        where[rows, :] = jnp.concatenate(picks(place, 0, 2), axis=1)
        near = place - mid_count
        own_pick[rows, :] = hot(near == lanes(LANES))
        far = place + 4 * mid_count
        there = slice(count + 2 * LANES + r * LANES, count + 2 * LANES + (r + 1) * LANES)
        where[there, :] = jnp.concatenate(picks(far, 0, 2), axis=1)
    for values, late in ((cross[two:], core), (swap[...], 1 - core)):
        rows = pl.ds(pl.multiple_of(late * LANES, LANES), LANES)
        table[rows, :] = product(values[:, :width], w_src[...]).astype(BF16)
        place = slots(values[:, width:].astype(F32).astype(I32), 1 + 2 * late, mid_count)
        rows = pl.ds(pl.multiple_of(count + late * LANES, LANES), LANES)
        where[rows, :] = jnp.concatenate(picks(place, 0, 2), axis=1)
    window[pl.ds(pl.multiple_of((1 - core) * 4 * mid_count, mid_count), mid_count), :] = mid_swap[...]
    window[pl.ds(pl.multiple_of(core * 3 * mid_count, mid_count), two), :] = cross[:two]
    window[pl.ds(pl.multiple_of((2 - core) * mid_count, mid_count), two), :] = pair[...]
    near = window[...]
    middle[...] = near[:, :width]
    half = picked.shape[1] // 2
    ids = row_ids(near, width)
    mine = ids - core * half
    place = jnp.where((mine >= 0) & (mine < half), mine, ids - (1 - core) * half + half)
    picked[...] = hot(place == lax.broadcasted_iota(I32, picked.shape, 1))

    def marks_of(k):
        rows = []
        for r in range(k * CHUNK // LANES, (k + 1) * CHUNK // LANES):
            row = picks(spread(source[r : r + 1, :]), 0, blocks + 2)
            row += picks(spread(target[r : r + 1, :]), 0, blocks)
            rows.append(jnp.concatenate(row, axis=1))
        return jnp.concatenate(rows, axis=0)

    chunks = out.shape[0] // CHUNK
    ready = []
    following = marks_of(0)
    for k in range(chunks):
        here = slice(k * CHUNK, (k + 1) * CHUNK)
        first.get(k * CHUNK // PIECE)
        marks = following
        if k + 1 < chunks:
            following = marks_of(k + 1)
        select[here, :] = product(marks, where[...]).astype(BF16)
        rest = product(marks[:, count : count + 2 * LANES], table[...])
        out[here, :] = (first.target[here, :].astype(F32) + rest).astype(BF16)
        ready += [k]
        if k % 2 == 1 or k >= chunks - 2:
            for i in ready:
                sent_out.start(i)
                sent_select.start(i)
            ready = []


def final_body(
    mine, theirs, w_src, w_descend, w_fine, w_dst, near, picked, target, select, edges, own_pick, fine,
    w_node, last, node_w3, sent_fine, sent_mid, sent_coarse, fine_out, mid_out, coarse_out, table, sums,
):
    core = lax.axis_index("c")
    half = mine.shape[0]
    count = near.shape[0] // 5
    parents = product(picked[:, :half], mine[...]) + product(picked[:, half:], theirs[...])
    down = product(parents.astype(BF16), w_descend[...]).astype(BF16)
    middle = (near[...].astype(F32) + down.astype(F32)).astype(BF16)
    mid_out[...] = middle[2 * count : 3 * count]
    sent_mid.start()
    fine_down = product(middle, w_fine[...]).astype(BF16)
    closer = fine_down[count : 4 * count]
    table[: 5 * count] = product(fine_down, w_src[...]).astype(BF16)
    table[5 * count :] = product(closer, w_dst[...]).astype(BF16)
    coarse_out[:half] = jnp.where(core == 0, mine[...], theirs[...])
    rest = coarse_out.shape[0] - half
    coarse_out[half:] = jnp.where(core == 0, theirs[:rest], mine[:rest])
    rows = lax.broadcasted_iota(I32, (fine.shape[0], LANES), 0)
    for k in range(edges.shape[0] // CHUNK):
        here = slice(k * CHUNK, (k + 1) * CHUNK)
        piece = k * CHUNK // PIECE
        edge_sum = edges.get(piece)[here, :].astype(F32) + product(select.get(piece)[here, :], table[...])
        hidden = silu(edge_sum.astype(BF16))
        marks = range(k * CHUNK // LANES, (k + 1) * CHUNK // LANES)
        scatter = jnp.concatenate([hot(rows == target[r : r + 1, :]) for r in marks], axis=1)
        part = product(scatter, hidden)
        if k == 0:
            sums[...] = part
        else:
            sums[...] += part
    sent_coarse.start()
    reach = fine_down[count : 5 * count]
    lifted = (fine[...].astype(F32) + product(own_pick[...], reach)).astype(BF16)
    hidden = silu(product(lifted, w_node[...]) + product(sums[...].astype(BF16), last[...])).astype(BF16)
    third = node_w3[...]
    rows = fine_out.shape[0] // 2
    for i in range(2):
        here = slice(i * rows, (i + 1) * rows)
        fine_out[here, :] = updated(lifted[here], hidden[here], third)
        sent_fine.start(i)


def swapped(values):
    return lax.ppermute(values, "c", [(0, 1), (1, 0)])


def crossed(values, tiles):
    pairs = [(t, t + 1) for t in range(1, tiles - 1, 2)]
    return lax.ppermute(values, TILE, pairs + [(b, a) for a, b in pairs])


def on_device(
    fine_latent,
    mid_latent,
    coarse_latent,
    fine_parent,
    mid_parent,
    halo_rows,
    edge_source,
    edge_target,
    w_child,
    mid_w1,
    mid_w2,
    mid_w3,
    w_coarse,
    coarse_w1,
    coarse_w2,
    coarse_w3,
    w_descend,
    w_fine,
    edge_w_src,
    edge_w_dst,
    edge_w2,
    node_w1,
    node_w2,
    node_w3,
):
    count, width = fine_latent.shape
    mids = mid_latent.shape[0]
    coarse_count = coarse_latent.shape[0]
    edge_count = edge_source.shape[0]
    planes, chips = lax.axis_size("z"), lax.axis_size("y") * lax.axis_size("x")
    tiles = 2 * chips
    half = chips * BLOCK
    wide = width + LANES
    parent = fine_parent.reshape(-1, LANES)
    source = edge_source.reshape(-1, LANES)
    target = edge_target.reshape(-1, LANES)
    halo = halo_rows.reshape(-1, LANES)

    def near(*shape, dtype=BF16):
        return pltpu.VMEM(shape, dtype)

    def far(*shape, dtype=BF16):
        return pltpu.HBM(shape, dtype)

    def here(array):
        return pltpu.with_memory_space_constraint(array, pltpu.VMEM)

    def free(*shape, dtype=BF16):
        return jax.ShapeDtypeStruct(shape, dtype)

    square = near(width, width)
    own, swap, cross = kernel_call(
        sums_body,
        [near(mids, width, dtype=F32), free(mids, width), free(mids, width)],
        [],
        stored=[parent, fine_latent],
        name="child_sums",
    )
    from_cross = crossed(cross, tiles)
    from_swap = swapped(swap)
    w_child, mid_w2, mid_w3, kept, hidden, labels = kernel_call(
        mid_ready_body,
        [square, square, square, near(mids, width), near(mids, width, dtype=F32), near(mids, LANES)],
        [],
        stored=[mid_latent, mid_parent[None], mid_w1, w_child, mid_w2, mid_w3],
        keep=[(3, 0), (4, 1), (5, 2)],
        after=[own],
        flops=1_000_000_000,
        name="mid_ready",
    )
    (labelled,) = kernel_call(
        mid_body,
        [free(mids, wide)],
        [here(own), from_swap, from_cross] + [here(a) for a in (kept, hidden, labels, w_child, mid_w2, mid_w3)],
        name="mid_update",
    )
    other = swapped(labelled)
    pair, blocks = kernel_call(
        blocks_body,
        [far(2 * mids, wide), near(half, width)],
        [labelled, other],
        name="coarse_blocks",
    )

    blocks = blocks.reshape(chips, BLOCK, width)
    parts = lax.all_to_all(blocks, PLANE, 0, 0)
    own_edges, halo_swap, cross, token = kernel_call(
        own_edges_body,
        [far(edge_count, width), far(LANES, wide), far(2 * mids + LANES, wide), free(8, LANES)],
        [],
        stored=[parent, halo, source, target, fine_latent, edge_w_src, edge_w_dst, pair],
        streams=[(0, edge_count // PIECE)],
        after=[blocks],
        limit=24,
        flops=4_000_000_000,
        name="own_edges",
    )

    (own_parts,) = kernel_call(
        gather_body, [near(planes, BLOCK, width)], [parts], after=[token], name="plane_sum"
    )
    in_planes = lax.all_to_all(own_parts, "z", 0, 0)
    halo_swap, cross, _ = lax.optimization_barrier((halo_swap, cross, own_parts))
    cross_in = crossed(cross, tiles)
    halo_in = swapped(halo_swap)
    coarse_w3, both, last, own_latent, own_hidden = kernel_call(
        coarse_ready_body,
        [square, square, far(width, width), near(BLOCK, width), near(BLOCK, width, dtype=F32)],
        [],
        stored=[coarse_latent, coarse_w1, w_coarse, coarse_w2, edge_w2, node_w2, coarse_w3],
        keep=[(6, 0)],
        after=[own_parts],
        flops=4_000_000_000,
        name="coarse_ready",
    )
    nearest, own_latent = lax.optimization_barrier((cross_in, own_latent))
    mid_in = swapped(jnp.where(lax.axis_index("c") == 0, nearest[mids : 2 * mids], nearest[:mids]))

    (results,) = kernel_call(
        coarse_body,
        [near(chips, BLOCK, width)],
        [in_planes] + [here(a) for a in (own_latent, own_hidden, both, coarse_w3)],
        after=[cross_in, halo_in],
        name="coarse_update",
    )
    mine = lax.all_to_all(results, PLANE, 0, 0).reshape(half, width)
    w_src, w_descend, w_fine, w_dst, edges, select, own_pick, middle, picked = kernel_call(
        functools.partial(rest_edges_body, mids),
        [square] * 4
        + [far(edge_count, width), far(edge_count, 2 * LANES), far(count, LANES)]
        + [near(5 * mids, width), near(5 * mids, 2 * half)],
        [mid_in],
        stored=[parent, source, target, cross_in, halo_in, edge_w_src, pair, own_edges, w_descend, w_fine, edge_w_dst],
        keep=[(5, 0), (8, 1), (9, 2), (10, 3)],
        pieces=[7],
        streams=[(4, edge_count // CHUNK), (5, edge_count // CHUNK)],
        after=[results],
        scratch=[
            pltpu.VMEM((2 * LANES, width), BF16),
            pltpu.VMEM((2 * count + 2 * LANES, 2 * LANES), BF16),
            pltpu.VMEM((5 * mids, wide), BF16),
        ],
        limit=24,
        flops=4_000_000_000,
        name="rest_edges",
    )
    mine, own_pick = lax.optimization_barrier((mine, own_pick))
    theirs = swapped(mine)

    fine_out, mid_out, coarse_out = kernel_call(
        final_body,
        [far(count, width), far(mids, width), far(coarse_count, width)],
        [mine, theirs] + [here(a) for a in (w_src, w_descend, w_fine, w_dst, middle, picked)],
        stored=[target, select, edges, own_pick, fine_latent, node_w1, last, node_w3],
        pieces=[1, 2],
        streams=[(0, 2), (1, 1), (2, 1)],
        scratch=[pltpu.VMEM((8 * mids, width), BF16), pltpu.VMEM((count, width), F32)],
        limit=24,
        name="final",
    )
    return (fine_out, mid_out, coarse_out)


def solution(mesh):
    groups, tiles = mesh.shape["rhombus"], mesh.shape["tile"]
    side = {32: (4, 4), 8: (2, 2)}[tiles]
    physical = jax.sharding.Mesh(mesh.devices.reshape(groups, *side, 2), ("z", "y", "x", "c"))
    every = ("z", "y", "x", "c")
    split, copied = P(every), P()
    return jax.shard_map(
        on_device,
        mesh=physical,
        in_specs=(split, split, copied) + (split,) * 5 + (copied,) * 16,
        out_specs=(split, split, copied),
        check_vma=False,
    )
```

```python
import functools

import jax
import jax.numpy as jnp
from jax import lax
from jax.experimental import pallas as pl
from jax.experimental.pallas import tpu as pltpu
from jax.sharding import PartitionSpec as P

EPSILON = 1e-05
BLOCK = 24
LANES = 128
CHUNK = 512
PIECE = 1024
PLANE = ("y", "x")
TILE = ("y", "x", "c")
F32, BF16, I32 = jnp.float32, jnp.bfloat16, jnp.int32
VMEM = pl.BlockSpec(memory_space=pltpu.VMEM)
STORED = pl.BlockSpec(memory_space=pltpu.HBM)
UNREAD = pl.BlockSpec(memory_space=pl.ANY)


class Copied:
    def __init__(self, source, target, semaphores, first=0, pieces=1):
        rows = target.shape[0] // pieces
        self.target, self.copies = target, []
        for k in range(pieces):
            part = slice(k * rows, (k + 1) * rows) if pieces > 1 else slice(None)
            self.copies.append(pltpu.make_async_copy(source.at[part], target.at[part], semaphores.at[first + k]))
        self.waiting = [False] * pieces

    def start(self, k=None):
        for i in range(len(self.copies)) if k is None else (k,):
            self.copies[i].start()
            self.waiting[i] = True
        return self

    def get(self, k=None):
        for i in range(len(self.copies)) if k is None else (k,):
            if self.waiting[i]:
                self.copies[i].wait()
                self.waiting[i] = False
        return self.target

    def __getitem__(self, index):
        return self.get()[index]

    @property
    def shape(self):
        return self.target.shape


def kernel_call(
    body, outs, operands, stored=(), after=(), scratch=(), keep=(), streams=(), pieces=(), limit=8, flops=0, name=None
):
    count, held, skipped, given = len(operands), len(stored), len(after), len(outs)
    target = dict(keep)
    cuts = [stored[i].shape[0] // PIECE if i in pieces else 1 for i in range(held)]
    flows = dict(streams)

    def kernel(*refs):
        inputs, refs = refs[:count], refs[count:]
        sources, refs = refs[:held], refs[held + skipped :]
        results, refs = refs[:given], refs[given:]
        own, refs = refs[: len(scratch)], refs[len(scratch) :]
        buffers = iter(refs)
        places = [results[target[i]] if i in target else next(buffers) for i in range(held)]
        leaving = {o: next(buffers) for o in flows}
        semaphores = next(buffers) if held or flows else None
        first, copies, fresh = 0, [], []
        for i in range(held):
            copies.append(Copied(sources[i], places[i], semaphores, first, cuts[i]).start())
            first += cuts[i]
        for o in range(given):
            if o in flows:
                fresh.append(Copied(leaving[o], results[o], semaphores, first, flows[o]))
                first += flows[o]
            elif o not in target.values():
                fresh.append(results[o])
        body(*inputs, *copies, *fresh, *leaving.values(), *own)
        for copy in copies + fresh:
            if isinstance(copy, Copied):
                copy.get()

    buffers = [pltpu.VMEM(stored[i].shape, stored[i].dtype) for i in range(held) if i not in target]
    buffers += [pltpu.VMEM(outs[o].shape, outs[o].dtype) for o in flows]
    if held or flows:
        buffers.append(pltpu.SemaphoreType.DMA((sum(cuts) + sum(flows.values()),)))
    return pl.pallas_call(
        kernel,
        out_shape=outs,
        in_specs=[VMEM] * count + [STORED] * held + [UNREAD] * skipped,
        out_specs=[STORED if o in flows else VMEM for o in range(given)],
        scratch_shapes=[*scratch, *buffers],
        compiler_params=pltpu.CompilerParams(vmem_limit_bytes=limit << 20),
        cost_estimate=pl.CostEstimate(flops=flops, bytes_accessed=1 << 20, transcendentals=0),
        name=name,
    )(*operands, *[pltpu.with_memory_space_constraint(array, pltpu.HBM) for array in stored], *after)


def product(left, right):
    return jnp.dot(left, right, preferred_element_type=F32)


def silu(values):
    half = 0.5 * values
    return half + half * jnp.tanh(half)


def updated(latent, hidden, third):
    values = product(hidden.astype(BF16), third)
    scale = lax.rsqrt(jnp.mean(values * values, axis=-1, keepdims=True) + EPSILON)
    return (latent.astype(F32) + values * scale).astype(BF16)


def lanes(height, first=0):
    return lax.broadcasted_iota(I32, (height, LANES), 1) + first


def spread(row):
    return jnp.broadcast_to(row, (LANES, LANES)).T


def hot(mask):
    return jnp.where(mask, 1.0, 0.0).astype(BF16)


def picks(spread_ids, first, blocks):
    return [hot(spread_ids == lanes(LANES, first + LANES * q)) for q in range(blocks)]


def sums_body(parent, fine, own, swap, cross):
    count = own.shape[0]
    core = lax.axis_index("c")
    rows = lax.broadcasted_iota(I32, (3 * count, LANES), 0)
    blocks = [hot(rows == parent[r : r + 1, :]) for r in range(parent.shape[0])]
    sums = product(jnp.concatenate(blocks, axis=1), fine[...])
    own[...] = sums[:count]
    down, up = sums[count : 2 * count].astype(BF16), sums[2 * count :].astype(BF16)
    swap[...] = jnp.where(core == 0, up, down)
    cross[...] = jnp.where(core == 0, down, up)


def mid_ready_body(latent, ids, first, w_child, second, third, kept, hidden, labels):
    count = hidden.shape[0]
    spread_ids = spread(jnp.concatenate([ids[...], jnp.zeros((1, LANES - count), I32)], axis=1))[:count]
    place = lanes(count)
    label = jnp.where(place == 0, spread_ids >> 5, jnp.where(place == 1, spread_ids & 31, 0))
    labels[...] = label.astype(F32).astype(BF16)
    values = latent[...]
    kept[...] = values
    hidden[...] = product(values, first[...])


def mid_body(own, before, after, latent, hidden, labels, w_child, second, third, out):
    width = latent.shape[1]
    total = own[...] + before[...].astype(F32) + after[...].astype(F32)
    incoming = product(total.astype(BF16), w_child[...]).astype(BF16)
    value = silu(hidden[...] + product(incoming, second[...]))
    out[:, :width] = updated(latent[...], value, third[...])
    out[:, width:] = labels[...]


def row_ids(labelled, width):
    label = labelled[:, width:].astype(F32)
    return (label[:, :1] * 32.0 + label[:, 1:2]).astype(I32)


def blocks_body(mine, theirs, pair, out):
    count, width = mine.shape[0], out.shape[1]
    half = out.shape[0]
    core = lax.axis_index("c")
    pair[pl.ds(pl.multiple_of(core * count, count), count), :] = mine[...]
    pair[pl.ds(pl.multiple_of((1 - core) * count, count), count), :] = theirs[...]
    both = pair[...]
    columns = lax.broadcasted_iota(I32, (2 * count, half), 1) + core * half
    picked = hot(row_ids(both, width) == columns)
    out[...] = lax.dot_general(
        picked, both[:, :width], (((0,), (0,)), ((), ())), preferred_element_type=F32
    ).astype(BF16)


def own_edges_body(
    parent, halo, source, target, fine, w_src, w_dst, pair, sent_out, swap, cross, token, out
):
    token[...] = jnp.zeros_like(token)
    count, width = fine.shape
    two, blocks = pair.shape[0], count // LANES
    core = lax.axis_index("c")
    codes = [(spread(parent[r : r + 1, :]) + 1).astype(F32).astype(BF16) for r in range(blocks)]
    codes = jnp.concatenate(codes, axis=0)
    rows = halo[...]
    values = fine[...]
    sent = product(values, w_src[...]).astype(BF16)
    received = product(values, w_dst[...]).astype(BF16)

    def marks_of(k):
        both = []
        for ids in (source, target):
            rows = range(k * CHUNK // LANES, (k + 1) * CHUNK // LANES)
            rows = [jnp.concatenate(picks(spread(ids[r : r + 1, :]), 0, blocks), axis=1) for r in rows]
            both.append(jnp.concatenate(rows, axis=0))
        return both

    chunks = out.shape[0] // CHUNK
    following = marks_of(0)
    for k in range(chunks):
        sources, targets = following
        if k + 1 < chunks:
            following = marks_of(k + 1)
        total = product(sources, sent) + product(targets, received)
        out[k * CHUNK : (k + 1) * CHUNK, :] = total.astype(BF16)
        if (k + 1) * CHUNK % PIECE == 0:
            sent_out.start(k * CHUNK // PIECE)
    for place, first, row in (
        (swap, 0, jnp.where(core == 0, rows[1:2], rows[:1])),
        (cross, two, jnp.where(core == 0, rows[:1], rows[1:2])),
    ):
        picked = jnp.concatenate(picks(spread(row), 0, blocks), axis=1)
        place[first : first + LANES, :width] = product(picked, values).astype(BF16)
        place[first : first + LANES, width:] = product(picked, codes).astype(BF16)
    cross[:two] = pair[...]


def gather_body(parts, out):
    total = jnp.sum(parts[...].astype(F32), axis=0).astype(BF16)
    for i in range(out.shape[0]):
        out[i] = total


def coarse_body(parts, own_latent, own_hidden, both, third, out):
    total = jnp.sum(parts[...].astype(F32), axis=0).astype(BF16)
    hidden = silu(own_hidden[...] + product(total, both[...]))
    result = updated(own_latent[...], hidden, third[...])
    for i in range(out.shape[0]):
        out[i] = result


def coarse_ready_body(
    coarse, coarse_w1, w_coarse, coarse_w2, edge_w2, node_w2, third, both, last, own_latent, own_hidden
):
    rows, total = own_latent.shape[0], coarse.shape[0]
    chips = lax.axis_size("y") * lax.axis_size("x")
    chip = lax.axis_index("y") * lax.axis_size("x") + lax.axis_index("x")
    first = (lax.axis_index("c") * chips + chip) * rows
    place = lax.broadcasted_iota(I32, (rows, total), 0) + first
    picked = hot(place == lax.broadcasted_iota(I32, (rows, total), 1))
    latent = product(picked, coarse[...]).astype(BF16)
    own_latent[...] = latent
    own_hidden[...] = product(latent, coarse_w1[...])
    both[...] = product(w_coarse[...], coarse_w2[...]).astype(BF16)
    last[...] = product(edge_w2[...], node_w2[...]).astype(BF16)


def slots(codes, tile, count):
    parent = codes - 1
    side = parent // count
    away = jnp.where(side == 1, -1, jnp.where(side == 2, 1, 0))
    return jnp.where(codes > 0, (tile + away) * count + (parent & (count - 1)), -1)


def rest_edges_body(
    mid_count, mid_swap, parent, source, target, cross, swap, w_src, pair, first, w_descend, w_fine, w_dst,
    sent_out, sent_select, own_pick, middle, picked, out, select, table, where, window
):
    core = lax.axis_index("c")
    count = own_pick.shape[0]
    width = out.shape[1]
    blocks = count // LANES
    two = pair.shape[0]
    for r in range(blocks):
        place = slots(spread(parent[r : r + 1, :]) + 1, 2, mid_count)
        rows = slice(r * LANES, (r + 1) * LANES)
        where[rows, :] = jnp.concatenate(picks(place, 0, 2), axis=1)
        near = place - mid_count
        own_pick[rows, :] = hot(near == lanes(LANES))
        far = place + 4 * mid_count
        there = slice(count + 2 * LANES + r * LANES, count + 2 * LANES + (r + 1) * LANES)
        where[there, :] = jnp.concatenate(picks(far, 0, 2), axis=1)
    for values, late in ((cross[two:], core), (swap[...], 1 - core)):
        rows = pl.ds(pl.multiple_of(late * LANES, LANES), LANES)
        table[rows, :] = product(values[:, :width], w_src[...]).astype(BF16)
        place = slots(values[:, width:].astype(F32).astype(I32), 1 + 2 * late, mid_count)
        rows = pl.ds(pl.multiple_of(count + late * LANES, LANES), LANES)
        where[rows, :] = jnp.concatenate(picks(place, 0, 2), axis=1)
    window[pl.ds(pl.multiple_of((1 - core) * 4 * mid_count, mid_count), mid_count), :] = mid_swap[...]
    window[pl.ds(pl.multiple_of(core * 3 * mid_count, mid_count), two), :] = cross[:two]
    window[pl.ds(pl.multiple_of((2 - core) * mid_count, mid_count), two), :] = pair[...]
    near = window[...]
    middle[...] = near[:, :width]
    half = picked.shape[1] // 2
    ids = row_ids(near, width)
    mine = ids - core * half
    place = jnp.where((mine >= 0) & (mine < half), mine, ids - (1 - core) * half + half)
    picked[...] = hot(place == lax.broadcasted_iota(I32, picked.shape, 1))

    def marks_of(k):
        rows = []
        for r in range(k * CHUNK // LANES, (k + 1) * CHUNK // LANES):
            row = picks(spread(source[r : r + 1, :]), 0, blocks + 2)
            row += picks(spread(target[r : r + 1, :]), 0, blocks)
            rows.append(jnp.concatenate(row, axis=1))
        return jnp.concatenate(rows, axis=0)

    chunks = out.shape[0] // CHUNK
    ready = []
    following = marks_of(0)
    for k in range(chunks):
        here = slice(k * CHUNK, (k + 1) * CHUNK)
        first.get(k * CHUNK // PIECE)
        marks = following
        if k + 1 < chunks:
            following = marks_of(k + 1)
        select[here, :] = product(marks, where[...]).astype(BF16)
        rest = product(marks[:, count : count + 2 * LANES], table[...])
        out[here, :] = (first.target[here, :].astype(F32) + rest).astype(BF16)
        ready += [k]
        if k % 2 == 1 or k >= chunks - 2:
            for i in ready:
                sent_out.start(i)
                sent_select.start(i)
            ready = []


def final_body(
    mine, theirs, w_src, w_descend, w_fine, w_dst, near, picked, target, select, edges, own_pick, fine,
    w_node, last, node_w3, sent_fine, sent_mid, sent_coarse, fine_out, mid_out, coarse_out, table, sums,
):
    core = lax.axis_index("c")
    half = mine.shape[0]
    count = near.shape[0] // 5
    parents = product(picked[:, :half], mine[...]) + product(picked[:, half:], theirs[...])
    down = product(parents.astype(BF16), w_descend[...]).astype(BF16)
    middle = (near[...].astype(F32) + down.astype(F32)).astype(BF16)
    mid_out[...] = middle[2 * count : 3 * count]
    sent_mid.start()
    fine_down = product(middle, w_fine[...]).astype(BF16)
    closer = fine_down[count : 4 * count]
    table[: 5 * count] = product(fine_down, w_src[...]).astype(BF16)
    table[5 * count :] = product(closer, w_dst[...]).astype(BF16)
    coarse_out[:half] = jnp.where(core == 0, mine[...], theirs[...])
    rest = coarse_out.shape[0] - half
    coarse_out[half:] = jnp.where(core == 0, theirs[:rest], mine[:rest])
    rows = lax.broadcasted_iota(I32, (fine.shape[0], LANES), 0)
    for k in range(edges.shape[0] // CHUNK):
        here = slice(k * CHUNK, (k + 1) * CHUNK)
        piece = k * CHUNK // PIECE
        edge_sum = edges.get(piece)[here, :].astype(F32) + product(select.get(piece)[here, :], table[...])
        hidden = silu(edge_sum.astype(BF16))
        marks = range(k * CHUNK // LANES, (k + 1) * CHUNK // LANES)
        scatter = jnp.concatenate([hot(rows == target[r : r + 1, :]) for r in marks], axis=1)
        part = product(scatter, hidden)
        if k == 0:
            sums[...] = part
        else:
            sums[...] += part
    sent_coarse.start()
    reach = fine_down[count : 5 * count]
    lifted = (fine[...].astype(F32) + product(own_pick[...], reach)).astype(BF16)
    hidden = silu(product(lifted, w_node[...]) + product(sums[...].astype(BF16), last[...])).astype(BF16)
    third = node_w3[...]
    rows = fine_out.shape[0] // 2
    for i in range(2):
        here = slice(i * rows, (i + 1) * rows)
        fine_out[here, :] = updated(lifted[here], hidden[here], third)
        sent_fine.start(i)


def swapped(values):
    return lax.ppermute(values, "c", [(0, 1), (1, 0)])


def crossed(values, tiles):
    pairs = [(t, t + 1) for t in range(1, tiles - 1, 2)]
    return lax.ppermute(values, TILE, pairs + [(b, a) for a, b in pairs])


def on_device(
    fine_latent,
    mid_latent,
    coarse_latent,
    fine_parent,
    mid_parent,
    halo_rows,
    edge_source,
    edge_target,
    w_child,
    mid_w1,
    mid_w2,
    mid_w3,
    w_coarse,
    coarse_w1,
    coarse_w2,
    coarse_w3,
    w_descend,
    w_fine,
    edge_w_src,
    edge_w_dst,
    edge_w2,
    node_w1,
    node_w2,
    node_w3,
):
    count, width = fine_latent.shape
    mids = mid_latent.shape[0]
    coarse_count = coarse_latent.shape[0]
    edge_count = edge_source.shape[0]
    planes, chips = lax.axis_size("z"), lax.axis_size("y") * lax.axis_size("x")
    tiles = 2 * chips
    half = chips * BLOCK
    wide = width + LANES
    parent = fine_parent.reshape(-1, LANES)
    source = edge_source.reshape(-1, LANES)
    target = edge_target.reshape(-1, LANES)
    halo = halo_rows.reshape(-1, LANES)

    def near(*shape, dtype=BF16):
        return pltpu.VMEM(shape, dtype)

    def far(*shape, dtype=BF16):
        return pltpu.HBM(shape, dtype)

    def here(array):
        return pltpu.with_memory_space_constraint(array, pltpu.VMEM)

    def free(*shape, dtype=BF16):
        return jax.ShapeDtypeStruct(shape, dtype)

    square = near(width, width)
    own, swap, cross = kernel_call(
        sums_body,
        [near(mids, width, dtype=F32), free(mids, width), free(mids, width)],
        [],
        stored=[parent, fine_latent],
        name="child_sums",
    )
    from_cross = crossed(cross, tiles)
    from_swap = swapped(swap)
    w_child, mid_w2, mid_w3, kept, hidden, labels = kernel_call(
        mid_ready_body,
        [square, square, square, near(mids, width), near(mids, width, dtype=F32), near(mids, LANES)],
        [],
        stored=[mid_latent, mid_parent[None], mid_w1, w_child, mid_w2, mid_w3],
        keep=[(3, 0), (4, 1), (5, 2)],
        after=[own],
        flops=1_000_000_000,
        name="mid_ready",
    )
    (labelled,) = kernel_call(
        mid_body,
        [free(mids, wide)],
        [here(own), from_swap, from_cross] + [here(a) for a in (kept, hidden, labels, w_child, mid_w2, mid_w3)],
        name="mid_update",
    )
    other = swapped(labelled)
    pair, blocks = kernel_call(
        blocks_body,
        [far(2 * mids, wide), near(half, width)],
        [labelled, other],
        name="coarse_blocks",
    )

    blocks = blocks.reshape(chips, BLOCK, width)
    parts = lax.all_to_all(blocks, PLANE, 0, 0)
    own_edges, halo_swap, cross, token = kernel_call(
        own_edges_body,
        [far(edge_count, width), far(LANES, wide), far(2 * mids + LANES, wide), free(8, LANES)],
        [],
        stored=[parent, halo, source, target, fine_latent, edge_w_src, edge_w_dst, pair],
        streams=[(0, edge_count // PIECE)],
        after=[blocks],
        limit=24,
        flops=4_000_000_000,
        name="own_edges",
    )

    (own_parts,) = kernel_call(
        gather_body, [near(planes, BLOCK, width)], [parts], after=[token], name="plane_sum"
    )
    in_planes = lax.all_to_all(own_parts, "z", 0, 0)
    cross_in = crossed(cross, tiles)
    halo_in = swapped(halo_swap)
    coarse_w3, both, last, own_latent, own_hidden = kernel_call(
        coarse_ready_body,
        [square, square, far(width, width), near(BLOCK, width), near(BLOCK, width, dtype=F32)],
        [],
        stored=[coarse_latent, coarse_w1, w_coarse, coarse_w2, edge_w2, node_w2, coarse_w3],
        keep=[(6, 0)],
        after=[own_parts],
        flops=4_000_000_000,
        name="coarse_ready",
    )
    nearest, own_latent = lax.optimization_barrier((cross_in, own_latent))
    mid_in = swapped(jnp.where(lax.axis_index("c") == 0, nearest[mids : 2 * mids], nearest[:mids]))

    (results,) = kernel_call(
        coarse_body,
        [near(chips, BLOCK, width)],
        [in_planes] + [here(a) for a in (own_latent, own_hidden, both, coarse_w3)],
        after=[cross_in, halo_in],
        name="coarse_update",
    )
    mine = lax.all_to_all(results, PLANE, 0, 0).reshape(half, width)
    w_src, w_descend, w_fine, w_dst, edges, select, own_pick, middle, picked = kernel_call(
        functools.partial(rest_edges_body, mids),
        [square] * 4
        + [far(edge_count, width), far(edge_count, 2 * LANES), far(count, LANES)]
        + [near(5 * mids, width), near(5 * mids, 2 * half)],
        [mid_in],
        stored=[parent, source, target, cross_in, halo_in, edge_w_src, pair, own_edges, w_descend, w_fine, edge_w_dst],
        keep=[(5, 0), (8, 1), (9, 2), (10, 3)],
        pieces=[7],
        streams=[(4, edge_count // CHUNK), (5, edge_count // CHUNK)],
        after=[results],
        scratch=[
            pltpu.VMEM((2 * LANES, width), BF16),
            pltpu.VMEM((2 * count + 2 * LANES, 2 * LANES), BF16),
            pltpu.VMEM((5 * mids, wide), BF16),
        ],
        limit=24,
        flops=4_000_000_000,
        name="rest_edges",
    )
    mine, own_pick = lax.optimization_barrier((mine, own_pick))
    theirs = swapped(mine)

    fine_out, mid_out, coarse_out = kernel_call(
        final_body,
        [far(count, width), far(mids, width), far(coarse_count, width)],
        [mine, theirs] + [here(a) for a in (w_src, w_descend, w_fine, w_dst, middle, picked)],
        stored=[target, select, edges, own_pick, fine_latent, node_w1, last, node_w3],
        pieces=[1, 2],
        streams=[(0, 2), (1, 1), (2, 1)],
        scratch=[pltpu.VMEM((8 * mids, width), BF16), pltpu.VMEM((count, width), F32)],
        limit=24,
        name="final",
    )
    return (fine_out, mid_out, coarse_out)


def solution(mesh):
    groups, tiles = mesh.shape["rhombus"], mesh.shape["tile"]
    side = {32: (4, 4), 8: (2, 2)}[tiles]
    physical = jax.sharding.Mesh(mesh.devices.reshape(groups, *side, 2), ("z", "y", "x", "c"))
    every = ("z", "y", "x", "c")
    split, copied = P(every), P()
    return jax.shard_map(
        on_device,
        mesh=physical,
        in_specs=(split, split, copied) + (split,) * 5 + (copied,) * 16,
        out_specs=(split, split, copied),
        check_vma=False,
    )
```
